32 devices in a mesh: pole: 4 (over x, core), row: 4 (over z), col: 2 (over y).
Axes of the slice: x: 2, y: 2, z: 4, core: 2. Of those that a mesh axis runs over, the one named last changes fastest.
Arguments:
- inverse: bfloat16 [4, 2, 4096, 4096], P('pole', None, 'row', 'col'), may hold values from -0.0625 to 0.0625
- factor: bfloat16 [4, 1, 2048, 1024], P('pole', None, ('row', 'col')), may hold values from -1.796875 to 1.796875
- dinv: float32 [512, 4, 1, 2, 512], P(('row', 'col'), 'pole'), may hold values from -6 to 6
- ancestors: int32 [1, 16], replicated, may hold values from 0 to 31, as said below
- owner: int32 [2048, 1], P(('row', 'col')), may hold values from 0 to 31; in each aligned block of 256 rows (0 to 255, 256 to 511, ...) at most 16 rows name the same one
- weight_table: float32 [2, 16], replicated, may hold values from -4 to 4
- pole_slot: int32 [4], P('pole'), may hold values from 0 to 15
Outputs:
- inverse_column: float32 [4096, 4, 1, 2, 512], P(('row', 'col'), 'pole')
- diag_inverse: float32 [512, 4, 1, 2, 512], P(('row', 'col'), 'pole')
- density_diag: float32 [512, 1, 512], P(('row', 'col'))
- tile_density: float32 [32, 8, 128], P(('pole', 'row', 'col'))
The draws below stay inside these ranges and needn't reach their ends.
Inputs may be any that keep to these rules, and one draw needn't show every extreme that they name: `ancestors`: each row lists 16 distinct block numbers in increasing order. In the rows of one device (256 rows of owner) no tile is named more than 16 times.
All inputs are finite; a program needn't handle non-finite values.
Results may differ from the reference program's by a relative error of at most 0.0028.
Values may be sent and summed in bfloat16 or wider, within the bound.
No kernel may reach another device: no remote copies, remote signals or barrier semaphores. Data moves between devices by JAX's collectives and lax.ppermute only.
A program may use at most 64 MiB of HBM per device.

```python
import math
import jax
import jax.numpy as jnp
import numpy as np
from jax import lax

A = 4096
S = 512
SN = 1
BS = 128
NSEL = 16
BR = 8
BC = 128
NWEIGHT = 16
POLES = 4
TILES = 32
NBLOCKS = 2048
HB = 256
CAP = 16


def draw_ancestors(key, part):
    listed = []
    for supernode in range(SN):
        shuffled = jax.random.permutation(jax.random.fold_in(key, 7919 + supernode), A // BS)
        listed.append(jnp.sort(shuffled[:NSEL]))
    return jnp.stack(listed).astype(jnp.int32)


def set_ends(result, own_key, low, top_value):
    dims = result.shape
    place = [jax.random.randint(jax.random.fold_in(own_key, axis), (), 0, dims[axis]) for axis in range(len(dims))]
    result = result.at[tuple(place)].set(low)
    longest = dims.index(max(dims))
    place[longest] = (place[longest] + 1) % dims[longest]
    return result.at[tuple(place)].set(top_value)


def level_of(key, dims, cuts, smallest, high):
    factor_of = 1.0
    for axis_at, shards_of in cuts:
        steps = jax.random.uniform(jax.random.fold_in(jax.random.fold_in(key, 6), axis_at), (shards_of,), jnp.float32, smallest / len(cuts), high / len(cuts))
        factor_of = factor_of * jnp.repeat(jnp.exp(steps), dims[axis_at] // shards_of).reshape((-1,) + (1,) * (len(dims) - 1 - axis_at))
    return factor_of


def routed_block(stream_key, own, number, rows, number_of, top, limit, skew):
    sequence = jax.random.permutation(stream_key, number_of)
    crowded, usual = load_shares(number_of, rows * top, limit, skew, True), load_shares(number_of, rows * top, limit, skew, False)
    places = jnp.arange(number_of)

    def named(lengths, turn):
        used = int((lengths > 0).sum())
        fixed = max(1, used // 4)
        moved = fixed + (places - fixed + turn * (used - fixed)) % max(1, number_of - fixed)
        return jnp.zeros((number_of,), jnp.int32).at[sequence[jnp.where(places < fixed, places, moved)]].set(jnp.asarray(lengths, jnp.int32))

    lengths = jnp.where(number % 4 == 0, named(crowded, number // 4), named(usual, number - number // 4 - 1))
    mixed = jax.random.permutation(jax.random.fold_in(own, 3), number_of)
    giver, taker = mixed[0:number_of // 2 * 2:2], mixed[1:number_of // 2 * 2:2]
    margin = jnp.minimum(lengths[giver] - 1, limit - lengths[taker]) // 2
    margin = jnp.where((giver == sequence[0]) | (taker == sequence[0]) | (lengths[taker] == 0), 0, jnp.maximum(margin, 0))
    moved = jax.random.randint(jax.random.fold_in(own, 4), (number_of // 2,), 0, 1 << 20) % (margin + 1)
    lengths = lengths.at[giver].add(-moved).at[taker].add(moved)
    labels = jnp.searchsorted(jnp.cumsum(lengths), jnp.arange(rows * top), side="right").astype(jnp.int32)
    listing = labels.reshape(top, rows).T
    listing = listing[jax.random.permutation(jax.random.fold_in(own, 1), rows)]
    turn = jax.random.randint(jax.random.fold_in(own, 2), (rows, 1), 0, top)
    return jnp.take_along_axis(listing, (jnp.arange(top)[None, :] + turn) % top, axis=1)


def load_shares(count, total, most, slope, full):
    loads = [(1 << 20) // math.isqrt(standing ** slope) + 1 for standing in range(1, count + 1)]
    largest = most if full else min(most, max(-(-total // count), total * loads[0] // sum(loads)))
    least = 1 if total - largest >= count - 1 else 0
    given, rest = [largest] + [least] * (count - 1), total - largest - least * (count - 1)
    while rest > 0:
        free = [i for i in range(1, count) if given[i] < largest] or [i for i in range(1, count) if given[i] < most]
        whole, budget = sum([loads[i] for i in free]), rest
        for i in free:
            addition = min(most - given[i], max(1, budget * loads[i] // whole), rest)
            given[i] = given[i] + addition
            rest = rest - addition
    return np.array(given)


def noise(own_key, shape, spread, limit, split=(), kind=jnp.bfloat16):
    loudness = level_of(own_key, shape, split, -0.22, 0.18) if split else 1.0
    drawn = jax.random.normal(own_key, shape, jnp.float32) * spread * loudness
    return jnp.minimum(jnp.maximum(drawn, -limit), limit).astype(kind)


def setup_inputs(seed: int = 0) -> dict:
    streams_of = jax.random.split(jax.random.key(seed), 8)
    inverse = noise(streams_of[0], (POLES, 2, A, A), (2 * A) ** -0.5, 0.0625, ((0, 4), (2, 4), (3, 2)))
    factor = noise(streams_of[1], (POLES, SN, NSEL * BS, 2 * S), 0.3, 1.796875, ((0, 4), (2, 8)))
    dinv = noise(streams_of[2], (S, POLES, SN, 2, S), 1.0, 6.0, ((0, 8), (1, 4)), jnp.float32)
    ancestors = draw_ancestors(jax.random.fold_in(streams_of[7], 71), 0)
    owner_keys = jax.random.split(jax.random.fold_in(streams_of[4], 1), NBLOCKS // HB)
    owner_turns = jax.random.permutation(jax.random.fold_in(streams_of[4], 3), NBLOCKS // HB)
    owner = jax.vmap(lambda own, number: routed_block(jax.random.fold_in(streams_of[4], 2), own, number, HB, TILES, 1, CAP, 2))(owner_keys, owner_turns).reshape((NBLOCKS, 1))
    weight_table = noise(streams_of[5], (2, NWEIGHT), 1.0, 4.0, (), jnp.float32)
    pole_slot = set_ends(jax.random.randint(streams_of[6], (POLES,), 0, NWEIGHT), jax.random.fold_in(streams_of[6], 1), 0, NWEIGHT - 1).astype(jnp.int32)
    return dict(inverse=inverse, factor=factor, dinv=dinv, ancestors=ancestors, owner=owner, weight_table=weight_table, pole_slot=pole_slot)


precise = lax.Precision.HIGHEST


def transposed(left, right):
    return lax.dot_general(left, right, (((0,), (0,)), ((), ())), preferred_element_type=jnp.float32)


def reference(inverse, factor, dinv, ancestors, owner, weight_table, pole_slot):
    count_blocks = A // BS
    choose_map = (jnp.arange(NWEIGHT)[None, :] == pole_slot[:, None]).astype(jnp.float32)
    weights = jnp.dot(choose_map, weight_table.T, precision=precise)
    block_of_row = jnp.arange(A) // BS
    selected = jnp.any(block_of_row[None, :, None] == ancestors[:, None, :], axis=2)
    columns = []
    diags = []
    for member in range(POLES):
        real_full = inverse[member, 0].reshape(A, count_blocks, BS)
        imag_full = inverse[member, 1].reshape(A, count_blocks, BS)
        col_list = []
        diag_list = []
        for supernode in range(SN):
            picked = ancestors[supernode]
            real_sel = jnp.take(real_full, picked, axis=1).reshape(A, NSEL * BS)
            imag_sel = jnp.take(imag_full, picked, axis=1).reshape(A, NSEL * BS)
            left_real = factor[member, supernode, :, :S]
            left_imag = factor[member, supernode, :, S:]
            prod_real = jnp.dot(real_sel, left_real, preferred_element_type=jnp.float32) - jnp.dot(imag_sel, left_imag, preferred_element_type=jnp.float32)
            prod_imag = jnp.dot(real_sel, left_imag, preferred_element_type=jnp.float32) + jnp.dot(imag_sel, left_real, preferred_element_type=jnp.float32)
            keep = selected[supernode][:, None]
            col_list.append(jnp.stack([jnp.where(keep, -prod_real, 0.0), jnp.where(keep, -prod_imag, 0.0)], axis=1))
            round_real = prod_real.astype(jnp.bfloat16).reshape(count_blocks, BS, S)
            round_imag = prod_imag.astype(jnp.bfloat16).reshape(count_blocks, BS, S)
            rows_real = jnp.take(round_real, picked, axis=0).reshape(NSEL * BS, S)
            rows_imag = jnp.take(round_imag, picked, axis=0).reshape(NSEL * BS, S)
            mat_real = transposed(left_real, rows_real) - transposed(left_imag, rows_imag)
            mat_imag = transposed(left_real, rows_imag) + transposed(left_imag, rows_real)
            diag_list.append(dinv[:, member, supernode] + jnp.stack([mat_real, mat_imag], axis=1))
        columns.append(jnp.stack(col_list, axis=1))
        diags.append(jnp.stack(diag_list, axis=1))
    inverse_column = jnp.stack(columns, axis=1)
    diag_inverse = jnp.stack(diags, axis=1)
    weight_real = weights[:, 0][None, :, None, None]
    weight_imag = weights[:, 1][None, :, None, None]
    density_diag = jnp.sum(weight_real * diag_inverse[:, :, :, 1] + weight_imag * diag_inverse[:, :, :, 0], axis=1)
    column_density = jnp.sum(weight_real * inverse_column[:, :, :, 1] + weight_imag * inverse_column[:, :, :, 0], axis=1)
    pieces = column_density.reshape(A // BR, BR, SN, S // BC, BC).transpose(0, 2, 3, 1, 4).reshape(NBLOCKS, BR * BC)
    tile_map = (jnp.arange(TILES)[:, None] == owner[None, :, 0]).astype(jnp.float32)
    tile_density = jnp.dot(tile_map, pieces, precision=precise).reshape(TILES, BR, BC)
    return inverse_column, diag_inverse, density_diag, tile_density
```

```python
import functools

import jax
import jax.numpy as jnp
from jax import lax
from jax.experimental import pallas as pl
from jax.experimental.pallas import tpu as pltpu
from jax.sharding import PartitionSpec as P

BS = 128
BR = 8
BC = 128


def shift_pairs(rows, cols, step, valid):
    return [
        (r * cols + c, r * cols + (c + step) % cols)
        for r in range(rows)
        if valid(r)
        for c in range(cols)
    ]


def gather_pieces(shard, rows, cols):
    grid = ("row", "col")
    pieces = [(shard, 0, 0)]
    line = [(shard, 0)]
    for step in range(1, cols):
        pairs = shift_pairs(rows, cols, step, lambda r: True)
        pieces.append((lax.ppermute(shard, grid, pairs), 0, step))
    up = down = shard
    for hop in range(1, rows):
        up = lax.ppermute(up, "row", [(r, r + 1) for r in range(hop - 1, rows - 1)])
        down = lax.ppermute(down, "row", [(r, r - 1) for r in range(1, rows - hop + 1)])
        for piece, offset in ((up, hop), (down, -hop)):
            pieces.append((piece, offset, 0))
            for step in range(1, cols):
                pairs = shift_pairs(rows, cols, step, lambda r: 0 <= r - offset < rows)
                pieces.append((lax.ppermute(piece, grid, pairs), offset, step))
    return pieces


def local_kernel(
    places, rows, cols, ancestors, table, slot, owner, inverse, *refs
):
    pieces = refs[: len(places)]
    keep, send, diag_keep, diag_send, tiles = refs[len(places) : len(places) + 5]
    full, picked, acc, diag, row_sem, piece_sem = refs[len(places) + 5 :]
    selected = ancestors.shape[0]
    wide = acc.shape[1]
    half = wide // 2
    shard_rows = pieces[0].shape[0]
    row_blocks = inverse.shape[1] // BS
    col_blocks = inverse.shape[2] // BS
    own_blocks = row_blocks // cols
    r = lax.axis_index("row")
    c = lax.axis_index("col")

    def below(limit):
        total = jnp.int32(0)
        for i in range(selected):
            total = total + (ancestors[i] < limit).astype(jnp.int32)
        return total

    row_first = below(r * row_blocks)
    row_count = below((r + 1) * row_blocks) - row_first
    col_first = below(c * col_blocks)
    col_count = below((c + 1) * col_blocks) - col_first

    def block_copy(i, k):
        row = pl.multiple_of((ancestors[row_first + i] - r * row_blocks) * BS, BS)
        col = pl.multiple_of((ancestors[col_first + k] - c * col_blocks) * BS, BS)
        return pltpu.make_async_copy(
            inverse.at[:, pl.ds(row, BS), pl.ds(col, BS)],
            picked.at[i, :, :, pl.ds(pl.multiple_of(k * BS, BS), BS)],
            row_sem.at[i],
        )

    def piece_copy(n):
        offset, step = places[n]
        source = (r - offset) * cols + lax.rem(c - step + cols, cols)
        start = pl.multiple_of(source * shard_rows, shard_rows)
        return pltpu.make_async_copy(
            pieces[n], full.at[pl.ds(start, shard_rows)], piece_sem.at[n]
        )

    def has_piece(n):
        offset = places[n][0]
        return jnp.logical_and(r - offset >= 0, r - offset < rows)

    for n in range(len(places)):
        pl.when(has_piece(n))(lambda n=n: piece_copy(n).start())

    @pl.loop(0, row_count)
    def _(i):
        @pl.loop(0, col_count)
        def _(k):
            block_copy(i, k).start()

    full[pl.ds(selected * BS, BS), :] = jnp.zeros((BS, wide), full.dtype)
    diag[...] = jnp.zeros_like(diag)
    tiles[...] = jnp.zeros_like(tiles)
    weight_real = table[0, slot[0]]
    weight_imag = table[1, slot[0]]

    @pl.when(lax.rem(col_count, 2) == 1)
    def _():
        @pl.loop(0, row_count)
        def _(i):
            start = pl.multiple_of(col_count * BS, BS)
            picked[i, :, :, pl.ds(start, BS)] = jnp.zeros((2, BS, BS), picked.dtype)

    for n in range(len(places)):
        pl.when(has_piece(n))(lambda n=n: piece_copy(n).wait())

    @pl.loop(0, row_count)
    def _(i):
        @pl.loop(0, col_count)
        def _(k):
            block_copy(i, k).wait()

        acc[...] = jnp.zeros_like(acc)

        @pl.loop(0, (col_count + 1) // 2)
        def _(k):
            left = picked[i, :, :, pl.ds(pl.multiple_of(k * 2 * BS, 2 * BS), 2 * BS)]
            right = full[pl.ds(pl.multiple_of((col_first + 2 * k) * BS, BS), 2 * BS), :]
            acc[...] += jnp.dot(
                left.reshape(2 * BS, 2 * BS), right, preferred_element_type=jnp.float32
            )

        real = acc[:BS, :half] - acc[BS:, half:]
        imag = acc[:BS, half:] + acc[BS:, :half]
        block = ancestors[row_first + i] - r * row_blocks
        place = block // own_blocks
        within = pl.multiple_of(lax.rem(block, own_blocks) * BS, BS)
        turn = lax.rem(place - c + cols, cols)

        @pl.when(turn == 0)
        def _():
            keep[pl.ds(within, BS), :half] = real
            keep[pl.ds(within, BS), half:] = imag

        @pl.when(turn > 0)
        def _():
            send[turn - 1, pl.ds(within, BS), :half] = real.astype(send.dtype)
            send[turn - 1, pl.ds(within, BS), half:] = imag.astype(send.dtype)

        mixed = -(weight_real * imag + weight_imag * real)
        across = half // BC
        per_device = own_blocks * (BS // BR) * across
        first = lax.rem(c - place + cols, cols) * per_device + lax.rem(block, own_blocks) * (
            BS // BR
        ) * across
        for group in range(BS // BR):
            for j in range(across):
                tile = owner[first + group * across + j]
                tiles[tile] += mixed[group * BR : (group + 1) * BR, j * BC : (j + 1) * BC]

        rows_of = full[pl.ds(pl.multiple_of((row_first + i) * BS, BS), BS), :]
        real_high = real.astype(jnp.bfloat16)
        imag_high = imag.astype(jnp.bfloat16)
        real_low = (real - real_high.astype(jnp.float32)).astype(jnp.bfloat16)
        imag_low = (imag - imag_high.astype(jnp.float32)).astype(jnp.bfloat16)
        left = jnp.concatenate([rows_of[:, :half], rows_of[:, half:]], axis=0)
        left = jnp.concatenate([left, left], axis=0)
        right = jnp.concatenate(
            [
                jnp.concatenate([real_high, imag_high], axis=1),
                jnp.concatenate([-imag_high, real_high], axis=1),
                jnp.concatenate([real_low, imag_low], axis=1),
                jnp.concatenate([-imag_low, real_low], axis=1),
            ],
            axis=0,
        )
        diag[...] += lax.dot_general(
            left, right, (((0,), (0,)), ((), ())), preferred_element_type=jnp.float32
        )

    part = half // (rows * cols)
    for row in range(rows):
        for step in range(cols):
            target = row * cols + lax.rem(c + step, cols)
            value = diag[pl.ds(pl.multiple_of(target * part, part), part), :]
            if step == 0:
                diag_keep[row] = value
            else:
                diag_send[step - 1, row] = value.astype(diag_send.dtype)


def body(inverse, factor, dinv, ancestors, owner, weight_table, pole_slot):
    rows = lax.axis_size("row")
    cols = lax.axis_size("col")
    poles = lax.axis_size("pole")
    r = lax.axis_index("row")
    c = lax.axis_index("col")
    grid = ("row", "col")
    tile_count = poles * rows * cols
    here = inverse[0]
    wide = factor.shape[3]
    half = wide // 2
    rows_here = here.shape[1] // cols
    row_blocks = here.shape[1] // BS
    col_blocks = here.shape[2] // BS
    selected = ancestors.shape[1]
    part = half // (rows * cols)
    everyone = lambda r: True

    owners = [owner[:, 0]]
    for step in range(1, cols):
        owners.append(lax.ppermute(owner[:, 0], grid, shift_pairs(rows, cols, step, everyone)))
    pieces = gather_pieces(factor[0, 0], rows, cols)
    places = [(offset, step) for _, offset, step in pieces]

    smem = pl.BlockSpec(memory_space=pltpu.SMEM)
    vmem = pl.BlockSpec(memory_space=pltpu.VMEM)
    whole = pl.BlockSpec(memory_space=pl.ANY)
    others = max(1, cols - 1)
    keep, send, diag_keep, diag_send, tiles = pl.pallas_call(
        functools.partial(local_kernel, places, rows, cols),
        out_shape=(
            jax.ShapeDtypeStruct((rows_here, wide), jnp.float32),
            jax.ShapeDtypeStruct((others, rows_here, wide), jnp.bfloat16),
            jax.ShapeDtypeStruct((rows, part, wide), jnp.float32),
            jax.ShapeDtypeStruct((others, rows, part, wide), jnp.bfloat16),
            jax.ShapeDtypeStruct((tile_count, BR, BC), jnp.float32),
        ),
        in_specs=[smem] * 4 + [whole] * (1 + len(pieces)),
        out_specs=(vmem,) * 5,
        scratch_shapes=[
            pltpu.VMEM(((selected + 1) * BS, wide), jnp.bfloat16),
            pltpu.VMEM((row_blocks, 2, BS, col_blocks * BS), jnp.bfloat16),
            pltpu.VMEM((2 * BS, wide), jnp.float32),
            pltpu.VMEM((half, wide), jnp.float32),
            pltpu.SemaphoreType.DMA((row_blocks,)),
            pltpu.SemaphoreType.DMA((len(pieces),)),
        ],
        compiler_params=pltpu.CompilerParams(vmem_limit_bytes=40 * 1024 * 1024),
        name="local_products",
    )(
        ancestors[0],
        weight_table,
        pole_slot,
        jnp.concatenate(owners),
        here,
        *[piece for piece, _, _ in pieces],
    )

    over_cols = diag_keep
    for step in range(1, cols):
        pairs = shift_pairs(rows, cols, step, everyone)
        over_cols = over_cols + lax.ppermute(diag_send[step - 1], grid, pairs)
    mixed = lax.dynamic_index_in_dim(over_cols, r, 0, keepdims=False)
    rounded = over_cols.astype(jnp.bfloat16)
    for step in range(1, rows):
        outgoing = lax.dynamic_index_in_dim(rounded, (r + step) % rows, 0, keepdims=False)
        mixed = mixed + lax.ppermute(
            outgoing, "row", [(i, (i + step) % rows) for i in range(rows)]
        )
    diag_inverse = dinv + mixed.reshape(dinv.shape)

    weight_real = weight_table[0, pole_slot[0]]
    weight_imag = weight_table[1, pole_slot[0]]
    share = weight_real * diag_inverse[:, 0, :, 1] + weight_imag * diag_inverse[:, 0, :, 0]
    share = lax.optimization_barrier(share)
    shares = [share]
    for step in range(1, poles):
        shares.append(lax.ppermute(share, "pole", [(i, i ^ step) for i in range(poles)]))
    while len(shares) > 1:
        shares = [a + b for a, b in zip(shares[::2], shares[1::2])]
    density_diag = shares[0]

    column = keep
    for step in range(1, cols):
        pairs = shift_pairs(rows, cols, step, everyone)
        column = column + lax.ppermute(send[step - 1], grid, pairs)
    own_blocks = rows_here // BS
    listed = ((r * cols + c) * own_blocks + jnp.arange(own_blocks))[:, None] == ancestors[0][None]
    listed = jnp.any(listed, axis=1)[:, None, None]
    column = jnp.where(listed, -column.reshape(own_blocks, BS, wide), 0.0)
    column_out = column.reshape(rows_here, 1, 1, 2, half)

    arrived = lax.all_to_all(tiles, ("pole", "row", "col"), split_axis=0, concat_axis=0, tiled=True)
    tile_sum = jnp.sum(arrived, axis=0, keepdims=True)
    return (column_out, diag_inverse, density_diag, tile_sum)


def solution(mesh):
    in_specs = (
        P("pole", None, "row", "col"),
        P("pole", None, ("row", "col"), None),
        P(("row", "col"), "pole", None, None, None),
        P(),
        P(("row", "col"), None),
        P(),
        P("pole"),
    )
    out_specs = (
        P(("row", "col"), "pole", None, None, None),
        P(("row", "col"), "pole", None, None, None),
        P(("row", "col"), None, None),
        P(("pole", "row", "col"), None, None),
    )
    return jax.shard_map(body, mesh=mesh, in_specs=in_specs, out_specs=out_specs, check_vma=False)
```

```python
import functools

import jax
import jax.numpy as jnp
from jax import lax
from jax.experimental import pallas as pl
from jax.experimental.pallas import tpu as pltpu
from jax.sharding import PartitionSpec as P

BS = 128
BR = 8
BC = 128
MIB = 1 << 20


def shift_pairs(rows, cols, step, valid):
    return [
        (r * cols + c, r * cols + (c + step) % cols)
        for r in range(rows)
        if valid(r)
        for c in range(cols)
    ]


def gather_stages(shard, rows, cols):
    grid = ("row", "col")
    if rows != 4:
        full = lax.all_gather(shard, grid, axis=0, tiled=True).reshape((rows, cols) + shard.shape)
        c = lax.axis_index("col")
        stages = []
        for row in range(rows):
            line = [lax.dynamic_index_in_dim(full[row], (c - step) % cols, 0, False) for step in range(cols)]
            stages.append([[piece] for piece in line])
        return stages, [[row] * rows for row in range(rows)]
    sources = [[0, 1, 2, 3], [1, 0, 3, 2], [2, 2, 1, 1], [3, 3, 0, 0]]
    outer = [(0, 1), (1, 0), (2, 3), (3, 2)]
    inner = [(1, 2), (2, 1)]
    r = lax.axis_index("row")
    middle = jnp.logical_or(r == 1, r == 2)
    height = shard.shape[0] // 2
    stages = [[[] for _ in range(cols)] for _ in range(rows)]
    for part in (0, 1):
        own = shard[part * height : (part + 1) * height]
        near = lax.ppermute(own, "row", outer)
        cross = lax.ppermute(own, "row", inner)
        cross_out = lax.ppermute(cross, "row", outer)
        far = lax.ppermute(near, "row", inner)
        far_out = lax.ppermute(far, "row", outer)
        line = [
            lambda: own,
            lambda: near,
            lambda: jnp.where(middle, cross, cross_out),
            lambda: jnp.where(middle, far, far_out),
        ]
        last = None
        for stage, make in enumerate(line):
            piece = make()
            stages[stage][0].append(piece)
            leaving = piece
            if last is not None:
                leaving, _ = lax.optimization_barrier((piece, last))
            for step in range(1, cols):
                pairs = shift_pairs(rows, cols, step, lambda r: True)
                last = lax.ppermute(leaving, grid, pairs)
                stages[stage][step].append(last)
    return stages, sources


def counts_of(ancestors, inverse_rows, inverse_cols):
    r = lax.axis_index("row")
    c = lax.axis_index("col")

    def below(limit):
        total = jnp.int32(0)
        for i in range(ancestors.shape[0]):
            total = total + (ancestors[i] < limit).astype(jnp.int32)
        return total

    row_first, row_last = below(r * inverse_rows), below((r + 1) * inverse_rows)
    col_first, col_last = below(c * inverse_cols), below((c + 1) * inverse_cols)
    return row_first, row_last - row_first, col_first, col_last


def pick_kernel(stage_blocks, ancestors, inverse, picked, row_sem):
    row_blocks = inverse.shape[1] // BS
    col_blocks = inverse.shape[2] // BS
    r = lax.axis_index("row")
    c = lax.axis_index("col")
    row_first, row_count, col_first, col_last = counts_of(ancestors, row_blocks, col_blocks)

    def block_copy(i, k):
        row = pl.multiple_of((ancestors[row_first + i] - r * row_blocks) * BS, BS)
        col = pl.multiple_of((ancestors[k] - c * col_blocks) * BS, BS)
        return pltpu.make_async_copy(
            inverse.at[:, pl.ds(row, BS), pl.ds(col, BS)],
            picked.at[i, :, :, pl.ds(pl.multiple_of(k * BS, BS), BS)],
            row_sem.at[i],
        )

    @pl.loop(0, row_count)
    def _(i):
        @pl.loop(col_first, col_last)
        def _(k):
            block_copy(i, k).start()

    start = col_first // stage_blocks * stage_blocks
    end = (col_last + stage_blocks - 1) // stage_blocks * stage_blocks

    @pl.loop(0, row_count)
    def _(i):
        def clear(k):
            place = pl.ds(pl.multiple_of(k * BS, BS), BS)
            picked[i, :, :, place] = jnp.zeros((2, BS, BS), picked.dtype)

        pl.loop(start, col_first)(clear)
        pl.loop(col_last, end)(clear)

        @pl.loop(col_first, col_last)
        def _(k):
            block_copy(i, k).wait()


def source_row(sources, stage):
    r = lax.axis_index("row")
    total = jnp.int32(0)
    for row, source in enumerate(sources[stage]):
        total = total + jnp.where(r == row, source, 0)
    return total


def fill(full, pieces, sources, stage, cols):
    c = lax.axis_index("col")
    source = source_row(sources, stage)
    chunks = len(pieces) // cols
    height = pieces[0].shape[0]
    for step in range(cols):
        shard = source * cols + lax.rem(c - step + cols, cols)
        for chunk in range(chunks):
            start = pl.multiple_of((shard * chunks + chunk) * height, height)
            full[pl.ds(start, height), :] = pieces[step * chunks + chunk][...]


def multiply(acc, picked, full, i, source, stage_blocks, col_first, col_last):
    low = source * stage_blocks

    @pl.when(jnp.logical_and(low < col_last, low + stage_blocks > col_first))
    def _():
        size = stage_blocks * BS
        place = pl.ds(pl.multiple_of(low * BS, BS), size)
        left = picked[i, :, :, place].reshape(2 * BS, size)
        acc[...] += jnp.dot(left, full[place, :], preferred_element_type=jnp.float32)


def combine(acc):
    half = acc.shape[1] // 2
    return acc[:BS, :half] - acc[BS:, half:], acc[:BS, half:] + acc[BS:, :half]


def first_kernel(sources, rows, cols, total_blocks, ancestors, picked, *refs):
    early, full, acc = refs[-3:]
    pieces = refs[:-3]
    each = len(pieces) // (rows - 1)
    stage_blocks = ancestors.shape[0] // rows
    half = acc.shape[1] // 2
    col_blocks = total_blocks // cols
    for stage in range(rows - 1):
        fill(full, pieces[stage * each : (stage + 1) * each], sources, stage, cols)
    _, row_count, col_first, col_last = counts_of(ancestors, early.shape[0], col_blocks)

    @pl.loop(0, row_count)
    def _(i):
        acc[...] = jnp.zeros_like(acc)
        for stage in range(rows - 1):
            source = source_row(sources, stage)
            multiply(acc, picked, full, i, source, stage_blocks, col_first, col_last)
        real, imag = combine(acc)
        early[i, :, :half] = real
        early[i, :, half:] = imag


def last_kernel(sources, rows, cols, total_blocks, ancestors, table, slot, owner, picked, early, *refs):
    keep, send, diag_keep, diag_send, tiles, full, acc, diag = refs[-8:]
    pieces = refs[:-8]
    each = len(pieces) // rows
    stage_blocks = ancestors.shape[0] // rows
    wide = acc.shape[1]
    half = wide // 2
    row_blocks = early.shape[0]
    own_blocks = row_blocks // cols
    r = lax.axis_index("row")
    c = lax.axis_index("col")
    for stage in range(rows):
        fill(full, pieces[stage * each : (stage + 1) * each], sources, stage, cols)
    row_first, row_count, col_first, col_last = counts_of(ancestors, row_blocks, total_blocks // cols)
    diag[...] = jnp.zeros_like(diag)
    tiles[...] = jnp.zeros_like(tiles)
    weight_real = table[0, slot[0]]
    weight_imag = table[1, slot[0]]

    @pl.loop(0, row_count)
    def _(i):
        acc[:BS, :] = early[i]
        acc[BS:, :] = jnp.zeros((BS, wide), jnp.float32)
        source = source_row(sources, rows - 1)
        multiply(acc, picked, full, i, source, stage_blocks, col_first, col_last)
        real, imag = combine(acc)
        block = ancestors[row_first + i] - r * row_blocks
        place = block // own_blocks
        within = pl.multiple_of(lax.rem(block, own_blocks) * BS, BS)
        turn = lax.rem(place - c + cols, cols)

        @pl.when(turn == 0)
        def _():
            keep[pl.ds(within, BS), :half] = real
            keep[pl.ds(within, BS), half:] = imag

        @pl.when(turn > 0)
        def _():
            send[turn - 1, pl.ds(within, BS), :half] = real.astype(send.dtype)
            send[turn - 1, pl.ds(within, BS), half:] = imag.astype(send.dtype)

        mixed = -(weight_real * imag + weight_imag * real)
        across = half // BC
        per_device = own_blocks * (BS // BR) * across
        first = lax.rem(c - place + cols, cols) * per_device + lax.rem(block, own_blocks) * (
            BS // BR
        ) * across
        for group in range(BS // BR):
            for j in range(across):
                tile = owner[first + group * across + j]
                tiles[tile] += mixed[group * BR : (group + 1) * BR, j * BC : (j + 1) * BC]

        rows_of = full[pl.ds(pl.multiple_of((row_first + i) * BS, BS), BS), :]
        real_high = real.astype(jnp.bfloat16)
        imag_high = imag.astype(jnp.bfloat16)
        real_low = (real - real_high.astype(jnp.float32)).astype(jnp.bfloat16)
        imag_low = (imag - imag_high.astype(jnp.float32)).astype(jnp.bfloat16)
        left = jnp.concatenate([rows_of[:, :half], rows_of[:, half:]], axis=0)
        left = jnp.concatenate([left, left], axis=0)
        right = jnp.concatenate(
            [
                jnp.concatenate([real_high, imag_high], axis=1),
                jnp.concatenate([-imag_high, real_high], axis=1),
                jnp.concatenate([real_low, imag_low], axis=1),
                jnp.concatenate([-imag_low, real_low], axis=1),
            ],
            axis=0,
        )
        diag[...] += lax.dot_general(
            left, right, (((0,), (0,)), ((), ())), preferred_element_type=jnp.float32
        )

    part = half // (rows * cols)
    for row in range(rows):
        for step in range(cols):
            target = row * cols + lax.rem(c + step, cols)
            value = diag[pl.ds(pl.multiple_of(target * part, part), part), :]
            if step == 0:
                diag_keep[row] = value
            else:
                diag_send[step - 1, row] = value.astype(diag_send.dtype)


def regroup_kernel(rows, kept, *refs):
    rounded, own = refs[-2:]
    arrived = refs[:-2]
    r = lax.axis_index("row")

    def total(row):
        value = kept[row]
        for ref in arrived:
            value = value + ref[row].astype(jnp.float32)
        return value

    own[...] = total(r)
    for step in range(1, rows):
        rounded[step - 1] = total(lax.rem(r + step, rows)).astype(rounded.dtype)


def body(inverse, factor, dinv, ancestors, owner, weight_table, pole_slot):
    rows = lax.axis_size("row")
    cols = lax.axis_size("col")
    poles = lax.axis_size("pole")
    r = lax.axis_index("row")
    c = lax.axis_index("col")
    grid = ("row", "col")
    tile_count = poles * rows * cols
    here = inverse[0]
    wide = factor.shape[3]
    half = wide // 2
    rows_here = here.shape[1] // cols
    row_blocks = here.shape[1] // BS
    col_blocks = here.shape[2] // BS
    selected = ancestors.shape[1]
    part = half // (rows * cols)
    everyone = lambda r: True

    owners = [owner[:, 0]]
    for step in range(1, cols):
        owners.append(lax.ppermute(owner[:, 0], grid, shift_pairs(rows, cols, step, everyone)))
    smem = pl.BlockSpec(memory_space=pltpu.SMEM)
    vmem = pl.BlockSpec(memory_space=pltpu.VMEM)
    whole = pl.BlockSpec(memory_space=pl.ANY)
    flat_dinv = lax.optimization_barrier(dinv.reshape(part, wide))
    stages, sources = gather_stages(factor[0, 0], rows, cols)
    stages = [[chunk for step in stage for chunk in step] for stage in stages]
    stage_blocks = selected // rows
    picked = pl.pallas_call(
        functools.partial(pick_kernel, stage_blocks),
        out_shape=jax.ShapeDtypeStruct((row_blocks, 2, BS, selected * BS), jnp.bfloat16),
        in_specs=[smem, whole],
        out_specs=vmem,
        scratch_shapes=[pltpu.SemaphoreType.DMA((row_blocks,))],
        compiler_params=pltpu.CompilerParams(vmem_limit_bytes=12 * MIB),
        cost_estimate=pl.CostEstimate(flops=0, bytes_accessed=8 * MIB, transcendentals=0),
        name="pick_blocks",
    )(ancestors[0], here)
    products = 2 * row_blocks * BS * 2 * wide * selected * BS // cols
    early_pieces = [piece for stage in stages[:-1] for piece in stage]
    early = pl.pallas_call(
        functools.partial(first_kernel, sources, rows, cols, col_blocks * cols),
        out_shape=jax.ShapeDtypeStruct((row_blocks, BS, wide), jnp.float32),
        in_specs=[smem, vmem] + [vmem] * len(early_pieces),
        out_specs=vmem,
        scratch_shapes=[
            pltpu.VMEM((selected * BS, wide), jnp.bfloat16),
            pltpu.VMEM((2 * BS, wide), jnp.float32),
        ],
        compiler_params=pltpu.CompilerParams(vmem_limit_bytes=32 * MIB),
        cost_estimate=pl.CostEstimate(flops=products, bytes_accessed=4 * MIB, transcendentals=0),
        name="first_products",
    )(ancestors[0], picked, *early_pieces)
    all_pieces = [piece for stage in stages for piece in stage]
    others = max(1, cols - 1)
    keep, send, diag_keep, diag_send, tiles = pl.pallas_call(
        functools.partial(last_kernel, sources, rows, cols, col_blocks * cols),
        out_shape=(
            jax.ShapeDtypeStruct((rows_here, wide), jnp.float32),
            jax.ShapeDtypeStruct((others, rows_here, wide), jnp.bfloat16),
            jax.ShapeDtypeStruct((rows, part, wide), jnp.float32),
            jax.ShapeDtypeStruct((others, rows, part, wide), jnp.bfloat16),
            jax.ShapeDtypeStruct((tile_count, BR, BC), jnp.float32),
        ),
        in_specs=[smem] * 4 + [vmem] * (2 + len(all_pieces)),
        out_specs=(vmem,) * 5,
        scratch_shapes=[
            pltpu.VMEM((selected * BS, wide), jnp.bfloat16),
            pltpu.VMEM((2 * BS, wide), jnp.float32),
            pltpu.VMEM((half, wide), jnp.float32),
        ],
        compiler_params=pltpu.CompilerParams(vmem_limit_bytes=36 * MIB),
        cost_estimate=pl.CostEstimate(flops=products, bytes_accessed=8 * MIB, transcendentals=0),
        name="last_products",
    )(ancestors[0], weight_table, pole_slot, jnp.concatenate(owners), picked, early, *all_pieces)

    everyone_pairs = [shift_pairs(rows, cols, step, everyone) for step in range(cols)]
    arrived = [
        lax.ppermute(diag_send[step - 1], grid, everyone_pairs[step]) for step in range(1, cols)
    ]
    rounded, mixed = pl.pallas_call(
        functools.partial(regroup_kernel, rows),
        out_shape=(
            jax.ShapeDtypeStruct((max(1, rows - 1), part, wide), jnp.bfloat16),
            jax.ShapeDtypeStruct((part, wide), jnp.float32),
        ),
        in_specs=[vmem] * (1 + len(arrived)),
        out_specs=(vmem,) * 2,
        name="regroup",
    )(diag_keep, *arrived)
    for step in range(1, rows):
        mixed = mixed + lax.ppermute(
            rounded[step - 1], "row", [(i, (i + step) % rows) for i in range(rows)]
        )
    mixed = flat_dinv + mixed
    diag_inverse = mixed.reshape(dinv.shape)

    weight_real = weight_table[0, pole_slot[0]]
    weight_imag = weight_table[1, pole_slot[0]]
    share = weight_real * mixed[:, half:] + weight_imag * mixed[:, :half]
    share = lax.optimization_barrier(share)
    shares = [share]
    for step in range(1, poles):
        shares.append(lax.ppermute(share, "pole", [(i, i ^ step) for i in range(poles)]))
    while len(shares) > 1:
        shares = [a + b for a, b in zip(shares[::2], shares[1::2])]
    density_diag = shares[0].reshape(part, 1, half)

    own_blocks = rows_here // BS
    listed = ((r * cols + c) * own_blocks + jnp.arange(own_blocks))[:, None] == ancestors[0][None]
    listed = jnp.repeat(jnp.any(listed, axis=1), BS)[:, None, None, None, None]
    laid = (rows_here, 1, 1, 2, half)
    column = lax.optimization_barrier(keep.reshape(laid))
    for step in range(1, cols):
        leaving = lax.optimization_barrier(send[step - 1].reshape(laid))
        column = column + lax.ppermute(leaving, grid, everyone_pairs[step])
    column_out = jnp.where(listed, -column, 0.0)

    scattered = lax.all_to_all(tiles, ("pole", "row", "col"), split_axis=0, concat_axis=0, tiled=True)
    tile_sum = jnp.sum(scattered, axis=0, keepdims=True)
    return (column_out, diag_inverse, density_diag, tile_sum)


def solution(mesh):
    in_specs = (
        P("pole", None, "row", "col"),
        P("pole", None, ("row", "col"), None),
        P(("row", "col"), "pole", None, None, None),
        P(),
        P(("row", "col"), None),
        P(),
        P("pole"),
    )
    out_specs = (
        P(("row", "col"), "pole", None, None, None),
        P(("row", "col"), "pole", None, None, None),
        P(("row", "col"), None, None),
        P(("pole", "row", "col"), None, None),
    )
    return jax.shard_map(body, mesh=mesh, in_specs=in_specs, out_specs=out_specs, check_vma=False)
```

```python
import functools

import jax
import jax.numpy as jnp
from jax import lax
from jax.experimental import pallas as pl
from jax.experimental.pallas import tpu as pltpu
from jax.sharding import PartitionSpec as P


BS = 128
BR = 8
BC = 128
MIB = 1 << 20


def shift_pairs(rows, cols, step, valid):
    return [
        (r * cols + c, r * cols + (c + step) % cols)
        for r in range(rows)
        if valid(r)
        for c in range(cols)
    ]


def gather_stages(shard, rows, cols):
    grid = ("row", "col")
    if rows != 4:
        full = lax.all_gather(shard, grid, axis=0, tiled=True).reshape((rows, cols) + shard.shape)
        c = lax.axis_index("col")
        stages = []
        for row in range(rows):
            line = [lax.dynamic_index_in_dim(full[row], (c - step) % cols, 0, False) for step in range(cols)]
            stages.append([[piece] for piece in line])
        return stages, [[row] * rows for row in range(rows)]
    sources = [[0, 1, 2, 3], [1, 0, 3, 2], [2, 2, 1, 1], [3, 3, 0, 0]]
    outer = [(0, 1), (1, 0), (2, 3), (3, 2)]
    inner = [(1, 2), (2, 1)]
    r = lax.axis_index("row")
    middle = jnp.logical_or(r == 1, r == 2)
    height = shard.shape[0] // 2
    stages = [[[] for _ in range(cols)] for _ in range(rows)]
    for part in (0, 1):
        own = shard[part * height : (part + 1) * height]
        near = lax.ppermute(own, "row", outer)
        cross = lax.ppermute(own, "row", inner)
        cross_out = lax.ppermute(cross, "row", outer)
        far = lax.ppermute(near, "row", inner)
        far_out = lax.ppermute(far, "row", outer)
        line = [
            lambda: own,
            lambda: near,
            lambda: jnp.where(middle, cross, cross_out),
            lambda: jnp.where(middle, far, far_out),
        ]
        last = None
        opened = []
        for stage, make in enumerate(line):
            piece = make()
            stages[stage][0].append(piece)
            leaving = piece
            if last is not None:
                leaving, _ = lax.optimization_barrier((piece, last))
            for step in range(1, cols):
                if stage == 1 and part == 1:
                    relayed, _ = lax.optimization_barrier((opened[step - 1], far_out))
                    stages[stage][step].append(lax.ppermute(relayed, "row", outer))
                    continue
                pairs = shift_pairs(rows, cols, step, lambda r: True)
                last = lax.ppermute(leaving, grid, pairs)
                stages[stage][step].append(last)
                if stage == 0:
                    opened.append(last)
    return stages, sources


def counts_of(ancestors, inverse_rows, inverse_cols):
    r = lax.axis_index("row")
    c = lax.axis_index("col")

    def below(limit):
        total = jnp.int32(0)
        for i in range(ancestors.shape[0]):
            total = total + (ancestors[i] < limit).astype(jnp.int32)
        return total

    row_first, row_last = below(r * inverse_rows), below((r + 1) * inverse_rows)
    col_first, col_last = below(c * inverse_cols), below((c + 1) * inverse_cols)
    return row_first, row_last - row_first, col_first, col_last


def pick_kernel(stage_blocks, ancestors, inverse, picked, row_sem):
    row_blocks = inverse.shape[1] // BS
    col_blocks = inverse.shape[2] // BS
    r = lax.axis_index("row")
    c = lax.axis_index("col")
    row_first, row_count, col_first, col_last = counts_of(ancestors, row_blocks, col_blocks)

    def block_copy(i, k):
        row = pl.multiple_of((ancestors[row_first + i] - r * row_blocks) * BS, BS)
        col = pl.multiple_of((ancestors[k] - c * col_blocks) * BS, BS)
        return pltpu.make_async_copy(
            inverse.at[:, pl.ds(row, BS), pl.ds(col, BS)],
            picked.at[i, :, :, pl.ds(pl.multiple_of(k * BS, BS), BS)],
            row_sem.at[i],
        )

    @pl.loop(0, row_count)
    def _(i):
        @pl.loop(col_first, col_last)
        def _(k):
            block_copy(i, k).start()

    start = col_first // stage_blocks * stage_blocks
    end = (col_last + stage_blocks - 1) // stage_blocks * stage_blocks

    @pl.loop(0, row_count)
    def _(i):
        def clear(k):
            place = pl.ds(pl.multiple_of(k * BS, BS), BS)
            picked[i, :, :, place] = jnp.zeros((2, BS, BS), picked.dtype)

        pl.loop(start, col_first)(clear)
        pl.loop(col_last, end)(clear)

        @pl.loop(col_first, col_last)
        def _(k):
            block_copy(i, k).wait()


def source_row(sources, stage):
    r = lax.axis_index("row")
    total = jnp.int32(0)
    for row, source in enumerate(sources[stage]):
        total = total + jnp.where(r == row, source, 0)
    return total


def fill(full, pieces, sources, stage, cols):
    c = lax.axis_index("col")
    source = source_row(sources, stage)
    chunks = len(pieces) // cols
    height = pieces[0].shape[0]
    for step in range(cols):
        shard = source * cols + lax.rem(c - step + cols, cols)
        for chunk in range(chunks):
            start = pl.multiple_of((shard * chunks + chunk) * height, height)
            full[pl.ds(start, height), :] = pieces[step * chunks + chunk][...]


def multiply(acc, picked, full, i, source, stage_blocks, col_first, col_last):
    low = source * stage_blocks

    @pl.when(jnp.logical_and(low < col_last, low + stage_blocks > col_first))
    def _():
        size = stage_blocks * BS
        place = pl.ds(pl.multiple_of(low * BS, BS), size)
        left = picked[i, :, :, place].reshape(2 * BS, size)
        acc[...] += jnp.dot(left, full[place, :], preferred_element_type=jnp.float32)


def combine(acc):
    half = acc.shape[1] // 2
    return acc[:BS, :half] - acc[BS:, half:], acc[:BS, half:] + acc[BS:, :half]


def stage_kernel(sources, stages, added, rows, cols, total_blocks, ancestors, picked, *refs):
    early, full, acc = refs[-3:]
    before = refs[0] if added else None
    pieces = refs[1 if added else 0 : -3]
    each = len(pieces) // len(stages)
    stage_blocks = ancestors.shape[0] // rows
    half = acc.shape[1] // 2
    for n, stage in enumerate(stages):
        fill(full, pieces[n * each : (n + 1) * each], sources, stage, cols)
    _, row_count, col_first, col_last = counts_of(ancestors, early.shape[0], total_blocks // cols)

    @pl.loop(0, row_count)
    def _(i):
        if added:
            acc[:BS, :] = before[i]
            acc[BS:, :] = jnp.zeros((BS, 2 * half), jnp.float32)
        else:
            acc[...] = jnp.zeros_like(acc)
        for stage in stages:
            source = source_row(sources, stage)
            multiply(acc, picked, full, i, source, stage_blocks, col_first, col_last)
        real, imag = combine(acc)
        early[i, :, :half] = real
        early[i, :, half:] = imag


def last_kernel(sources, rows, cols, total_blocks, ancestors, table, slot, owner, picked, early, *refs):
    keep, send, diag_keep, diag_send, full, acc, diag, tiles = refs[-8:]
    pieces = refs[:-8]
    each = len(pieces) // rows
    stage_blocks = ancestors.shape[0] // rows
    wide = acc.shape[1]
    half = wide // 2
    row_blocks = early.shape[0]
    own_blocks = row_blocks // cols
    r = lax.axis_index("row")
    c = lax.axis_index("col")
    for stage in range(rows):
        fill(full, pieces[stage * each : (stage + 1) * each], sources, stage, cols)
    row_first, row_count, col_first, col_last = counts_of(ancestors, row_blocks, total_blocks // cols)
    diag[...] = jnp.zeros_like(diag)
    tiles[...] = jnp.zeros_like(tiles)
    weight_real = table[0, slot[0]]
    weight_imag = table[1, slot[0]]

    @pl.loop(0, row_count)
    def _(i):
        acc[:BS, :] = early[i]
        acc[BS:, :] = jnp.zeros((BS, wide), jnp.float32)
        source = source_row(sources, rows - 1)
        multiply(acc, picked, full, i, source, stage_blocks, col_first, col_last)
        real, imag = combine(acc)
        block = ancestors[row_first + i] - r * row_blocks
        place = block // own_blocks
        within = pl.multiple_of(lax.rem(block, own_blocks) * BS, BS)
        turn = lax.rem(place - c + cols, cols)

        @pl.when(turn == 0)
        def _():
            keep[pl.ds(within, BS), :half] = real
            keep[pl.ds(within, BS), half:] = imag

        @pl.when(turn > 0)
        def _():
            send[turn - 1, pl.ds(within, BS), :half] = real.astype(send.dtype)
            send[turn - 1, pl.ds(within, BS), half:] = imag.astype(send.dtype)

        mixed = -(weight_real * imag + weight_imag * real)
        across = half // BC
        per_device = own_blocks * (BS // BR) * across
        first = lax.rem(c - place + cols, cols) * per_device + lax.rem(block, own_blocks) * (
            BS // BR
        ) * across
        for group in range(BS // BR):
            for j in range(across):
                tile = owner[first + group * across + j]
                tiles[j, tile] += mixed[group * BR : (group + 1) * BR, j * BC : (j + 1) * BC]

        rows_of = full[pl.ds(pl.multiple_of((row_first + i) * BS, BS), BS), :]
        real_high = real.astype(jnp.bfloat16)
        imag_high = imag.astype(jnp.bfloat16)
        real_low = (real - real_high.astype(jnp.float32)).astype(jnp.bfloat16)
        imag_low = (imag - imag_high.astype(jnp.float32)).astype(jnp.bfloat16)
        left = jnp.concatenate([rows_of[:, :half], rows_of[:, half:]], axis=0)
        left = jnp.concatenate([left, left], axis=0)
        right = jnp.concatenate(
            [
                jnp.concatenate([real_high, imag_high], axis=1),
                jnp.concatenate([-imag_high, real_high], axis=1),
                jnp.concatenate([real_low, imag_low], axis=1),
                jnp.concatenate([-imag_low, real_low], axis=1),
            ],
            axis=0,
        )
        diag[...] += lax.dot_general(
            left, right, (((0,), (0,)), ((), ())), preferred_element_type=jnp.float32
        )

    part = half // (rows * cols)
    poles = tiles.shape[1] // (rows * cols)
    for row in range(rows):
        for step in range(cols):
            place = row * cols + lax.rem(c + step, cols)
            value = diag[pl.ds(pl.multiple_of(place * part, part), part), :]
            if step == 0:
                diag_keep[row, :part] = value
                diag_keep[row, part:] = jnp.zeros((BR, wide), jnp.float32)
            else:
                diag_send[step - 1, row, :part] = value.astype(diag_send.dtype)
                diag_send[step - 1, row, part:] = jnp.zeros((BR, wide), diag_send.dtype)
            for pole in range(poles):
                total = tiles[0, pole * rows * cols + place]
                for j in range(1, half // BC):
                    total = total + tiles[j, pole * rows * cols + place]
                if step == 0:
                    diag_keep[row, part:, 2 * pole * BC : (2 * pole + 1) * BC] = total
                else:
                    diag_send[step - 1, row, part:, 2 * pole * BC : 2 * (pole + 1) * BC] = halves(total)


def halves(value):
    high = value.astype(jnp.bfloat16)
    low = (value - high.astype(jnp.float32)).astype(jnp.bfloat16)
    return jnp.concatenate([high, low], axis=1)


def regroup_kernel(poles, rows, kept, *refs):
    *rounded, own = refs[-rows:]
    arrived = refs[:-rows]
    part = own.shape[0] - BR
    r = lax.axis_index("row")

    def total(row):
        value = kept[row]
        for ref in arrived:
            value = value + ref[row].astype(jnp.float32)
        return value

    own[...] = total(r)
    for step in range(1, rows):
        value = total(lax.rem(r + step, rows))
        out = rounded[step - 1]
        out[:part] = value[:part].astype(out.dtype)
        for pole in range(poles):
            first = 2 * pole * BC
            band = value[part:, first : first + BC] + value[part:, first + BC : first + 2 * BC]
            out[part:, first : first + 2 * BC] = halves(band)


def finish_kernel(poles, table, slot, flat_dinv, own, *refs):
    diag_out, message = refs[-2:]
    arrived = refs[:-2]
    part, wide = flat_dinv.shape
    half = wide // 2
    total = own[...]
    for ref in arrived:
        total = total + ref[...].astype(jnp.float32)
    block = flat_dinv[...] + total[:part]
    diag_out[...] = block
    weight_real = table[0, slot[0]]
    weight_imag = table[1, slot[0]]
    message[:part] = weight_real * block[:, half:] + weight_imag * block[:, :half]
    for pole in range(poles):
        first = 2 * pole * BC
        band = total[part:, first : first + BC] + total[part:, first + BC : first + 2 * BC]
        message[part:, pole * BC : (pole + 1) * BC] = band


def compute(inverse, factor, dinv, ancestors, owner, weight_table, pole_slot):
    rows = lax.axis_size("row")
    cols = lax.axis_size("col")
    poles = lax.axis_size("pole")
    r = lax.axis_index("row")
    c = lax.axis_index("col")
    grid = ("row", "col")
    tile_count = poles * rows * cols
    here = inverse[0]
    wide = factor.shape[3]
    half = wide // 2
    rows_here = here.shape[1] // cols
    row_blocks = here.shape[1] // BS
    col_blocks = here.shape[2] // BS
    selected = ancestors.shape[1]
    part = half // (rows * cols)
    everyone = lambda r: True

    owners = [owner[:, 0]]
    for step in range(1, cols):
        owners.append(lax.ppermute(owner[:, 0], grid, shift_pairs(rows, cols, step, everyone)))
    smem = pl.BlockSpec(memory_space=pltpu.SMEM)
    vmem = pl.BlockSpec(memory_space=pltpu.VMEM)
    whole = pl.BlockSpec(memory_space=pl.ANY)
    flat_dinv = lax.optimization_barrier(dinv.reshape(part, wide))
    stages, sources = gather_stages(factor[0, 0], rows, cols)
    stages = [[chunk for step in stage for chunk in step] for stage in stages]
    listed_blocks, _ = lax.optimization_barrier((ancestors[0], stages[1][0]))
    stage_blocks = selected // rows
    picked = pl.pallas_call(
        functools.partial(pick_kernel, stage_blocks),
        out_shape=jax.ShapeDtypeStruct((row_blocks, 2, BS, selected * BS), jnp.bfloat16),
        in_specs=[smem, pl.BlockSpec(memory_space=pltpu.HBM)],
        out_specs=vmem,
        scratch_shapes=[pltpu.SemaphoreType.DMA((row_blocks,))],
        compiler_params=pltpu.CompilerParams(vmem_limit_bytes=12 * MIB),
        cost_estimate=pl.CostEstimate(flops=0, bytes_accessed=8 * MIB, transcendentals=0),
        name="pick_blocks",
    )(listed_blocks, here)
    products = 2 * row_blocks * BS * 2 * wide * selected * BS // cols
    early = None
    for group in (tuple(range(rows - 2)), (rows - 2,)):
        added = early is not None
        group_pieces = [piece for stage in group for piece in stages[stage]]
        early = pl.pallas_call(
            functools.partial(stage_kernel, sources, group, added, rows, cols, col_blocks * cols),
            out_shape=jax.ShapeDtypeStruct((row_blocks, BS, wide), jnp.float32),
            in_specs=[smem, vmem] + [vmem] * (added + len(group_pieces)),
            out_specs=vmem,
            scratch_shapes=[
                pltpu.VMEM((selected * BS, wide), jnp.bfloat16),
                pltpu.VMEM((2 * BS, wide), jnp.float32),
            ],
            input_output_aliases={2: 0} if added else {},
            compiler_params=pltpu.CompilerParams(vmem_limit_bytes=32 * MIB),
            cost_estimate=pl.CostEstimate(
                flops=products * len(group) // rows, bytes_accessed=4 * MIB, transcendentals=0
            ),
            name="stage_products",
        )(ancestors[0], picked, *([early] if added else []), *group_pieces)
    all_pieces = [piece for stage in stages for piece in stage]
    others = max(1, cols - 1)
    keep, send, diag_keep, diag_send = pl.pallas_call(
        functools.partial(last_kernel, sources, rows, cols, col_blocks * cols),
        out_shape=(
            jax.ShapeDtypeStruct((rows_here, wide), jnp.float32),
            jax.ShapeDtypeStruct((others, rows_here, wide), jnp.bfloat16),
            jax.ShapeDtypeStruct((rows, part + BR, wide), jnp.float32),
            jax.ShapeDtypeStruct((others, rows, part + BR, wide), jnp.bfloat16),
        ),
        in_specs=[smem] * 4 + [vmem] * (2 + len(all_pieces)),
        out_specs=(vmem,) * 4,
        scratch_shapes=[
            pltpu.VMEM((selected * BS, wide), jnp.bfloat16),
            pltpu.VMEM((2 * BS, wide), jnp.float32),
            pltpu.VMEM((half, wide), jnp.float32),
            pltpu.VMEM((half // BC, tile_count, BR, BC), jnp.float32),
        ],
        compiler_params=pltpu.CompilerParams(vmem_limit_bytes=36 * MIB),
        cost_estimate=pl.CostEstimate(flops=products, bytes_accessed=8 * MIB, transcendentals=0),
        name="last_products",
    )(ancestors[0], weight_table, pole_slot, jnp.concatenate(owners), picked, early, *all_pieces)

    everyone_pairs = [shift_pairs(rows, cols, step, everyone) for step in range(cols)]
    arrived = [
        lax.ppermute(diag_send[step - 1], grid, everyone_pairs[step]) for step in range(1, cols)
    ]
    *rounded, own = pl.pallas_call(
        functools.partial(regroup_kernel, poles, rows),
        out_shape=(jax.ShapeDtypeStruct((part + BR, wide), jnp.bfloat16),) * (rows - 1)
        + (jax.ShapeDtypeStruct((part + BR, wide), jnp.float32),),
        in_specs=[vmem] * (1 + len(arrived)),
        out_specs=(vmem,) * rows,
        name="regroup",
    )(diag_keep, *arrived)
    parts = [
        lax.ppermute(rounded[step - 1], "row", [(i, (i + step) % rows) for i in range(rows)])
        for step in range(1, rows)
    ]
    flat_diag, message = pl.pallas_call(
        functools.partial(finish_kernel, poles),
        out_shape=(
            jax.ShapeDtypeStruct((part, wide), jnp.float32),
            jax.ShapeDtypeStruct((part + BR, half), jnp.float32),
        ),
        in_specs=[smem] * 2 + [vmem] * (2 + len(parts)),
        out_specs=(vmem,) * 2,
        name="finish",
    )(weight_table, pole_slot, flat_dinv, own, *parts)
    diag_inverse = flat_diag.reshape(dinv.shape)
    messages = [message]
    for step in range(1, poles):
        messages.append(lax.ppermute(message, "pole", [(i, i ^ step) for i in range(poles)]))
    while len(messages) > 1:
        messages = [a + b for a, b in zip(messages[::2], messages[1::2])]
    density_diag = messages[0][:part].reshape(part, 1, half)
    tile_sum = lax.dynamic_slice(messages[0], (part, lax.axis_index("pole") * BC), (BR, BC))[None]

    own_blocks = rows_here // BS
    listed = ((r * cols + c) * own_blocks + jnp.arange(own_blocks))[:, None] == ancestors[0][None]
    listed = jnp.repeat(jnp.any(listed, axis=1), BS * wide // BC)[:, None]

    def laid(value):
        value = value.reshape(rows_here, 2, half // BC, BC).transpose(0, 2, 1, 3)
        return lax.optimization_barrier(value.reshape(rows_here * wide // BC, BC))

    column = laid(keep)
    for step in range(1, cols):
        leaving = laid(send[step - 1])
        column = column + lax.ppermute(leaving, grid, everyone_pairs[step])
    column = jnp.where(listed, -column, 0.0)
    column = column.reshape(rows_here, half // BC, 2, BC).transpose(0, 2, 1, 3)
    column_out = column.reshape(rows_here, 1, 1, 2, half)
    return (column_out, diag_inverse, density_diag, tile_sum)


def solution(mesh):
    in_specs = (
        P("pole", None, "row", "col"),
        P("pole", None, ("row", "col"), None),
        P(("row", "col"), "pole", None, None, None),
        P(),
        P(("row", "col"), None),
        P(),
        P("pole"),
    )
    out_specs = (
        P(("row", "col"), "pole", None, None, None),
        P(("row", "col"), "pole", None, None, None),
        P(("row", "col"), None, None),
        P(("pole", "row", "col"), None, None),
    )
    return jax.shard_map(compute, mesh=mesh, in_specs=in_specs, out_specs=out_specs, check_vma=False)
```

```python
import functools

import jax
import jax.numpy as jnp
from jax import lax
from jax.experimental import pallas as pl
from jax.experimental.pallas import tpu as pltpu
from jax.sharding import PartitionSpec as P


BS = 128
BR = 8
BC = 128
MIB = 1 << 20


def shift_pairs(rows, cols, step, valid):
    return [
        (r * cols + c, r * cols + (c + step) % cols)
        for r in range(rows)
        if valid(r)
        for c in range(cols)
    ]


def gather_stages(shard, rows, cols):
    grid = ("row", "col")
    if rows != 4:
        full = lax.all_gather(shard, grid, axis=0, tiled=True).reshape((rows, cols) + shard.shape)
        c = lax.axis_index("col")
        stages = []
        for row in range(rows):
            line = [lax.dynamic_index_in_dim(full[row], (c - step) % cols, 0, False) for step in range(cols)]
            stages.append([[piece] for piece in line])
        return stages, [[row] * rows for row in range(rows)]
    sources = [[0, 1, 2, 3], [1, 0, 3, 2], [2, 2, 1, 1], [3, 3, 0, 0]]
    outer = [(0, 1), (1, 0), (2, 3), (3, 2)]
    inner = [(1, 2), (2, 1)]
    r = lax.axis_index("row")
    middle = jnp.logical_or(r == 1, r == 2)
    height = shard.shape[0] // 2
    stages = [[[] for _ in range(cols)] for _ in range(rows)]
    for part in (0, 1):
        own = shard[part * height : (part + 1) * height]
        near = lax.ppermute(own, "row", outer)
        cross = lax.ppermute(own, "row", inner)
        cross_out = lax.ppermute(cross, "row", outer)
        far = lax.ppermute(near, "row", inner)
        far_out = lax.ppermute(far, "row", outer)
        line = [
            lambda: own,
            lambda: near,
            lambda: jnp.where(middle, cross, cross_out),
            lambda: jnp.where(middle, far, far_out),
        ]
        last = None
        opened = []
        for stage, make in enumerate(line):
            piece = make()
            stages[stage][0].append(piece)
            leaving = piece
            if last is not None:
                leaving, _ = lax.optimization_barrier((piece, last))
            for step in range(1, cols):
                if stage == 1 and part == 1:
                    relayed, _ = lax.optimization_barrier((opened[step - 1], far_out))
                    stages[stage][step].append(lax.ppermute(relayed, "row", outer))
                    continue
                pairs = shift_pairs(rows, cols, step, lambda r: True)
                last = lax.ppermute(leaving, grid, pairs)
                stages[stage][step].append(last)
                if stage == 0:
                    opened.append(last)
    return stages, sources


def counts_of(ancestors, inverse, rows, cols):
    row_blocks, col_blocks = inverse.shape[1] // BS, inverse.shape[2] // BS
    r = lax.axis_index("row")
    c = lax.axis_index("col")

    def below(limit):
        total = jnp.int32(0)
        for i in range(ancestors.shape[0]):
            total = total + (ancestors[i] < limit).astype(jnp.int32)
        return total

    row_first, row_last = below(r * row_blocks), below((r + 1) * row_blocks)
    col_first, col_last = below(c * col_blocks), below((c + 1) * col_blocks)
    count = row_last - row_first
    return rows, cols, row_blocks, col_blocks, row_first, count, col_first, col_last


def source_row(sources, stage):
    r = lax.axis_index("row")
    total = jnp.int32(0)
    for row, source in enumerate(sources[stage]):
        total = total + jnp.where(r == row, source, 0)
    return total


def fill(full, pieces, sources, stage, cols):
    c = lax.axis_index("col")
    source = source_row(sources, stage)
    chunks = len(pieces) // cols
    height = pieces[0].shape[0]
    for step in range(cols):
        shard = source * cols + lax.rem(c - step + cols, cols)
        for chunk in range(chunks):
            start = pl.multiple_of((shard * chunks + chunk) * height, height)
            full[pl.ds(start, height), :] = pieces[step * chunks + chunk][...]


def multiply(acc, inverse, full, ancestors, counts, i, source):
    rows, _, row_blocks, col_blocks = counts[:4]
    row_first, _, col_first, col_last = counts[4:]
    stage_blocks = ancestors.shape[0] // rows
    low = source * stage_blocks
    r = lax.axis_index("row")
    c = lax.axis_index("col")

    @pl.when(jnp.logical_and(low < col_last, low + stage_blocks > col_first))
    def _():
        row = pl.multiple_of((ancestors[row_first + i] - r * row_blocks) * BS, BS)
        left = []
        for n in range(stage_blocks):
            k = low + n
            inside = jnp.logical_and(k >= col_first, k < col_last)
            block = jnp.where(inside, ancestors[k] - c * col_blocks, 0)
            value = inverse[:, pl.ds(row, BS), pl.ds(pl.multiple_of(block * BS, BS), BS)]
            left.append(value.reshape(2 * BS, BS) * inside.astype(value.dtype))
        place = pl.ds(pl.multiple_of(low * BS, BS), stage_blocks * BS)
        acc[...] += jnp.dot(
            jnp.concatenate(left, axis=1), full[place, :], preferred_element_type=jnp.float32
        )


def combine(acc):
    half = acc.shape[1] // 2
    return acc[:BS, :half] - acc[BS:, half:], acc[:BS, half:] + acc[BS:, :half]


def early_kernel(sources, stages, rows, cols, ancestors, inverse, *refs):
    early, full, acc = refs[-3:]
    pieces = refs[:-3]
    each = len(pieces) // len(stages)
    half = acc.shape[1] // 2
    for n, stage in enumerate(stages):
        fill(full, pieces[n * each : (n + 1) * each], sources, stage, cols)
    counts = counts_of(ancestors, inverse, rows, cols)

    @pl.loop(0, counts[5])
    def _(i):
        acc[...] = jnp.zeros_like(acc)
        for stage in stages:
            multiply(acc, inverse, full, ancestors, counts, i, source_row(sources, stage))
        real, imag = combine(acc)
        early[i, :, :half] = real
        early[i, :, half:] = imag


def last_kernel(
    sources, stages, rows, cols, ancestors, table, slot, owner, inverse, early, *refs
):
    keep, send, diag_keep, diag_send, full, acc, diag, tiles, leaving = refs[-9:]
    pieces = refs[:-9]
    each = len(pieces) // rows
    wide = acc.shape[1]
    half = wide // 2
    row_blocks = early.shape[0]
    own_blocks = row_blocks // cols
    r = lax.axis_index("row")
    c = lax.axis_index("col")
    for stage in range(rows):
        fill(full, pieces[stage * each : (stage + 1) * each], sources, stage, cols)
    counts = counts_of(ancestors, inverse, rows, cols)
    row_first, row_count = counts[4:6]
    keep[...] = jnp.zeros_like(keep)
    leaving[...] = jnp.zeros_like(leaving)
    diag[...] = jnp.zeros_like(diag)
    tiles[...] = jnp.zeros_like(tiles)
    weight_real = table[0, slot[0]]
    weight_imag = table[1, slot[0]]

    @pl.loop(0, row_count)
    def _(i):
        acc[:BS, :] = early[i]
        acc[BS:, :] = jnp.zeros((BS, wide), jnp.float32)
        for stage in stages:
            multiply(acc, inverse, full, ancestors, counts, i, source_row(sources, stage))
        real, imag = combine(acc)
        block = ancestors[row_first + i] - r * row_blocks
        place = block // own_blocks
        across = half // BC
        within = lax.rem(block, own_blocks) * (BS * 2 * across)
        turn = lax.rem(place - c + cols, cols)

        def lay(target, start):
            for j in range(across):
                for n, value in enumerate((real, imag)):
                    rows_of = pl.ds(start + 2 * j + n, BS, stride=2 * across)
                    target[rows_of, :] = -value[:, j * BC : (j + 1) * BC]

        @pl.when(turn == 0)
        def _():
            lay(keep, within)

        @pl.when(turn > 0)
        def _():
            lay(leaving, (turn - 1) * keep.shape[0] + within)

        mixed = -(weight_real * imag + weight_imag * real)
        per_device = own_blocks * (BS // BR) * across
        first = lax.rem(c - place + cols, cols) * per_device + lax.rem(block, own_blocks) * (
            BS // BR
        ) * across
        for group in range(BS // BR):
            for j in range(across):
                tile = owner[first + group * across + j]
                tiles[j, tile] += mixed[group * BR : (group + 1) * BR, j * BC : (j + 1) * BC]

        rows_of = full[pl.ds(pl.multiple_of((row_first + i) * BS, BS), BS), :]
        real_high = real.astype(jnp.bfloat16)
        imag_high = imag.astype(jnp.bfloat16)
        real_low = (real - real_high.astype(jnp.float32)).astype(jnp.bfloat16)
        imag_low = (imag - imag_high.astype(jnp.float32)).astype(jnp.bfloat16)
        left = jnp.concatenate([rows_of[:, :half], rows_of[:, half:]], axis=0)
        left = jnp.concatenate([left, left], axis=0)
        right = jnp.concatenate(
            [
                jnp.concatenate([real_high, imag_high], axis=1),
                jnp.concatenate([-imag_high, real_high], axis=1),
                jnp.concatenate([real_low, imag_low], axis=1),
                jnp.concatenate([-imag_low, real_low], axis=1),
            ],
            axis=0,
        )
        diag[...] += lax.dot_general(
            left, right, (((0,), (0,)), ((), ())), preferred_element_type=jnp.float32
        )

    send[...] = leaving[...].astype(send.dtype)
    part = half // (rows * cols)
    poles = tiles.shape[1] // (rows * cols)
    for row in range(rows):
        for step in range(cols):
            place = row * cols + lax.rem(c + step, cols)
            value = diag[pl.ds(pl.multiple_of(place * part, part), part), :]
            if step == 0:
                diag_keep[row, :part] = value
                diag_keep[row, part:] = jnp.zeros((BR, wide), jnp.float32)
            else:
                diag_send[step - 1, row, :part] = value.astype(diag_send.dtype)
                diag_send[step - 1, row, part:] = jnp.zeros((BR, wide), diag_send.dtype)
            for pole in range(poles):
                total = tiles[0, pole * rows * cols + place]
                for j in range(1, half // BC):
                    total = total + tiles[j, pole * rows * cols + place]
                if step == 0:
                    diag_keep[row, part:, 2 * pole * BC : (2 * pole + 1) * BC] = total
                else:
                    diag_send[step - 1, row, part:, 2 * pole * BC : 2 * (pole + 1) * BC] = halves(total)


def halves(value):
    high = value.astype(jnp.bfloat16)
    low = (value - high.astype(jnp.float32)).astype(jnp.bfloat16)
    return jnp.concatenate([high, low], axis=1)


def regroup_kernel(poles, rows, kept, *refs):
    *rounded, own = refs[-rows:]
    arrived = refs[:-rows]
    part = own.shape[0] - BR
    r = lax.axis_index("row")

    def total(row):
        value = kept[row]
        for ref in arrived:
            value = value + ref[row].astype(jnp.float32)
        return value

    own[...] = total(r)
    for step in range(1, rows):
        value = total(lax.rem(r + step, rows))
        out = rounded[step - 1]
        out[:part] = value[:part].astype(out.dtype)
        for pole in range(poles):
            first = 2 * pole * BC
            band = value[part:, first : first + BC] + value[part:, first + BC : first + 2 * BC]
            out[part:, first : first + 2 * BC] = halves(band)


def finish_kernel(poles, table, slot, laid_dinv, own, *refs):
    diag_out, message = refs[-2:]
    arrived = refs[:-2]
    part, wide = own.shape[0] - BR, own.shape[1]
    across = wide // (2 * BC)
    total = own[...]
    for ref in arrived:
        total = total + ref[...].astype(jnp.float32)
    weight_real = table[0, slot[0]]
    weight_imag = table[1, slot[0]]
    for j in range(across):
        values = []
        for n in range(2):
            rows_of = pl.ds(2 * j + n, part, stride=2 * across)
            first = (n * across + j) * BC
            values.append(laid_dinv[rows_of, :] + total[:part, first : first + BC])
            diag_out[rows_of, :] = values[n]
        share = weight_real * values[1] + weight_imag * values[0]
        message[pl.ds(j, part, stride=across), :] = share
    for pole in range(poles):
        first = 2 * pole * BC
        band = total[part:, first : first + BC] + total[part:, first + BC : first + 2 * BC]
        start = part * across + pole * BR
        message[start : start + BR] = band


def compute(inverse, factor, dinv, ancestors, owner, weight_table, pole_slot):
    rows = lax.axis_size("row")
    cols = lax.axis_size("col")
    poles = lax.axis_size("pole")
    grid = ("row", "col")
    tile_count = poles * rows * cols
    here = inverse[0]
    wide = factor.shape[3]
    half = wide // 2
    rows_here = here.shape[1] // cols
    row_blocks = here.shape[1] // BS
    selected = ancestors.shape[1]
    part = half // (rows * cols)
    everyone = lambda r: True

    owners = [owner[:, 0]]
    for step in range(1, cols):
        pairs = shift_pairs(rows, cols, step, everyone)
        owners.append(lax.ppermute(owner[:, 0], grid, pairs))
    smem = pl.BlockSpec(memory_space=pltpu.SMEM)
    vmem = pl.BlockSpec(memory_space=pltpu.VMEM)
    whole = pl.BlockSpec(memory_space=pl.ANY)
    across = half // BC

    def laid(value):
        value = value.reshape(-1, 2, across, BC).transpose(0, 2, 1, 3)
        return value.reshape(-1, BC)

    def plain(value, shape):
        value = value.reshape(-1, across, 2, BC).transpose(0, 2, 1, 3)
        return value.reshape(shape)

    stages, sources = gather_stages(factor[0, 0], rows, cols)
    stages = [[chunk for step in stage for chunk in step] for stage in stages]
    late_owners, _ = lax.optimization_barrier((tuple(owners), stages[2][-1]))
    products = 2 * row_blocks * BS * 2 * wide * selected * BS // cols
    first = (0, rows - 2)
    last = tuple(stage for stage in range(rows) if stage not in first)
    early_pieces = [piece for stage in first for piece in stages[stage]]
    early = pl.pallas_call(
        functools.partial(early_kernel, sources, first, rows, cols),
        out_shape=jax.ShapeDtypeStruct((row_blocks, BS, wide), jnp.float32),
        in_specs=[smem, vmem] + [vmem] * len(early_pieces),
        out_specs=vmem,
        scratch_shapes=[
            pltpu.VMEM((selected * BS, wide), jnp.bfloat16),
            pltpu.VMEM((2 * BS, wide), jnp.float32),
        ],
        compiler_params=pltpu.CompilerParams(vmem_limit_bytes=24 * MIB),
        cost_estimate=pl.CostEstimate(
            flops=products * len(first) // rows, bytes_accessed=4 * MIB, transcendentals=0
        ),
        name="early_products",
    )(ancestors[0], here, *early_pieces)
    all_pieces = [piece for stage in stages for piece in stage]
    others = max(1, cols - 1)
    laid_rows = rows_here * wide // BC
    keep, send, diag_keep, diag_send = pl.pallas_call(
        functools.partial(last_kernel, sources, last, rows, cols),
        out_shape=(
            jax.ShapeDtypeStruct((laid_rows, BC), jnp.float32),
            jax.ShapeDtypeStruct((others * laid_rows, BC), jnp.bfloat16),
            jax.ShapeDtypeStruct((rows, part + BR, wide), jnp.float32),
            jax.ShapeDtypeStruct((others, rows, part + BR, wide), jnp.bfloat16),
        ),
        in_specs=[smem] * 4 + [vmem] * (2 + len(all_pieces)),
        out_specs=(vmem,) * 4,
        scratch_shapes=[
            pltpu.VMEM((selected * BS, wide), jnp.bfloat16),
            pltpu.VMEM((2 * BS, wide), jnp.float32),
            pltpu.VMEM((half, wide), jnp.float32),
            pltpu.VMEM((half // BC, tile_count, BR, BC), jnp.float32),
            pltpu.VMEM((others * laid_rows, BC), jnp.float32),
        ],
        compiler_params=pltpu.CompilerParams(vmem_limit_bytes=28 * MIB),
        cost_estimate=pl.CostEstimate(flops=products, bytes_accessed=8 * MIB, transcendentals=0),
        name="last_products",
    )(ancestors[0], weight_table, pole_slot, jnp.concatenate(late_owners), here, early, *all_pieces)

    everyone_pairs = [shift_pairs(rows, cols, step, everyone) for step in range(cols)]
    arrived = [
        lax.ppermute(diag_send[step - 1], grid, everyone_pairs[step]) for step in range(1, cols)
    ]
    *rounded, own = pl.pallas_call(
        functools.partial(regroup_kernel, poles, rows),
        out_shape=(jax.ShapeDtypeStruct((part + BR, wide), jnp.bfloat16),) * (rows - 1)
        + (jax.ShapeDtypeStruct((part + BR, wide), jnp.float32),),
        in_specs=[vmem] * (1 + len(arrived)),
        out_specs=(vmem,) * rows,
        compiler_params=pltpu.CompilerParams(vmem_limit_bytes=16 * MIB),
        name="regroup",
    )(diag_keep, *arrived)
    parts = [
        lax.ppermute(rounded[step - 1], "row", [(i, (i + step) % rows) for i in range(rows)])
        for step in range(1, rows)
    ]
    laid_diag, message = pl.pallas_call(
        functools.partial(finish_kernel, poles),
        out_shape=(
            jax.ShapeDtypeStruct((part * 2 * across, BC), jnp.float32),
            jax.ShapeDtypeStruct((part * across + poles * BR, BC), jnp.float32),
        ),
        in_specs=[smem] * 2 + [vmem] * (2 + len(parts)),
        out_specs=(vmem,) * 2,
        compiler_params=pltpu.CompilerParams(vmem_limit_bytes=8 * MIB),
        name="finish",
    )(weight_table, pole_slot, laid(dinv), own, *parts)
    diag_inverse = plain(laid_diag, dinv.shape)
    messages = [message]
    for step in range(1, poles):
        messages.append(lax.ppermute(message, "pole", [(i, i ^ step) for i in range(poles)]))

    def summed(values):
        while len(values) > 1:
            values = [a + b for a, b in zip(values[::2], values[1::2])]
        return values[0]

    split = part * across
    density_diag = summed([value[:split] for value in messages]).reshape(part, 1, half)
    start = split + lax.axis_index("pole") * BR
    tile_sum = summed([lax.dynamic_slice_in_dim(value, start, BR) for value in messages])[None]

    column = keep
    for step in range(1, cols):
        leaving = send[(step - 1) * laid_rows : step * laid_rows]
        column = column + lax.ppermute(leaving, grid, everyone_pairs[step])
    column_out = plain(column, (rows_here, 1, 1, 2, half))
    return (column_out, diag_inverse, density_diag, tile_sum)


def solution(mesh):
    in_specs = (
        P("pole", None, "row", "col"),
        P("pole", None, ("row", "col"), None),
        P(("row", "col"), "pole", None, None, None),
        P(),
        P(("row", "col"), None),
        P(),
        P("pole"),
    )
    out_specs = (
        P(("row", "col"), "pole", None, None, None),
        P(("row", "col"), "pole", None, None, None),
        P(("row", "col"), None, None),
        P(("pole", "row", "col"), None, None),
    )
    return jax.shard_map(compute, mesh=mesh, in_specs=in_specs, out_specs=out_specs, check_vma=False)
```

```python
import functools

import jax
import jax.numpy as jnp
from jax import lax
from jax.experimental import pallas as pl
from jax.experimental.pallas import tpu as pltpu
from jax.sharding import PartitionSpec as P


BS = 128
BR = 8
BC = 128
MIB = 1 << 20
SPLIT = (1, 3)


def shift_pairs(rows, cols, step, valid):
    return [
        (r * cols + c, r * cols + (c + step) % cols)
        for r in range(rows)
        if valid(r)
        for c in range(cols)
    ]


def gather_stages(shard, rows, cols):
    grid = ("row", "col")
    if rows != 4:
        full = lax.all_gather(shard, grid, axis=0, tiled=True).reshape((rows, cols) + shard.shape)
        c = lax.axis_index("col")
        stages = []
        for row in range(rows):
            line = [lax.dynamic_index_in_dim(full[row], (c - step) % cols, 0, False) for step in range(cols)]
            stages.append([[piece] for piece in line])
        return stages, [[row] * rows for row in range(rows)]
    sources = [[0, 1, 2, 3], [1, 0, 3, 2], [2, 2, 1, 1], [3, 3, 0, 0]]
    outer = [(0, 1), (1, 0), (2, 3), (3, 2)]
    inner = [(1, 2), (2, 1)]
    r = lax.axis_index("row")
    middle = jnp.logical_or(r == 1, r == 2)
    height = shard.shape[0] // 2
    stages = [[[] for _ in range(cols)] for _ in range(rows)]
    for part in (0, 1):
        own = shard[part * height : (part + 1) * height]
        near = lax.ppermute(own, "row", outer)
        cross = lax.ppermute(own, "row", inner)
        cross_out = lax.ppermute(cross, "row", outer)
        far = lax.ppermute(near, "row", inner)
        far_out = lax.ppermute(far, "row", outer)
        line = [
            lambda: own,
            lambda: near,
            lambda: jnp.where(middle, cross, cross_out),
            lambda: jnp.where(middle, far, far_out),
        ]
        last = None
        opened = []
        for stage, make in enumerate(line):
            piece = make()
            stages[stage][0].append(piece)
            leaving = piece
            if last is not None:
                leaving, _ = lax.optimization_barrier((piece, last))
            for step in range(1, cols):
                if stage == 1 and part == 1:
                    relayed, _ = lax.optimization_barrier((opened[step - 1], far_out))
                    stages[stage][step].append(lax.ppermute(relayed, "row", outer))
                    continue
                pairs = shift_pairs(rows, cols, step, lambda r: True)
                last = lax.ppermute(leaving, grid, pairs)
                stages[stage][step].append(last)
                if stage == 0:
                    opened.append(last)
    return stages, sources


def counts_of(ancestors, inverse, rows, cols):
    row_blocks, col_blocks = inverse.shape[1] // BS, inverse.shape[2] // BS
    r = lax.axis_index("row")
    c = lax.axis_index("col")

    def below(limit):
        total = jnp.int32(0)
        for i in range(ancestors.shape[0]):
            total = total + (ancestors[i] < limit).astype(jnp.int32)
        return total

    row_first, row_last = below(r * row_blocks), below((r + 1) * row_blocks)
    col_first, col_last = below(c * col_blocks), below((c + 1) * col_blocks)
    count = row_last - row_first
    return rows, cols, row_blocks, col_blocks, row_first, count, col_first, col_last


def source_row(sources, stage):
    r = lax.axis_index("row")
    total = jnp.int32(0)
    for row, source in enumerate(sources[stage]):
        total = total + jnp.where(r == row, source, 0)
    return total


def fill(full, pieces, sources, stage, cols):
    c = lax.axis_index("col")
    source = source_row(sources, stage)
    chunks = len(pieces) // cols
    height = pieces[0].shape[0]
    for step in range(cols):
        shard = source * cols + lax.rem(c - step + cols, cols)
        for chunk in range(chunks):
            start = pl.multiple_of((shard * chunks + chunk) * height, height)
            full[pl.ds(start, height), :] = pieces[step * chunks + chunk][...]


def multiply(acc, inverse, full, ancestors, counts, pair, source):
    rows, _, row_blocks, col_blocks = counts[:4]
    row_first, row_count, col_first, col_last = counts[4:]
    stage_blocks = ancestors.shape[0] // rows
    low = source * stage_blocks
    r = lax.axis_index("row")
    c = lax.axis_index("col")

    @pl.when(jnp.logical_and(low < col_last, low + stage_blocks > col_first))
    def _():
        left = []
        for n in range(stage_blocks):
            k = low + n
            inside = jnp.logical_and(k >= col_first, k < col_last)
            block = jnp.where(inside, ancestors[k] - c * col_blocks, 0)
            column = pl.ds(pl.multiple_of(block * BS, BS), BS)
            both = []
            for i in range(2):
                listed = ancestors[row_first + jnp.minimum(2 * pair + i, row_count - 1)]
                row = pl.multiple_of((listed - r * row_blocks) * BS, BS)
                both.append(inverse[:, pl.ds(row, BS), column].reshape(2 * BS, BS))
            value = jnp.concatenate(both, axis=0)
            left.append(value * inside.astype(value.dtype))
        place = pl.ds(pl.multiple_of(low * BS, BS), stage_blocks * BS)
        acc[...] += jnp.dot(
            jnp.concatenate(left, axis=1), full[place, :], preferred_element_type=jnp.float32
        )


def combine(acc, n):
    half = acc.shape[1] // 2
    upper, lower = acc.at[2 * n * BS : (2 * n + 1) * BS], acc.at[(2 * n + 1) * BS : (2 * n + 2) * BS]
    return upper[:, :half] - lower[:, half:], upper[:, half:] + lower[:, :half]


def add_products(sources, stages, ancestors, inverse, before, full, acc, counts, store):
    row_count = counts[5]

    @pl.loop(0, (row_count + 1) // 2)
    def _(pair):
        if before is None:
            acc[...] = jnp.zeros_like(acc)
        else:
            for n in range(2):
                i = jnp.minimum(2 * pair + n, row_count - 1)
                acc[2 * n * BS : (2 * n + 1) * BS, :] = before[i]
                acc[(2 * n + 1) * BS : (2 * n + 2) * BS, :] = jnp.zeros((BS, acc.shape[1]), acc.dtype)
        for stage in stages:
            multiply(acc, inverse, full, ancestors, counts, pair, source_row(sources, stage))
        for n in range(2):

            @pl.when(2 * pair + n < row_count)
            def _():
                store(2 * pair + n, *combine(acc, n))


def early_kernel(sources, stages, added, rows, cols, ancestors, inverse, *refs):
    early, full, acc = refs[-3:]
    before = refs[0] if added else None
    pieces = refs[1 if added else 0 : -3]
    each = len(pieces) // len(stages)
    half = acc.shape[1] // 2
    for n, stage in enumerate(stages):
        fill(full, pieces[n * each : (n + 1) * each], sources, stage, cols)
    counts = counts_of(ancestors, inverse, rows, cols)

    def store(i, real, imag):
        early[i, :, :half] = real
        early[i, :, half:] = imag

    add_products(sources, stages, ancestors, inverse, before, full, acc, counts, store)


def last_kernel(sources, stages, rows, cols, ancestors, inverse, early, *refs):
    keep, *sends, total, turned, full, acc, leaving = refs[-(6 + len(SPLIT)) :]
    pieces = refs[: -(6 + len(SPLIT))]
    each = len(pieces) // rows
    half = acc.shape[1] // 2
    across = half // BC
    row_blocks = early.shape[0]
    own_blocks = row_blocks // cols
    r = lax.axis_index("row")
    c = lax.axis_index("col")
    for stage in range(rows):
        fill(full, pieces[stage * each : (stage + 1) * each], sources, stage, cols)
    counts = counts_of(ancestors, inverse, rows, cols)
    row_first = counts[4]
    keep[...] = jnp.zeros_like(keep)
    leaving[...] = jnp.zeros_like(leaving)

    def store(i, real, imag):
        total[i, :, :half] = real
        total[i, :, half:] = imag
        block = ancestors[row_first + i] - r * row_blocks
        within = lax.rem(block, own_blocks) * (BS * 2 * across)
        turn = lax.rem(block // own_blocks - c + cols, cols)

        def lay(target, start):
            for j in range(across):
                for n, value in enumerate((real, imag)):
                    rows_of = pl.ds(start + 2 * j + n, BS, stride=2 * across)
                    target[rows_of, :] = -value[:, j * BC : (j + 1) * BC]

        @pl.when(turn == 0)
        def _():
            lay(keep, within)

        @pl.when(turn > 0)
        def _():
            lay(leaving, (turn - 1) * keep.shape[0] + within)

        rows_of = full[pl.ds(pl.multiple_of((row_first + i) * BS, BS), BS), :]
        left = jnp.concatenate([rows_of[:, :half], rows_of[:, half:]], axis=0)
        turned[i] = left.T

    add_products(sources, stages, ancestors, inverse, early, full, acc, counts, store)
    height = keep.shape[0]
    for step in range(cols - 1):
        first = 0
        for send, share in zip(sends, SPLIT):
            size = height * share // sum(SPLIT)
            value = leaving[step * height + first : step * height + first + size, :]
            send[step * size : (step + 1) * size, :] = value.astype(send.dtype)
            first += size


def diag_kernel(poles, rows, cols, row_blocks, ancestors, table, slot, owner, total, turned, *refs):
    diag_keep, diag_send, diag, tiles = refs
    half, wide = diag.shape
    across = half // BC
    own_blocks = row_blocks // cols
    r = lax.axis_index("row")
    c = lax.axis_index("col")

    def below(limit):
        count = jnp.int32(0)
        for i in range(ancestors.shape[0]):
            count = count + (ancestors[i] < limit).astype(jnp.int32)
        return count

    row_first = below(r * row_blocks)
    diag[...] = jnp.zeros_like(diag)
    tiles[...] = jnp.zeros_like(tiles)
    weight_real = table[0, slot[0]]
    weight_imag = table[1, slot[0]]

    @pl.loop(0, below((r + 1) * row_blocks) - row_first)
    def _(i):
        real = total[i, :, :half]
        imag = total[i, :, half:]
        left = turned[i]
        real_high = real.astype(jnp.bfloat16)
        imag_high = imag.astype(jnp.bfloat16)
        real_low = (real - real_high.astype(jnp.float32)).astype(jnp.bfloat16)
        imag_low = (imag - imag_high.astype(jnp.float32)).astype(jnp.bfloat16)
        right = jnp.concatenate(
            [
                jnp.concatenate([real_high, imag_high], axis=1),
                jnp.concatenate([-imag_high, real_high], axis=1),
                jnp.concatenate([real_low, imag_low], axis=1),
                jnp.concatenate([-imag_low, real_low], axis=1),
            ],
            axis=0,
        )
        diag[...] += jnp.dot(
            jnp.concatenate([left, left], axis=1), right, preferred_element_type=jnp.float32
        )
        block = ancestors[row_first + i] - r * row_blocks
        place = block // own_blocks
        mixed = -(weight_real * imag + weight_imag * real)
        per_device = own_blocks * (BS // BR) * across
        first = lax.rem(c - place + cols, cols) * per_device + lax.rem(block, own_blocks) * (
            BS // BR
        ) * across
        for group in range(BS // BR):
            for j in range(across):
                tile = owner[first + group * across + j]
                tiles[j, tile] += mixed[group * BR : (group + 1) * BR, j * BC : (j + 1) * BC]

    part = half // (rows * cols)
    for row in range(rows):
        for step in range(cols):
            place = row * cols + lax.rem(c + step, cols)
            value = diag[pl.ds(pl.multiple_of(place * part, part), part), :]
            if step == 0:
                diag_keep[row, :part] = value
                diag_keep[row, part:] = jnp.zeros((BR, wide), jnp.float32)
            else:
                diag_send[step - 1, row, :part] = value.astype(diag_send.dtype)
                diag_send[step - 1, row, part:] = jnp.zeros((BR, wide), diag_send.dtype)
            for pole in range(poles):
                sum_of = tiles[0, pole * rows * cols + place]
                for j in range(1, across):
                    sum_of = sum_of + tiles[j, pole * rows * cols + place]
                if step == 0:
                    diag_keep[row, part:, 2 * pole * BC : (2 * pole + 1) * BC] = sum_of
                else:
                    diag_send[step - 1, row, part:, 2 * pole * BC : 2 * (pole + 1) * BC] = halves(sum_of)


def join_kernel(steps, keep, *refs):
    out = refs[-1]
    block = pl.program_id(0)
    first = 0
    for n, share in enumerate(SPLIT):
        arrived = refs[n * steps : (n + 1) * steps]

        @pl.when(jnp.logical_and(block >= first, block < first + share))
        def _():
            value = keep[...]
            for ref in arrived:
                value = value + ref[...].astype(jnp.float32)
            out[...] = value

        first += share


def halves(value):
    high = value.astype(jnp.bfloat16)
    low = (value - high.astype(jnp.float32)).astype(jnp.bfloat16)
    return jnp.concatenate([high, low], axis=1)


def regroup_kernel(poles, rows, kept, *refs):
    *rounded, own = refs[-rows:]
    arrived = refs[:-rows]
    part = own.shape[0] - BR
    r = lax.axis_index("row")

    def total(row):
        value = kept[row]
        for ref in arrived:
            value = value + ref[row].astype(jnp.float32)
        return value

    own[...] = total(r)
    for step in range(1, rows):
        value = total(lax.rem(r + step, rows))
        out = rounded[step - 1]
        out[:part] = value[:part].astype(out.dtype)
        for pole in range(poles):
            first = 2 * pole * BC
            band = value[part:, first : first + BC] + value[part:, first + BC : first + 2 * BC]
            out[part:, first : first + 2 * BC] = halves(band)


def finish_kernel(poles, table, slot, laid_dinv, own, *refs):
    diag_out, message = refs[-2:]
    arrived = refs[:-2]
    part, wide = own.shape[0] - BR, own.shape[1]
    across = wide // (2 * BC)
    total = own[...]
    for ref in arrived:
        total = total + ref[...].astype(jnp.float32)
    weight_real = table[0, slot[0]]
    weight_imag = table[1, slot[0]]
    for j in range(across):
        values = []
        for n in range(2):
            rows_of = pl.ds(2 * j + n, part, stride=2 * across)
            first = (n * across + j) * BC
            values.append(laid_dinv[rows_of, :] + total[:part, first : first + BC])
            diag_out[rows_of, :] = values[n]
        share = weight_real * values[1] + weight_imag * values[0]
        message[pl.ds(j, part, stride=across), :] = share
    for pole in range(poles):
        first = 2 * pole * BC
        band = total[part:, first : first + BC] + total[part:, first + BC : first + 2 * BC]
        start = part * across + pole * BR
        message[start : start + BR] = band


def compute(inverse, factor, dinv, ancestors, owner, weight_table, pole_slot):
    rows = lax.axis_size("row")
    cols = lax.axis_size("col")
    poles = lax.axis_size("pole")
    grid = ("row", "col")
    tile_count = poles * rows * cols
    here = inverse[0]
    wide = factor.shape[3]
    half = wide // 2
    rows_here = here.shape[1] // cols
    row_blocks = here.shape[1] // BS
    selected = ancestors.shape[1]
    part = half // (rows * cols)
    everyone = lambda r: True

    owners = [owner[:, 0]]
    for step in range(1, cols):
        pairs = shift_pairs(rows, cols, step, everyone)
        owners.append(lax.ppermute(owner[:, 0], grid, pairs))
    smem = pl.BlockSpec(memory_space=pltpu.SMEM)
    vmem = pl.BlockSpec(memory_space=pltpu.VMEM)
    whole = pl.BlockSpec(memory_space=pl.ANY)
    across = half // BC

    def laid(value):
        value = value.reshape(-1, 2, across, BC).transpose(0, 2, 1, 3)
        return value.reshape(-1, BC)

    def plain(value, shape):
        value = value.reshape(-1, across, 2, BC).transpose(0, 2, 1, 3)
        return value.reshape(shape)

    stages, sources = gather_stages(factor[0, 0], rows, cols)
    stages = [[chunk for step in stage for chunk in step] for stage in stages]
    late_owners, _ = lax.optimization_barrier((tuple(owners), stages[2][-1]))
    products = 2 * row_blocks * BS * 2 * wide * selected * BS // cols
    scratch = [
        pltpu.VMEM((selected * BS, wide), jnp.bfloat16),
        pltpu.VMEM((4 * BS, wide), jnp.float32),
    ]
    row_products = jax.ShapeDtypeStruct((row_blocks, BS, wide), jnp.float32)
    groups = [(0,)] + ([(rows - 2,)] if rows > 2 else [])
    last = tuple(stage for stage in range(rows) if (stage,) not in groups)
    early = []
    for group in groups:
        group_pieces = [piece for stage in group for piece in stages[stage]]
        early = [
            pl.pallas_call(
                functools.partial(early_kernel, sources, group, bool(early), rows, cols),
                out_shape=row_products,
                in_specs=[smem, vmem] + [vmem] * (len(early) + len(group_pieces)),
                out_specs=vmem,
                scratch_shapes=scratch,
                input_output_aliases={2: 0} if early else {},
                compiler_params=pltpu.CompilerParams(vmem_limit_bytes=24 * MIB),
                cost_estimate=pl.CostEstimate(
                    flops=products * len(group) // rows,
                    bytes_accessed=4 * MIB,
                    transcendentals=0,
                ),
                name="early_products",
            )(ancestors[0], here, *early, *group_pieces)
        ]
    all_pieces = [piece for stage in stages for piece in stage]
    others = max(1, cols - 1)
    laid_rows = rows_here * wide // BC
    sizes = [laid_rows * share // sum(SPLIT) for share in SPLIT]
    keep, *sends, total, turned = pl.pallas_call(
        functools.partial(last_kernel, sources, last, rows, cols),
        out_shape=(jax.ShapeDtypeStruct((laid_rows, BC), jnp.float32),)
        + tuple(jax.ShapeDtypeStruct((others * size, BC), jnp.bfloat16) for size in sizes)
        + (row_products, jax.ShapeDtypeStruct((row_blocks, half, 2 * BS), jnp.bfloat16)),
        in_specs=[smem] + [vmem] * (2 + len(all_pieces)),
        out_specs=(vmem,) * (3 + len(SPLIT)),
        scratch_shapes=scratch + [pltpu.VMEM((others * laid_rows, BC), jnp.float32)],
        compiler_params=pltpu.CompilerParams(vmem_limit_bytes=28 * MIB),
        cost_estimate=pl.CostEstimate(
            flops=products // 2, bytes_accessed=8 * MIB, transcendentals=0
        ),
        name="last_products",
    )(ancestors[0], here, *early, *all_pieces)
    diag_keep, diag_send = pl.pallas_call(
        functools.partial(diag_kernel, poles, rows, cols, row_blocks),
        out_shape=(
            jax.ShapeDtypeStruct((rows, part + BR, wide), jnp.float32),
            jax.ShapeDtypeStruct((others, rows, part + BR, wide), jnp.bfloat16),
        ),
        in_specs=[smem] * 4 + [vmem] * 2,
        out_specs=(vmem,) * 2,
        scratch_shapes=[
            pltpu.VMEM((half, wide), jnp.float32),
            pltpu.VMEM((half // BC, tile_count, BR, BC), jnp.float32),
        ],
        compiler_params=pltpu.CompilerParams(vmem_limit_bytes=20 * MIB),
        cost_estimate=pl.CostEstimate(
            flops=products // 2, bytes_accessed=8 * MIB, transcendentals=0
        ),
        name="diag_products",
    )(ancestors[0], weight_table, pole_slot, jnp.concatenate(late_owners), total, turned)

    everyone_pairs = [shift_pairs(rows, cols, step, everyone) for step in range(cols)]
    arrived = [
        lax.ppermute(diag_send[step - 1], grid, everyone_pairs[step])
        for step in range(1, cols)
    ]
    *rounded, own = pl.pallas_call(
        functools.partial(regroup_kernel, poles, rows),
        out_shape=(jax.ShapeDtypeStruct((part + BR, wide), jnp.bfloat16),) * (rows - 1)
        + (jax.ShapeDtypeStruct((part + BR, wide), jnp.float32),),
        in_specs=[vmem] * (1 + len(arrived)),
        out_specs=(vmem,) * rows,
        compiler_params=pltpu.CompilerParams(vmem_limit_bytes=16 * MIB),
        name="regroup",
    )(diag_keep, *arrived)
    parts = [
        lax.ppermute(rounded[step - 1], "row", [(i, (i + step) % rows) for i in range(rows)])
        for step in range(1, rows)
    ]
    laid_diag, message = pl.pallas_call(
        functools.partial(finish_kernel, poles),
        out_shape=(
            jax.ShapeDtypeStruct((part * 2 * across, BC), jnp.float32),
            jax.ShapeDtypeStruct((part * across + poles * BR, BC), jnp.float32),
        ),
        in_specs=[smem] * 2 + [vmem] * (2 + len(parts)),
        out_specs=(vmem,) * 2,
        compiler_params=pltpu.CompilerParams(vmem_limit_bytes=8 * MIB),
        name="finish",
    )(weight_table, pole_slot, laid(dinv), own, *parts)
    diag_inverse = plain(laid_diag, dinv.shape)
    messages = [message]
    for step in range(1, poles):
        messages.append(lax.ppermute(message, "pole", [(i, i ^ step) for i in range(poles)]))

    def summed(values):
        while len(values) > 1:
            values = [a + b for a, b in zip(values[::2], values[1::2])]
        return values[0]

    split = part * across
    density_diag = summed([value[:split] for value in messages]).reshape(part, 1, half)
    start = split + lax.axis_index("pole") * BR
    tile_sum = summed([lax.dynamic_slice_in_dim(value, start, BR) for value in messages])[None]

    parts = []
    for send, size in zip(sends, sizes):
        parts += [
            lax.ppermute(send[(step - 1) * size : step * size], grid, everyone_pairs[step])
            for step in range(1, cols)
        ]
    block = laid_rows // sum(SPLIT)
    specs = [pl.BlockSpec((block, BC), lambda i: (i, 0))]
    first = 0
    for share in SPLIT:
        spec = pl.BlockSpec(
            (block, BC), lambda i, f=first, n=share: (jnp.clip(i - f, 0, n - 1), 0)
        )
        specs += [spec] * (cols - 1)
        first += share
    column = pl.pallas_call(
        functools.partial(join_kernel, cols - 1),
        grid=(sum(SPLIT),),
        out_shape=jax.ShapeDtypeStruct((laid_rows, BC), jnp.float32),
        in_specs=specs,
        out_specs=pl.BlockSpec((block, BC), lambda i: (i, 0)),
        compiler_params=pltpu.CompilerParams(vmem_limit_bytes=16 * MIB),
        name="join_columns",
    )(keep, *parts)
    column_out = plain(column, (rows_here, 1, 1, 2, half))
    return (column_out, diag_inverse, density_diag, tile_sum)


def solution(mesh):
    in_specs = (
        P("pole", None, "row", "col"),
        P("pole", None, ("row", "col"), None),
        P(("row", "col"), "pole", None, None, None),
        P(),
        P(("row", "col"), None),
        P(),
        P("pole"),
    )
    out_specs = (
        P(("row", "col"), "pole", None, None, None),
        P(("row", "col"), "pole", None, None, None),
        P(("row", "col"), None, None),
        P(("pole", "row", "col"), None, None),
    )
    return jax.shard_map(compute, mesh=mesh, in_specs=in_specs, out_specs=out_specs, check_vma=False)
```

```python
import functools

import jax
import jax.numpy as jnp
from jax import lax
from jax.experimental import pallas as pl
from jax.experimental.pallas import tpu as pltpu
from jax.sharding import PartitionSpec as P


BS = 128
BR = 8
BC = 128
MIB = 1 << 20
SPLIT = (1, 7)


def shift_pairs(rows, cols, step, valid):
    return [
        (r * cols + c, r * cols + (c + step) % cols)
        for r in range(rows)
        if valid(r)
        for c in range(cols)
    ]


def gather_stages(shard, rows, cols):
    grid = ("row", "col")
    if rows != 4:
        full = lax.all_gather(shard, grid, axis=0, tiled=True).reshape((rows, cols) + shard.shape)
        c = lax.axis_index("col")
        stages = []
        for row in range(rows):
            line = [lax.dynamic_index_in_dim(full[row], (c - step) % cols, 0, False) for step in range(cols)]
            stages.append([[piece] for piece in line])
        return stages, [[row] * rows for row in range(rows)]
    sources = [[0, 1, 2, 3], [1, 0, 3, 2], [2, 2, 1, 1], [3, 3, 0, 0]]
    outer = [(0, 1), (1, 0), (2, 3), (3, 2)]
    inner = [(1, 2), (2, 1)]
    r = lax.axis_index("row")
    middle = jnp.logical_or(r == 1, r == 2)
    height = shard.shape[0] // 2
    stages = [[[] for _ in range(cols)] for _ in range(rows)]
    for part in (0, 1):
        own = shard[part * height : (part + 1) * height]
        near = lax.ppermute(own, "row", outer)
        cross = lax.ppermute(own, "row", inner)
        cross_out = lax.ppermute(cross, "row", outer)
        far = lax.ppermute(near, "row", inner)
        far_out = lax.ppermute(far, "row", outer)
        line = [
            lambda: own,
            lambda: near,
            lambda: jnp.where(middle, cross, cross_out),
            lambda: jnp.where(middle, far, far_out),
        ]
        last = None
        opened = []
        for stage, make in enumerate(line):
            piece = make()
            stages[stage][0].append(piece)
            leaving = piece
            if last is not None:
                leaving, _ = lax.optimization_barrier((piece, last))
            for step in range(1, cols):
                if stage == 1 and part == 1:
                    relayed, _ = lax.optimization_barrier((opened[step - 1], far_out))
                    stages[stage][step].append(lax.ppermute(relayed, "row", outer))
                    continue
                pairs = shift_pairs(rows, cols, step, lambda r: True)
                last = lax.ppermute(leaving, grid, pairs)
                stages[stage][step].append(last)
                if stage == 0:
                    opened.append(last)
    return stages, sources


def counts_of(ancestors, inverse, rows, cols):
    row_blocks, col_blocks = inverse.shape[1] // BS, inverse.shape[2] // BS
    r = lax.axis_index("row")
    c = lax.axis_index("col")

    def below(limit):
        total = jnp.int32(0)
        for i in range(ancestors.shape[0]):
            total = total + (ancestors[i] < limit).astype(jnp.int32)
        return total

    row_first, row_last = below(r * row_blocks), below((r + 1) * row_blocks)
    col_first, col_last = below(c * col_blocks), below((c + 1) * col_blocks)
    count = row_last - row_first
    return rows, cols, row_blocks, col_blocks, row_first, count, col_first, col_last


def source_row(sources, stage):
    r = lax.axis_index("row")
    total = jnp.int32(0)
    for row, source in enumerate(sources[stage]):
        total = total + jnp.where(r == row, source, 0)
    return total


def fill(full, pieces, sources, stage, cols):
    c = lax.axis_index("col")
    source = source_row(sources, stage)
    chunks = len(pieces) // cols
    height = pieces[0].shape[0]
    for step in range(cols):
        shard = source * cols + lax.rem(c - step + cols, cols)
        for chunk in range(chunks):
            start = pl.multiple_of((shard * chunks + chunk) * height, height)
            full[pl.ds(start, height), :] = pieces[step * chunks + chunk][...]


def multiply(acc, inverse, full, ancestors, counts, pair, source):
    rows, _, row_blocks, col_blocks = counts[:4]
    row_first, row_count, col_first, col_last = counts[4:]
    stage_blocks = ancestors.shape[0] // rows
    low = source * stage_blocks
    r = lax.axis_index("row")
    c = lax.axis_index("col")

    @pl.when(jnp.logical_and(low < col_last, low + stage_blocks > col_first))
    def _():
        left = []
        for n in range(stage_blocks):
            k = low + n
            inside = jnp.logical_and(k >= col_first, k < col_last)
            block = jnp.where(inside, ancestors[k] - c * col_blocks, 0)
            column = pl.ds(pl.multiple_of(block * BS, BS), BS)
            both = []
            for i in range(2):
                listed = ancestors[row_first + jnp.minimum(2 * pair + i, row_count - 1)]
                row = pl.multiple_of((listed - r * row_blocks) * BS, BS)
                both.append(inverse[:, pl.ds(row, BS), column].reshape(2 * BS, BS))
            value = jnp.concatenate(both, axis=0)
            left.append(value * inside.astype(value.dtype))
        place = pl.ds(pl.multiple_of(low * BS, BS), stage_blocks * BS)
        acc[...] += jnp.dot(
            jnp.concatenate(left, axis=1), full[place, :], preferred_element_type=jnp.float32
        )


def combine(acc, n):
    half = acc.shape[1] // 2
    upper, lower = acc.at[2 * n * BS : (2 * n + 1) * BS], acc.at[(2 * n + 1) * BS : (2 * n + 2) * BS]
    return upper[:, :half] - lower[:, half:], upper[:, half:] + lower[:, :half]


def add_products(sources, stages, ancestors, inverse, before, full, acc, counts, store):
    row_count = counts[5]

    @pl.loop(0, (row_count + 1) // 2)
    def _(pair):
        if before is None:
            acc[...] = jnp.zeros_like(acc)
        else:
            for n in range(2):
                i = jnp.minimum(2 * pair + n, row_count - 1)
                acc[2 * n * BS : (2 * n + 1) * BS, :] = before[i]
                acc[(2 * n + 1) * BS : (2 * n + 2) * BS, :] = jnp.zeros((BS, acc.shape[1]), acc.dtype)
        for stage in stages:
            multiply(acc, inverse, full, ancestors, counts, pair, source_row(sources, stage))
        for n in range(2):

            @pl.when(2 * pair + n < row_count)
            def _():
                store(2 * pair + n, *combine(acc, n))


def early_kernel(sources, stages, added, rows, cols, ancestors, inverse, *refs):
    early, full, acc = refs[-3:]
    before = refs[0] if added else None
    pieces = refs[1 if added else 0 : -3]
    each = len(pieces) // len(stages)
    half = acc.shape[1] // 2
    for n, stage in enumerate(stages):
        fill(full, pieces[n * each : (n + 1) * each], sources, stage, cols)
    counts = counts_of(ancestors, inverse, rows, cols)

    def store(i, real, imag):
        early[i, :, :half] = real
        early[i, :, half:] = imag

    add_products(sources, stages, ancestors, inverse, before, full, acc, counts, store)


def last_kernel(sources, stages, rows, cols, ancestors, inverse, early, *refs):
    keep, *sends, total, turned, full, acc, leaving = refs[-(6 + len(SPLIT)) :]
    pieces = refs[: -(6 + len(SPLIT))]
    each = len(pieces) // rows
    half = acc.shape[1] // 2
    across = half // BC
    row_blocks = early.shape[0]
    own_blocks = row_blocks // cols
    r = lax.axis_index("row")
    c = lax.axis_index("col")
    for stage in range(rows):
        fill(full, pieces[stage * each : (stage + 1) * each], sources, stage, cols)
    counts = counts_of(ancestors, inverse, rows, cols)
    row_first = counts[4]
    keep[...] = jnp.zeros_like(keep)
    leaving[...] = jnp.zeros_like(leaving)

    def store(i, real, imag):
        total[i, :, :half] = real
        total[i, :, half:] = imag
        block = ancestors[row_first + i] - r * row_blocks
        within = lax.rem(block, own_blocks) * (BS * 2 * across)
        turn = lax.rem(block // own_blocks - c + cols, cols)

        def lay(target, start):
            for j in range(across):
                for n, value in enumerate((real, imag)):
                    rows_of = pl.ds(start + 2 * j + n, BS, stride=2 * across)
                    target[rows_of, :] = -value[:, j * BC : (j + 1) * BC]

        @pl.when(turn == 0)
        def _():
            lay(keep, within)

        @pl.when(turn > 0)
        def _():
            lay(leaving, (turn - 1) * keep.shape[0] + within)

        rows_of = full[pl.ds(pl.multiple_of((row_first + i) * BS, BS), BS), :]
        left = jnp.concatenate([rows_of[:, :half], rows_of[:, half:]], axis=0)
        turned[i] = left.T

    add_products(sources, stages, ancestors, inverse, early, full, acc, counts, store)
    height = keep.shape[0]
    for step in range(cols - 1):
        first = 0
        for send, share in zip(sends, SPLIT):
            size = height * share // sum(SPLIT)
            value = leaving[step * height + first : step * height + first + size, :]
            send[step * size : (step + 1) * size, :] = value.astype(send.dtype)
            first += size


def diag_kernel(poles, rows, cols, row_blocks, ancestors, table, slot, owner, total, turned, *refs):
    diag_keep, diag_send, diag, tiles = refs
    half, wide = diag.shape
    across = half // BC
    own_blocks = row_blocks // cols
    r = lax.axis_index("row")
    c = lax.axis_index("col")

    def below(limit):
        count = jnp.int32(0)
        for i in range(ancestors.shape[0]):
            count = count + (ancestors[i] < limit).astype(jnp.int32)
        return count

    row_first = below(r * row_blocks)
    diag[...] = jnp.zeros_like(diag)
    tiles[...] = jnp.zeros_like(tiles)
    weight_real = table[0, slot[0]]
    weight_imag = table[1, slot[0]]

    @pl.loop(0, below((r + 1) * row_blocks) - row_first)
    def _(i):
        real = total[i, :, :half]
        imag = total[i, :, half:]
        left = turned[i]
        real_high = real.astype(jnp.bfloat16)
        imag_high = imag.astype(jnp.bfloat16)
        real_low = (real - real_high.astype(jnp.float32)).astype(jnp.bfloat16)
        imag_low = (imag - imag_high.astype(jnp.float32)).astype(jnp.bfloat16)
        right = jnp.concatenate(
            [
                jnp.concatenate([real_high, imag_high], axis=1),
                jnp.concatenate([-imag_high, real_high], axis=1),
                jnp.concatenate([real_low, imag_low], axis=1),
                jnp.concatenate([-imag_low, real_low], axis=1),
            ],
            axis=0,
        )
        diag[...] += jnp.dot(
            jnp.concatenate([left, left], axis=1), right, preferred_element_type=jnp.float32
        )
        block = ancestors[row_first + i] - r * row_blocks
        place = block // own_blocks
        mixed = -(weight_real * imag + weight_imag * real)
        per_device = own_blocks * (BS // BR) * across
        first = lax.rem(c - place + cols, cols) * per_device + lax.rem(block, own_blocks) * (
            BS // BR
        ) * across
        for group in range(BS // BR):
            for j in range(across):
                tile = owner[first + group * across + j]
                tiles[j, tile] += mixed[group * BR : (group + 1) * BR, j * BC : (j + 1) * BC]

    part = half // (rows * cols)
    for row in range(rows):
        for step in range(cols):
            place = row * cols + lax.rem(c + step, cols)
            value = diag[pl.ds(pl.multiple_of(place * part, part), part), :]
            if step == 0:
                diag_keep[row, :part] = value
                diag_keep[row, part:] = jnp.zeros((BR, wide), jnp.float32)
            else:
                diag_send[step - 1, row, :part] = value.astype(diag_send.dtype)
                diag_send[step - 1, row, part:] = jnp.zeros((BR, wide), diag_send.dtype)
            for pole in range(poles):
                sum_of = tiles[0, pole * rows * cols + place]
                for j in range(1, across):
                    sum_of = sum_of + tiles[j, pole * rows * cols + place]
                if step == 0:
                    diag_keep[row, part:, 2 * pole * BC : (2 * pole + 1) * BC] = sum_of
                else:
                    diag_send[step - 1, row, part:, 2 * pole * BC : 2 * (pole + 1) * BC] = halves(sum_of)


def density_kernel(split, *refs):
    *messages, density, tile = refs
    start = pl.multiple_of(split + lax.axis_index("pole") * BR, BR)
    for place, out in ((pl.ds(0, split), density.at[...]), (pl.ds(start, BR), tile.at[0])):
        values = [message[place, :] for message in messages]
        while len(values) > 1:
            values = [a + b for a, b in zip(values[::2], values[1::2])]
        out[...] = values[0]


def join_kernel(steps, keep, *refs):
    out = refs[-1]
    block = pl.program_id(0)
    first = 0
    for n, share in enumerate(SPLIT):
        arrived = refs[n * steps : (n + 1) * steps]

        @pl.when(jnp.logical_and(block >= first, block < first + share))
        def _():
            value = keep[...]
            for ref in arrived:
                value = value + ref[...].astype(jnp.float32)
            out[...] = value

        first += share


def halves(value):
    high = value.astype(jnp.bfloat16)
    low = (value - high.astype(jnp.float32)).astype(jnp.bfloat16)
    return jnp.concatenate([high, low], axis=1)


def regroup_kernel(poles, rows, kept, *refs):
    *rounded, own = refs[-rows:]
    arrived = refs[:-rows]
    part = own.shape[0] - BR
    r = lax.axis_index("row")

    def total(row):
        value = kept[row]
        for ref in arrived:
            value = value + ref[row].astype(jnp.float32)
        return value

    own[...] = total(r)
    for step in range(1, rows):
        value = total(lax.rem(r + step, rows))
        out = rounded[step - 1]
        out[:part] = value[:part].astype(out.dtype)
        for pole in range(poles):
            first = 2 * pole * BC
            band = value[part:, first : first + BC] + value[part:, first + BC : first + 2 * BC]
            out[part:, first : first + 2 * BC] = halves(band)


def finish_kernel(poles, table, slot, laid_dinv, own, *refs):
    diag_out, message = refs[-2:]
    arrived = refs[:-2]
    part, wide = own.shape[0] - BR, own.shape[1]
    across = wide // (2 * BC)
    total = own[...]
    for ref in arrived:
        total = total + ref[...].astype(jnp.float32)
    weight_real = table[0, slot[0]]
    weight_imag = table[1, slot[0]]
    for j in range(across):
        values = []
        for n in range(2):
            rows_of = pl.ds(2 * j + n, part, stride=2 * across)
            first = (n * across + j) * BC
            values.append(laid_dinv[rows_of, :] + total[:part, first : first + BC])
            diag_out[rows_of, :] = values[n]
        share = weight_real * values[1] + weight_imag * values[0]
        message[pl.ds(j, part, stride=across), :] = share
    for pole in range(poles):
        first = 2 * pole * BC
        band = total[part:, first : first + BC] + total[part:, first + BC : first + 2 * BC]
        start = part * across + pole * BR
        message[start : start + BR] = band


def compute(inverse, factor, dinv, ancestors, owner, weight_table, pole_slot):
    rows = lax.axis_size("row")
    cols = lax.axis_size("col")
    poles = lax.axis_size("pole")
    grid = ("row", "col")
    tile_count = poles * rows * cols
    here = inverse[0]
    wide = factor.shape[3]
    half = wide // 2
    rows_here = here.shape[1] // cols
    row_blocks = here.shape[1] // BS
    selected = ancestors.shape[1]
    part = half // (rows * cols)
    everyone = lambda r: True

    owners = [owner[:, 0]]
    for step in range(1, cols):
        pairs = shift_pairs(rows, cols, step, everyone)
        owners.append(lax.ppermute(owner[:, 0], grid, pairs))
    smem = pl.BlockSpec(memory_space=pltpu.SMEM)
    vmem = pl.BlockSpec(memory_space=pltpu.VMEM)
    whole = pl.BlockSpec(memory_space=pl.ANY)
    across = half // BC

    def laid(value):
        value = value.reshape(-1, 2, across, BC).transpose(0, 2, 1, 3)
        return value.reshape(-1, BC)

    def plain(value, shape):
        value = value.reshape(-1, across, 2, BC).transpose(0, 2, 1, 3)
        return value.reshape(shape)

    stages, sources = gather_stages(factor[0, 0], rows, cols)
    stages = [[chunk for step in stage for chunk in step] for stage in stages]
    late_owners, _ = lax.optimization_barrier((tuple(owners), stages[2][-1]))
    products = 2 * row_blocks * BS * 2 * wide * selected * BS // cols
    scratch = [
        pltpu.VMEM((selected * BS, wide), jnp.bfloat16),
        pltpu.VMEM((4 * BS, wide), jnp.float32),
    ]
    row_products = jax.ShapeDtypeStruct((row_blocks, BS, wide), jnp.float32)
    groups = [(0, rows - 2)] if rows > 2 else [(0,)]
    last = tuple(stage for stage in range(rows) if stage not in groups[0])
    early = []
    for group in groups:
        group_pieces = [piece for stage in group for piece in stages[stage]]
        early = [
            pl.pallas_call(
                functools.partial(early_kernel, sources, group, bool(early), rows, cols),
                out_shape=row_products,
                in_specs=[smem, vmem] + [vmem] * (len(early) + len(group_pieces)),
                out_specs=vmem,
                scratch_shapes=scratch,
                input_output_aliases={2: 0} if early else {},
                compiler_params=pltpu.CompilerParams(vmem_limit_bytes=24 * MIB),
                cost_estimate=pl.CostEstimate(
                    flops=products * len(group) // rows,
                    bytes_accessed=4 * MIB,
                    transcendentals=0,
                ),
                name="early_products",
            )(ancestors[0], here, *early, *group_pieces)
        ]
    all_pieces = [piece for stage in stages for piece in stage]
    others = max(1, cols - 1)
    laid_rows = rows_here * wide // BC
    sizes = [laid_rows * share // sum(SPLIT) for share in SPLIT]
    keep, *sends, total, turned = pl.pallas_call(
        functools.partial(last_kernel, sources, last, rows, cols),
        out_shape=(jax.ShapeDtypeStruct((laid_rows, BC), jnp.float32),)
        + tuple(jax.ShapeDtypeStruct((others * size, BC), jnp.bfloat16) for size in sizes)
        + (row_products, jax.ShapeDtypeStruct((row_blocks, half, 2 * BS), jnp.bfloat16)),
        in_specs=[smem] + [vmem] * (2 + len(all_pieces)),
        out_specs=(vmem,) * (3 + len(SPLIT)),
        scratch_shapes=scratch + [pltpu.VMEM((others * laid_rows, BC), jnp.float32)],
        compiler_params=pltpu.CompilerParams(vmem_limit_bytes=28 * MIB),
        cost_estimate=pl.CostEstimate(
            flops=products // 2, bytes_accessed=8 * MIB, transcendentals=0
        ),
        name="last_products",
    )(ancestors[0], here, *early, *all_pieces)
    diag_keep, diag_send = pl.pallas_call(
        functools.partial(diag_kernel, poles, rows, cols, row_blocks),
        out_shape=(
            jax.ShapeDtypeStruct((rows, part + BR, wide), jnp.float32),
            jax.ShapeDtypeStruct((others, rows, part + BR, wide), jnp.bfloat16),
        ),
        in_specs=[smem] * 4 + [vmem] * 2,
        out_specs=(vmem,) * 2,
        scratch_shapes=[
            pltpu.VMEM((half, wide), jnp.float32),
            pltpu.VMEM((half // BC, tile_count, BR, BC), jnp.float32),
        ],
        compiler_params=pltpu.CompilerParams(vmem_limit_bytes=20 * MIB),
        cost_estimate=pl.CostEstimate(
            flops=products // 2, bytes_accessed=8 * MIB, transcendentals=0
        ),
        name="diag_products",
    )(ancestors[0], weight_table, pole_slot, jnp.concatenate(late_owners), total, turned)

    everyone_pairs = [shift_pairs(rows, cols, step, everyone) for step in range(cols)]
    arrived = [
        lax.ppermute(diag_send[step - 1], grid, everyone_pairs[step])
        for step in range(1, cols)
    ]
    *rounded, own = pl.pallas_call(
        functools.partial(regroup_kernel, poles, rows),
        out_shape=(jax.ShapeDtypeStruct((part + BR, wide), jnp.bfloat16),) * (rows - 1)
        + (jax.ShapeDtypeStruct((part + BR, wide), jnp.float32),),
        in_specs=[vmem] * (1 + len(arrived)),
        out_specs=(vmem,) * rows,
        compiler_params=pltpu.CompilerParams(vmem_limit_bytes=16 * MIB),
        name="regroup",
    )(diag_keep, *arrived)
    parts = [
        lax.ppermute(rounded[step - 1], "row", [(i, (i + step) % rows) for i in range(rows)])
        for step in range(1, rows)
    ]
    laid_diag, message = pl.pallas_call(
        functools.partial(finish_kernel, poles),
        out_shape=(
            jax.ShapeDtypeStruct((part * 2 * across, BC), jnp.float32),
            jax.ShapeDtypeStruct((part * across + poles * BR, BC), jnp.float32),
        ),
        in_specs=[smem] * 2 + [vmem] * (2 + len(parts)),
        out_specs=(vmem,) * 2,
        compiler_params=pltpu.CompilerParams(vmem_limit_bytes=8 * MIB),
        name="finish",
    )(weight_table, pole_slot, laid(dinv), own, *parts)
    diag_inverse = plain(laid_diag, dinv.shape)
    messages = [message]
    for step in range(1, poles):
        messages.append(lax.ppermute(message, "pole", [(i, i ^ step) for i in range(poles)]))

    split = part * across
    laid_density, tile_sum = pl.pallas_call(
        functools.partial(density_kernel, split),
        out_shape=(
            jax.ShapeDtypeStruct((split, BC), jnp.float32),
            jax.ShapeDtypeStruct((1, BR, BC), jnp.float32),
        ),
        in_specs=[vmem] * poles,
        out_specs=(vmem,) * 2,
        compiler_params=pltpu.CompilerParams(vmem_limit_bytes=8 * MIB),
        name="density",
    )(*messages)
    density_diag = laid_density.reshape(part, 1, half)

    parts = []
    for send, size in zip(sends, sizes):
        parts += [
            lax.ppermute(send[(step - 1) * size : step * size], grid, everyone_pairs[step])
            for step in range(1, cols)
        ]
    block = laid_rows // sum(SPLIT)
    specs = [pl.BlockSpec((block, BC), lambda i: (i, 0))]
    first = 0
    for share in SPLIT:
        spec = pl.BlockSpec(
            (block, BC), lambda i, f=first, n=share: (jnp.clip(i - f, 0, n - 1), 0)
        )
        specs += [spec] * (cols - 1)
        first += share
    column = pl.pallas_call(
        functools.partial(join_kernel, cols - 1),
        grid=(sum(SPLIT),),
        out_shape=jax.ShapeDtypeStruct((laid_rows, BC), jnp.float32),
        in_specs=specs,
        out_specs=pl.BlockSpec((block, BC), lambda i: (i, 0)),
        compiler_params=pltpu.CompilerParams(vmem_limit_bytes=16 * MIB),
        name="join_columns",
    )(keep, *parts)
    column_out = plain(column, (rows_here, 1, 1, 2, half))
    return (column_out, diag_inverse, density_diag, tile_sum)


def solution(mesh):
    in_specs = (
        P("pole", None, "row", "col"),
        P("pole", None, ("row", "col"), None),
        P(("row", "col"), "pole", None, None, None),
        P(),
        P(("row", "col"), None),
        P(),
        P("pole"),
    )
    out_specs = (
        P(("row", "col"), "pole", None, None, None),
        P(("row", "col"), "pole", None, None, None),
        P(("row", "col"), None, None),
        P(("pole", "row", "col"), None, None),
    )
    return jax.shard_map(compute, mesh=mesh, in_specs=in_specs, out_specs=out_specs, check_vma=False)
```

```python
import functools

import jax
import jax.numpy as jnp
from jax import lax
from jax.experimental import pallas as pl
from jax.experimental.pallas import tpu as pltpu
from jax.sharding import PartitionSpec as P


BS = 128
BR = 8
BC = 128
MIB = 1 << 20
SPLIT = (4,)


def shift_pairs(rows, cols, step, valid):
    return [
        (r * cols + c, r * cols + (c + step) % cols)
        for r in range(rows)
        if valid(r)
        for c in range(cols)
    ]


def gather_stages(shard, rows, cols):
    grid = ("row", "col")
    if rows != 4:
        full = lax.all_gather(shard, grid, axis=0, tiled=True).reshape((rows, cols) + shard.shape)
        c = lax.axis_index("col")
        stages = []
        for row in range(rows):
            line = [lax.dynamic_index_in_dim(full[row], (c - step) % cols, 0, False) for step in range(cols)]
            stages.append([[piece] for piece in line])
        return stages, [[row] * rows for row in range(rows)]
    sources = [[0, 1, 2, 3], [1, 0, 3, 2], [2, 2, 1, 1], [3, 3, 0, 0]]
    outer = [(0, 1), (1, 0), (2, 3), (3, 2)]
    inner = [(1, 2), (2, 1)]
    r = lax.axis_index("row")
    middle = jnp.logical_or(r == 1, r == 2)
    height = shard.shape[0] // 2
    stages = [[[] for _ in range(cols)] for _ in range(rows)]
    for part in (0, 1):
        own = shard[part * height : (part + 1) * height]
        near = lax.ppermute(own, "row", outer)
        cross = lax.ppermute(own, "row", inner)
        cross_out = lax.ppermute(cross, "row", outer)
        far = lax.ppermute(near, "row", inner)
        far_out = lax.ppermute(far, "row", outer)
        line = [
            lambda: own,
            lambda: near,
            lambda: jnp.where(middle, cross, cross_out),
            lambda: jnp.where(middle, far, far_out),
        ]
        last = None
        opened = []
        for stage, make in enumerate(line):
            piece = make()
            stages[stage][0].append(piece)
            leaving = piece
            if last is not None and stage < rows - 1:
                leaving, _ = lax.optimization_barrier((piece, last))
            for step in range(1, cols):
                if stage == 1 and part == 1:
                    relayed, _ = lax.optimization_barrier((opened[step - 1], far_out))
                    stages[stage][step].append(lax.ppermute(relayed, "row", outer))
                    continue
                pairs = shift_pairs(rows, cols, step, lambda r: True)
                last = lax.ppermute(leaving, grid, pairs)
                stages[stage][step].append(last)
                if stage == 0:
                    opened.append(last)
    return stages, sources


def counts_of(ancestors, inverse, rows, cols):
    row_blocks, col_blocks = inverse.shape[1] // BS, inverse.shape[2] // BS
    r = lax.axis_index("row")
    c = lax.axis_index("col")

    def below(limit):
        total = jnp.int32(0)
        for i in range(ancestors.shape[0]):
            total = total + (ancestors[i] < limit).astype(jnp.int32)
        return total

    row_first, row_last = below(r * row_blocks), below((r + 1) * row_blocks)
    col_first, col_last = below(c * col_blocks), below((c + 1) * col_blocks)
    count = row_last - row_first
    return rows, cols, row_blocks, col_blocks, row_first, count, col_first, col_last


def source_row(sources, stage):
    r = lax.axis_index("row")
    total = jnp.int32(0)
    for row, source in enumerate(sources[stage]):
        total = total + jnp.where(r == row, source, 0)
    return total


def fill(full, pieces, sources, stage, cols):
    c = lax.axis_index("col")
    source = source_row(sources, stage)
    chunks = len(pieces) // cols
    height = pieces[0].shape[0]
    for step in range(cols):
        shard = source * cols + lax.rem(c - step + cols, cols)
        for chunk in range(chunks):
            start = pl.multiple_of((shard * chunks + chunk) * height, height)
            full[pl.ds(start, height), :] = pieces[step * chunks + chunk][...]


def multiply(acc, inverse, full, ancestors, counts, pair, source):
    rows, _, row_blocks, col_blocks = counts[:4]
    row_first, row_count, col_first, col_last = counts[4:]
    stage_blocks = ancestors.shape[0] // rows
    low = source * stage_blocks
    r = lax.axis_index("row")
    c = lax.axis_index("col")

    @pl.when(jnp.logical_and(low < col_last, low + stage_blocks > col_first))
    def _():
        left = []
        for n in range(stage_blocks):
            k = low + n
            inside = jnp.logical_and(k >= col_first, k < col_last)
            block = jnp.where(inside, ancestors[k] - c * col_blocks, 0)
            column = pl.ds(pl.multiple_of(block * BS, BS), BS)
            both = []
            for i in range(2):
                listed = ancestors[row_first + jnp.minimum(2 * pair + i, row_count - 1)]
                row = pl.multiple_of((listed - r * row_blocks) * BS, BS)
                both.append(inverse[:, pl.ds(row, BS), column].reshape(2 * BS, BS))
            value = jnp.concatenate(both, axis=0)
            left.append(value * inside.astype(value.dtype))
        place = pl.ds(pl.multiple_of(low * BS, BS), stage_blocks * BS)
        acc[...] += jnp.dot(
            jnp.concatenate(left, axis=1), full[place, :], preferred_element_type=jnp.float32
        )


def combine(acc, n):
    half = acc.shape[1] // 2
    upper, lower = acc.at[2 * n * BS : (2 * n + 1) * BS], acc.at[(2 * n + 1) * BS : (2 * n + 2) * BS]
    return upper[:, :half] - lower[:, half:], upper[:, half:] + lower[:, :half]


def add_products(sources, stages, ancestors, inverse, before, full, acc, counts, store):
    row_count = counts[5]

    @pl.loop(0, (row_count + 1) // 2)
    def _(pair):
        if before is None:
            acc[...] = jnp.zeros_like(acc)
        else:
            for n in range(2):
                i = jnp.minimum(2 * pair + n, row_count - 1)
                acc[2 * n * BS : (2 * n + 1) * BS, :] = before[i]
                acc[(2 * n + 1) * BS : (2 * n + 2) * BS, :] = jnp.zeros((BS, acc.shape[1]), acc.dtype)
        for stage in stages:
            multiply(acc, inverse, full, ancestors, counts, pair, source_row(sources, stage))
        for n in range(2):

            @pl.when(2 * pair + n < row_count)
            def _():
                store(2 * pair + n, *combine(acc, n))


def early_kernel(sources, stages, added, rows, cols, ancestors, inverse, *refs):
    early, full, acc = refs[-3:]
    before = refs[0] if added else None
    pieces = refs[1 if added else 0 : -3]
    each = len(pieces) // len(stages)
    half = acc.shape[1] // 2
    for n, stage in enumerate(stages):
        fill(full, pieces[n * each : (n + 1) * each], sources, stage, cols)
    counts = counts_of(ancestors, inverse, rows, cols)

    def store(i, real, imag):
        early[i, :, :half] = real
        early[i, :, half:] = imag

    add_products(sources, stages, ancestors, inverse, before, full, acc, counts, store)


def last_kernel(sources, stages, rows, cols, ancestors, inverse, early, *refs):
    keep, *sends, total, turned, full, acc, leaving = refs[-(6 + len(SPLIT)) :]
    pieces = refs[: -(6 + len(SPLIT))]
    each = len(pieces) // rows
    half = acc.shape[1] // 2
    across = half // BC
    row_blocks = early.shape[0]
    own_blocks = row_blocks // cols
    r = lax.axis_index("row")
    c = lax.axis_index("col")
    for stage in range(rows):
        fill(full, pieces[stage * each : (stage + 1) * each], sources, stage, cols)
    counts = counts_of(ancestors, inverse, rows, cols)
    row_first = counts[4]
    keep[...] = jnp.zeros_like(keep)
    leaving[...] = jnp.zeros_like(leaving)

    def store(i, real, imag):
        total[i, :, :half] = real
        total[i, :, half:] = imag
        block = ancestors[row_first + i] - r * row_blocks
        within = lax.rem(block, own_blocks) * (BS * 2 * across)
        turn = lax.rem(block // own_blocks - c + cols, cols)

        def lay(target, start):
            for j in range(across):
                for n, value in enumerate((real, imag)):
                    rows_of = pl.ds(start + 2 * j + n, BS, stride=2 * across)
                    target[rows_of, :] = -value[:, j * BC : (j + 1) * BC]

        @pl.when(turn == 0)
        def _():
            lay(keep, within)

        @pl.when(turn > 0)
        def _():
            lay(leaving, (turn - 1) * keep.shape[0] + within)

        rows_of = full[pl.ds(pl.multiple_of((row_first + i) * BS, BS), BS), :]
        left = jnp.concatenate([rows_of[:, :half], rows_of[:, half:]], axis=0)
        turned[i] = left.T

    add_products(sources, stages, ancestors, inverse, early, full, acc, counts, store)
    height = keep.shape[0]
    for step in range(cols - 1):
        first = 0
        for send, share in zip(sends, SPLIT):
            size = height * share // sum(SPLIT)
            value = leaving[step * height + first : step * height + first + size, :]
            send[step * size : (step + 1) * size, :] = value.astype(send.dtype)
            first += size


def diag_kernel(poles, rows, cols, row_blocks, ancestors, table, slot, owner, total, turned, *refs):
    diag_keep, diag_send, diag, tiles = refs
    half, wide = diag.shape
    across = half // BC
    own_blocks = row_blocks // cols
    r = lax.axis_index("row")
    c = lax.axis_index("col")

    def below(limit):
        count = jnp.int32(0)
        for i in range(ancestors.shape[0]):
            count = count + (ancestors[i] < limit).astype(jnp.int32)
        return count

    row_first = below(r * row_blocks)
    diag[...] = jnp.zeros_like(diag)
    tiles[...] = jnp.zeros_like(tiles)
    weight_real = table[0, slot[0]]
    weight_imag = table[1, slot[0]]

    @pl.loop(0, below((r + 1) * row_blocks) - row_first)
    def _(i):
        real = total[i, :, :half]
        imag = total[i, :, half:]
        left = turned[i]
        real_high = real.astype(jnp.bfloat16)
        imag_high = imag.astype(jnp.bfloat16)
        real_low = (real - real_high.astype(jnp.float32)).astype(jnp.bfloat16)
        imag_low = (imag - imag_high.astype(jnp.float32)).astype(jnp.bfloat16)
        right = jnp.concatenate(
            [
                jnp.concatenate([real_high, imag_high], axis=1),
                jnp.concatenate([-imag_high, real_high], axis=1),
                jnp.concatenate([real_low, imag_low], axis=1),
                jnp.concatenate([-imag_low, real_low], axis=1),
            ],
            axis=0,
        )
        diag[...] += jnp.dot(
            jnp.concatenate([left, left], axis=1), right, preferred_element_type=jnp.float32
        )
        block = ancestors[row_first + i] - r * row_blocks
        place = block // own_blocks
        mixed = -(weight_real * imag + weight_imag * real)
        per_device = own_blocks * (BS // BR) * across
        first = lax.rem(c - place + cols, cols) * per_device + lax.rem(block, own_blocks) * (
            BS // BR
        ) * across
        for group in range(BS // BR):
            for j in range(across):
                tile = owner[first + group * across + j]
                tiles[j, tile] += mixed[group * BR : (group + 1) * BR, j * BC : (j + 1) * BC]

    part = half // (rows * cols)
    for row in range(rows):
        for step in range(cols):
            place = row * cols + lax.rem(c + step, cols)
            value = diag[pl.ds(pl.multiple_of(place * part, part), part), :]
            if step == 0:
                diag_keep[row, :part] = value
                diag_keep[row, part:] = jnp.zeros((BR, wide), jnp.float32)
            else:
                diag_send[step - 1, row, :part] = value.astype(diag_send.dtype)
                diag_send[step - 1, row, part:] = jnp.zeros((BR, wide), diag_send.dtype)
            for pole in range(poles):
                sum_of = tiles[0, pole * rows * cols + place]
                for j in range(1, across):
                    sum_of = sum_of + tiles[j, pole * rows * cols + place]
                if step == 0:
                    diag_keep[row, part:, 2 * pole * BC : (2 * pole + 1) * BC] = sum_of
                else:
                    diag_send[step - 1, row, part:, 2 * pole * BC : 2 * (pole + 1) * BC] = halves(sum_of)


def density_kernel(split, *refs):
    *messages, density, tile = refs
    start = pl.multiple_of(split + lax.axis_index("pole") * BR, BR)
    for place, out in ((pl.ds(0, split), density.at[...]), (pl.ds(start, BR), tile.at[0])):
        values = [message[place, :] for message in messages]
        while len(values) > 1:
            values = [a + b for a, b in zip(values[::2], values[1::2])]
        out[...] = values[0]


def join_kernel(steps, keep, *refs):
    out = refs[-1]
    block = pl.program_id(0)
    first = 0
    for n, share in enumerate(SPLIT):
        arrived = refs[n * steps : (n + 1) * steps]

        @pl.when(jnp.logical_and(block >= first, block < first + share))
        def _():
            value = keep[...]
            for ref in arrived:
                value = value + ref[...].astype(jnp.float32)
            out[...] = value

        first += share


def halves(value):
    high = value.astype(jnp.bfloat16)
    low = (value - high.astype(jnp.float32)).astype(jnp.bfloat16)
    return jnp.concatenate([high, low], axis=1)


def regroup_kernel(poles, rows, kept, *refs):
    *rounded, own = refs[-rows:]
    arrived = refs[:-rows]
    part = own.shape[0] - BR
    r = lax.axis_index("row")

    def total(row):
        value = kept[row]
        for ref in arrived:
            value = value + ref[row].astype(jnp.float32)
        return value

    own[...] = total(r)
    for step in range(1, rows):
        value = total(lax.rem(r + step, rows))
        out = rounded[step - 1]
        out[:part] = value[:part].astype(out.dtype)
        for pole in range(poles):
            first = 2 * pole * BC
            band = value[part:, first : first + BC] + value[part:, first + BC : first + 2 * BC]
            out[part:, first : first + 2 * BC] = halves(band)


def finish_kernel(poles, table, slot, laid_dinv, own, *refs):
    diag_out, message = refs[-2:]
    arrived = refs[:-2]
    part, wide = own.shape[0] - BR, own.shape[1]
    across = wide // (2 * BC)
    total = own[...]
    for ref in arrived:
        total = total + ref[...].astype(jnp.float32)
    weight_real = table[0, slot[0]]
    weight_imag = table[1, slot[0]]
    for j in range(across):
        values = []
        for n in range(2):
            rows_of = pl.ds(2 * j + n, part, stride=2 * across)
            first = (n * across + j) * BC
            values.append(laid_dinv[rows_of, :] + total[:part, first : first + BC])
            diag_out[rows_of, :] = values[n]
        share = weight_real * values[1] + weight_imag * values[0]
        message[pl.ds(j, part, stride=across), :] = share
    for pole in range(poles):
        first = 2 * pole * BC
        band = total[part:, first : first + BC] + total[part:, first + BC : first + 2 * BC]
        start = part * across + pole * BR
        message[start : start + BR] = band


def compute(inverse, factor, dinv, ancestors, owner, weight_table, pole_slot):
    rows = lax.axis_size("row")
    cols = lax.axis_size("col")
    poles = lax.axis_size("pole")
    grid = ("row", "col")
    tile_count = poles * rows * cols
    here = inverse[0]
    wide = factor.shape[3]
    half = wide // 2
    rows_here = here.shape[1] // cols
    row_blocks = here.shape[1] // BS
    selected = ancestors.shape[1]
    part = half // (rows * cols)
    everyone = lambda r: True

    owners = [owner[:, 0]]
    for step in range(1, cols):
        pairs = shift_pairs(rows, cols, step, everyone)
        owners.append(lax.ppermute(owner[:, 0], grid, pairs))
    smem = pl.BlockSpec(memory_space=pltpu.SMEM)
    vmem = pl.BlockSpec(memory_space=pltpu.VMEM)
    whole = pl.BlockSpec(memory_space=pl.ANY)
    across = half // BC

    def laid(value):
        value = value.reshape(-1, 2, across, BC).transpose(0, 2, 1, 3)
        return value.reshape(-1, BC)

    def plain(value, shape):
        value = value.reshape(-1, across, 2, BC).transpose(0, 2, 1, 3)
        return value.reshape(shape)

    stages, sources = gather_stages(factor[0, 0], rows, cols)
    stages = [[chunk for step in stage for chunk in step] for stage in stages]
    products = 2 * row_blocks * BS * 2 * wide * selected * BS // cols
    scratch = [
        pltpu.VMEM((selected * BS, wide), jnp.bfloat16),
        pltpu.VMEM((4 * BS, wide), jnp.float32),
    ]
    row_products = jax.ShapeDtypeStruct((row_blocks, BS, wide), jnp.float32)
    groups = [(0, rows - 2)] if rows > 2 else [(0,)]
    last = tuple(stage for stage in range(rows) if stage not in groups[0])
    early = []
    for group in groups:
        group_pieces = [piece for stage in group for piece in stages[stage]]
        early = [
            pl.pallas_call(
                functools.partial(early_kernel, sources, group, bool(early), rows, cols),
                out_shape=row_products,
                in_specs=[smem, vmem] + [vmem] * (len(early) + len(group_pieces)),
                out_specs=vmem,
                scratch_shapes=scratch,
                input_output_aliases={2: 0} if early else {},
                compiler_params=pltpu.CompilerParams(vmem_limit_bytes=24 * MIB),
                cost_estimate=pl.CostEstimate(
                    flops=products * len(group) // rows,
                    bytes_accessed=4 * MIB,
                    transcendentals=0,
                ),
                name="early_products",
            )(ancestors[0], here, *early, *group_pieces)
        ]
    late_owners, _ = lax.optimization_barrier((tuple(owners), early))
    all_pieces = [piece for stage in stages for piece in stage]
    others = max(1, cols - 1)
    laid_rows = rows_here * wide // BC
    sizes = [laid_rows * share // sum(SPLIT) for share in SPLIT]
    keep, *sends, total, turned = pl.pallas_call(
        functools.partial(last_kernel, sources, last, rows, cols),
        out_shape=(jax.ShapeDtypeStruct((laid_rows, BC), jnp.float32),)
        + tuple(jax.ShapeDtypeStruct((others * size, BC), jnp.bfloat16) for size in sizes)
        + (row_products, jax.ShapeDtypeStruct((row_blocks, half, 2 * BS), jnp.bfloat16)),
        in_specs=[smem] + [vmem] * (2 + len(all_pieces)),
        out_specs=(vmem,) * (3 + len(SPLIT)),
        scratch_shapes=scratch + [pltpu.VMEM((others * laid_rows, BC), jnp.float32)],
        compiler_params=pltpu.CompilerParams(vmem_limit_bytes=28 * MIB),
        cost_estimate=pl.CostEstimate(
            flops=products // 2, bytes_accessed=8 * MIB, transcendentals=0
        ),
        name="last_products",
    )(ancestors[0], here, *early, *all_pieces)
    diag_keep, diag_send = pl.pallas_call(
        functools.partial(diag_kernel, poles, rows, cols, row_blocks),
        out_shape=(
            jax.ShapeDtypeStruct((rows, part + BR, wide), jnp.float32),
            jax.ShapeDtypeStruct((others, rows, part + BR, wide), jnp.bfloat16),
        ),
        in_specs=[smem] * 4 + [vmem] * 2,
        out_specs=(vmem,) * 2,
        scratch_shapes=[
            pltpu.VMEM((half, wide), jnp.float32),
            pltpu.VMEM((half // BC, tile_count, BR, BC), jnp.float32),
        ],
        compiler_params=pltpu.CompilerParams(vmem_limit_bytes=20 * MIB),
        cost_estimate=pl.CostEstimate(
            flops=products // 2, bytes_accessed=8 * MIB, transcendentals=0
        ),
        name="diag_products",
    )(ancestors[0], weight_table, pole_slot, jnp.concatenate(late_owners), total, turned)

    everyone_pairs = [shift_pairs(rows, cols, step, everyone) for step in range(cols)]
    arrived = [
        lax.ppermute(diag_send[step - 1], grid, everyone_pairs[step])
        for step in range(1, cols)
    ]
    *rounded, own = pl.pallas_call(
        functools.partial(regroup_kernel, poles, rows),
        out_shape=(jax.ShapeDtypeStruct((part + BR, wide), jnp.bfloat16),) * (rows - 1)
        + (jax.ShapeDtypeStruct((part + BR, wide), jnp.float32),),
        in_specs=[vmem] * (1 + len(arrived)),
        out_specs=(vmem,) * rows,
        compiler_params=pltpu.CompilerParams(vmem_limit_bytes=16 * MIB),
        name="regroup",
    )(diag_keep, *arrived)
    parts = [
        lax.ppermute(rounded[step - 1], "row", [(i, (i + step) % rows) for i in range(rows)])
        for step in range(1, rows)
    ]
    laid_diag, message = pl.pallas_call(
        functools.partial(finish_kernel, poles),
        out_shape=(
            jax.ShapeDtypeStruct((part * 2 * across, BC), jnp.float32),
            jax.ShapeDtypeStruct((part * across + poles * BR, BC), jnp.float32),
        ),
        in_specs=[smem] * 2 + [vmem] * (2 + len(parts)),
        out_specs=(vmem,) * 2,
        compiler_params=pltpu.CompilerParams(vmem_limit_bytes=8 * MIB),
        name="finish",
    )(weight_table, pole_slot, laid(dinv), own, *parts)
    diag_inverse = plain(laid_diag, dinv.shape)
    messages = [message]
    for step in range(1, poles):
        messages.append(lax.ppermute(message, "pole", [(i, i ^ step) for i in range(poles)]))

    split = part * across
    laid_density, tile_sum = pl.pallas_call(
        functools.partial(density_kernel, split),
        out_shape=(
            jax.ShapeDtypeStruct((split, BC), jnp.float32),
            jax.ShapeDtypeStruct((1, BR, BC), jnp.float32),
        ),
        in_specs=[vmem] * poles,
        out_specs=(vmem,) * 2,
        compiler_params=pltpu.CompilerParams(vmem_limit_bytes=8 * MIB),
        name="density",
    )(*messages)
    density_diag = laid_density.reshape(part, 1, half)

    parts = []
    for send, size in zip(sends, sizes):
        parts += [
            lax.ppermute(send[(step - 1) * size : step * size], grid, everyone_pairs[step])
            for step in range(1, cols)
        ]
    block = laid_rows // sum(SPLIT)
    specs = [pl.BlockSpec((block, BC), lambda i: (i, 0))]
    first = 0
    for share in SPLIT:
        spec = pl.BlockSpec(
            (block, BC), lambda i, f=first, n=share: (jnp.clip(i - f, 0, n - 1), 0)
        )
        specs += [spec] * (cols - 1)
        first += share
    column = pl.pallas_call(
        functools.partial(join_kernel, cols - 1),
        grid=(sum(SPLIT),),
        out_shape=jax.ShapeDtypeStruct((laid_rows, BC), jnp.float32),
        in_specs=specs,
        out_specs=pl.BlockSpec((block, BC), lambda i: (i, 0)),
        compiler_params=pltpu.CompilerParams(vmem_limit_bytes=16 * MIB),
        name="join_columns",
    )(keep, *parts)
    column_out = plain(column, (rows_here, 1, 1, 2, half))
    return (column_out, diag_inverse, density_diag, tile_sum)


def solution(mesh):
    in_specs = (
        P("pole", None, "row", "col"),
        P("pole", None, ("row", "col"), None),
        P(("row", "col"), "pole", None, None, None),
        P(),
        P(("row", "col"), None),
        P(),
        P("pole"),
    )
    out_specs = (
        P(("row", "col"), "pole", None, None, None),
        P(("row", "col"), "pole", None, None, None),
        P(("row", "col"), None, None),
        P(("pole", "row", "col"), None, None),
    )
    return jax.shard_map(compute, mesh=mesh, in_specs=in_specs, out_specs=out_specs, check_vma=False)
```

```python
import functools

import jax
import jax.numpy as jnp
from jax import lax
from jax.experimental import pallas as pl
from jax.experimental.pallas import tpu as pltpu
from jax.sharding import PartitionSpec as P


BS = 128
BR = 8
BC = 128
MIB = 1 << 20
SPLIT = (4,)


def shift_pairs(rows, cols, step, valid):
    return [
        (r * cols + c, r * cols + (c + step) % cols)
        for r in range(rows)
        if valid(r)
        for c in range(cols)
    ]


def gather_stages(shard, rows, cols):
    grid = ("row", "col")
    if rows != 4:
        full = lax.all_gather(shard, grid, axis=0, tiled=True).reshape((rows, cols) + shard.shape)
        c = lax.axis_index("col")
        stages = []
        for row in range(rows):
            line = [lax.dynamic_index_in_dim(full[row], (c - step) % cols, 0, False) for step in range(cols)]
            stages.append([[piece] for piece in line])
        return stages, [[row] * rows for row in range(rows)]
    sources = [[0, 1, 2, 3], [1, 0, 3, 2], [2, 2, 1, 1], [3, 3, 0, 0]]
    outer = [(0, 1), (1, 0), (2, 3), (3, 2)]
    inner = [(1, 2), (2, 1)]
    r = lax.axis_index("row")
    middle = jnp.logical_or(r == 1, r == 2)
    height = shard.shape[0] // 2
    stages = [[[] for _ in range(cols)] for _ in range(rows)]
    for part in (0, 1):
        own = shard[part * height : (part + 1) * height]
        near = lax.ppermute(own, "row", outer)
        cross = lax.ppermute(own, "row", inner)
        cross_out = lax.ppermute(cross, "row", outer)
        far = lax.ppermute(near, "row", inner)
        far_out = lax.ppermute(far, "row", outer)
        line = [
            lambda: own,
            lambda: near,
            lambda: jnp.where(middle, cross, cross_out),
            lambda: jnp.where(middle, far, far_out),
        ]
        last = None
        opened = []
        for stage, make in enumerate(line):
            piece = make()
            stages[stage][0].append(piece)
            leaving = piece
            if last is not None and stage < rows - 1:
                leaving, _ = lax.optimization_barrier((piece, last))
            for step in range(1, cols):
                if stage == 1 and part == 1:
                    relayed, _ = lax.optimization_barrier((opened[step - 1], far_out))
                    stages[stage][step].append(lax.ppermute(relayed, "row", outer))
                    continue
                pairs = shift_pairs(rows, cols, step, lambda r: True)
                last = lax.ppermute(leaving, grid, pairs)
                stages[stage][step].append(last)
                if stage == 0:
                    opened.append(last)
    return stages, sources


def counts_of(ancestors, inverse, rows, cols):
    row_blocks, col_blocks = inverse.shape[1] // BS, inverse.shape[2] // BS
    r = lax.axis_index("row")
    c = lax.axis_index("col")

    def below(limit):
        total = jnp.int32(0)
        for i in range(ancestors.shape[0]):
            total = total + (ancestors[i] < limit).astype(jnp.int32)
        return total

    row_first, row_last = below(r * row_blocks), below((r + 1) * row_blocks)
    col_first, col_last = below(c * col_blocks), below((c + 1) * col_blocks)
    count = row_last - row_first
    return rows, cols, row_blocks, col_blocks, row_first, count, col_first, col_last


def source_row(sources, stage):
    r = lax.axis_index("row")
    total = jnp.int32(0)
    for row, source in enumerate(sources[stage]):
        total = total + jnp.where(r == row, source, 0)
    return total


def fill(full, pieces, sources, stage, cols):
    c = lax.axis_index("col")
    source = source_row(sources, stage)
    chunks = len(pieces) // cols
    height = pieces[0].shape[0]
    for step in range(cols):
        shard = source * cols + lax.rem(c - step + cols, cols)
        for chunk in range(chunks):
            start = pl.multiple_of((shard * chunks + chunk) * height, height)
            full[pl.ds(start, height), :] = pieces[step * chunks + chunk][...]


def multiply(acc, inverse, full, ancestors, counts, pair, source):
    rows, _, row_blocks, col_blocks = counts[:4]
    row_first, row_count, col_first, col_last = counts[4:]
    stage_blocks = ancestors.shape[0] // rows
    low = source * stage_blocks
    r = lax.axis_index("row")
    c = lax.axis_index("col")

    start = jnp.maximum(low, col_first)
    width = jnp.minimum(low + stage_blocks, col_last) - start

    def add(first, blocks):
        left = []
        for n in range(blocks):
            k = first + n
            inside = jnp.logical_and(k >= col_first, k < col_last)
            block = jnp.where(inside, ancestors[k] - c * col_blocks, 0)
            column = pl.ds(pl.multiple_of(block * BS, BS), BS)
            both = []
            for i in range(2):
                listed = ancestors[row_first + jnp.minimum(2 * pair + i, row_count - 1)]
                row = pl.multiple_of((listed - r * row_blocks) * BS, BS)
                both.append(inverse[:, pl.ds(row, BS), column].reshape(2 * BS, BS))
            value = jnp.concatenate(both, axis=0)
            left.append(value * inside.astype(value.dtype))
        place = pl.ds(pl.multiple_of(first * BS, BS), blocks * BS)
        acc[...] += jnp.dot(
            jnp.concatenate(left, axis=1), full[place, :], preferred_element_type=jnp.float32
        )

    few = stage_blocks // 2

    @pl.when(width > few)
    def _():
        add(low, stage_blocks)

    @pl.when(jnp.logical_and(width > 0, width <= few))
    def _():
        add(jnp.minimum(start, low + stage_blocks - few), few)


def combine(acc, n):
    half = acc.shape[1] // 2
    upper, lower = acc.at[2 * n * BS : (2 * n + 1) * BS], acc.at[(2 * n + 1) * BS : (2 * n + 2) * BS]
    return upper[:, :half] - lower[:, half:], upper[:, half:] + lower[:, :half]


def add_products(sources, stages, ancestors, inverse, before, full, acc, counts, store):
    row_count = counts[5]

    @pl.loop(0, (row_count + 1) // 2)
    def _(pair):
        if before is None:
            acc[...] = jnp.zeros_like(acc)
        else:
            for n in range(2):
                i = jnp.minimum(2 * pair + n, row_count - 1)
                acc[2 * n * BS : (2 * n + 1) * BS, :] = before[i]
                acc[(2 * n + 1) * BS : (2 * n + 2) * BS, :] = jnp.zeros((BS, acc.shape[1]), acc.dtype)
        for stage in stages:
            multiply(acc, inverse, full, ancestors, counts, pair, source_row(sources, stage))
        for n in range(2):

            @pl.when(2 * pair + n < row_count)
            def _():
                store(2 * pair + n, *combine(acc, n))


def list_kernel(ancestors, out):
    for i in range(ancestors.shape[0]):
        out[i] = ancestors[i]


def early_kernel(sources, stages, added, rows, cols, ancestors, inverse, *refs):
    early, full, acc = refs[-3:]
    before = refs[0] if added else None
    pieces = refs[1 if added else 0 : -3]
    each = len(pieces) // len(stages)
    half = acc.shape[1] // 2
    for n, stage in enumerate(stages):
        fill(full, pieces[n * each : (n + 1) * each], sources, stage, cols)
    counts = counts_of(ancestors, inverse, rows, cols)

    def store(i, real, imag):
        early[i, :, :half] = real
        early[i, :, half:] = imag

    add_products(sources, stages, ancestors, inverse, before, full, acc, counts, store)


def last_kernel(sources, stages, rows, cols, ancestors, inverse, early, *refs):
    keep, *sends, total, turned, full, acc, leaving = refs[-(6 + len(SPLIT)) :]
    pieces = refs[: -(6 + len(SPLIT))]
    each = len(pieces) // rows
    half = acc.shape[1] // 2
    across = half // BC
    row_blocks = early.shape[0]
    own_blocks = row_blocks // cols
    r = lax.axis_index("row")
    c = lax.axis_index("col")
    for stage in range(rows):
        fill(full, pieces[stage * each : (stage + 1) * each], sources, stage, cols)
    counts = counts_of(ancestors, inverse, rows, cols)
    row_first = counts[4]
    keep[...] = jnp.zeros_like(keep)
    leaving[...] = jnp.zeros_like(leaving)

    def store(i, real, imag):
        total[i, :, :half] = real
        total[i, :, half:] = imag
        block = ancestors[row_first + i] - r * row_blocks
        within = lax.rem(block, own_blocks) * (BS * 2 * across)
        turn = lax.rem(block // own_blocks - c + cols, cols)

        def lay(target, start):
            for j in range(across):
                for n, value in enumerate((real, imag)):
                    rows_of = pl.ds(start + 2 * j + n, BS, stride=2 * across)
                    target[rows_of, :] = -value[:, j * BC : (j + 1) * BC]

        @pl.when(turn == 0)
        def _():
            lay(keep, within)

        @pl.when(turn > 0)
        def _():
            lay(leaving, (turn - 1) * keep.shape[0] + within)

        rows_of = full[pl.ds(pl.multiple_of((row_first + i) * BS, BS), BS), :]
        left = jnp.concatenate([rows_of[:, :half], rows_of[:, half:]], axis=0)
        turned[i] = left.T

    add_products(sources, stages, ancestors, inverse, early, full, acc, counts, store)
    height = keep.shape[0]
    for step in range(cols - 1):
        first = 0
        for send, share in zip(sends, SPLIT):
            size = height * share // sum(SPLIT)
            value = leaving[step * height + first : step * height + first + size, :]
            send[step * size : (step + 1) * size, :] = value.astype(send.dtype)
            first += size


def diag_kernel(poles, rows, cols, row_blocks, ancestors, table, slot, owner, total, turned, *refs):
    diag_keep, diag_send, diag, tiles = refs
    half, wide = diag.shape
    across = half // BC
    own_blocks = row_blocks // cols
    r = lax.axis_index("row")
    c = lax.axis_index("col")

    def below(limit):
        count = jnp.int32(0)
        for i in range(ancestors.shape[0]):
            count = count + (ancestors[i] < limit).astype(jnp.int32)
        return count

    row_first = below(r * row_blocks)
    diag[...] = jnp.zeros_like(diag)
    tiles[...] = jnp.zeros_like(tiles)
    weight_real = table[0, slot[0]]
    weight_imag = table[1, slot[0]]

    @pl.loop(0, below((r + 1) * row_blocks) - row_first)
    def _(i):
        real = total[i, :, :half]
        imag = total[i, :, half:]
        left = turned[i]
        real_high = real.astype(jnp.bfloat16)
        imag_high = imag.astype(jnp.bfloat16)
        real_low = (real - real_high.astype(jnp.float32)).astype(jnp.bfloat16)
        imag_low = (imag - imag_high.astype(jnp.float32)).astype(jnp.bfloat16)
        right = jnp.concatenate(
            [
                jnp.concatenate([real_high, imag_high], axis=1),
                jnp.concatenate([-imag_high, real_high], axis=1),
                jnp.concatenate([real_low, imag_low], axis=1),
                jnp.concatenate([-imag_low, real_low], axis=1),
            ],
            axis=0,
        )
        diag[...] += jnp.dot(
            jnp.concatenate([left, left], axis=1), right, preferred_element_type=jnp.float32
        )
        block = ancestors[row_first + i] - r * row_blocks
        place = block // own_blocks
        mixed = -(weight_real * imag + weight_imag * real)
        per_device = own_blocks * (BS // BR) * across
        first = lax.rem(c - place + cols, cols) * per_device + lax.rem(block, own_blocks) * (
            BS // BR
        ) * across
        for group in range(BS // BR):
            for j in range(across):
                tile = owner[first + group * across + j]
                tiles[j, tile] += mixed[group * BR : (group + 1) * BR, j * BC : (j + 1) * BC]

    part = half // (rows * cols)
    for row in range(rows):
        for step in range(cols):
            place = row * cols + lax.rem(c + step, cols)
            value = diag[pl.ds(pl.multiple_of(place * part, part), part), :]
            if step == 0:
                diag_keep[row, :part] = value
                diag_keep[row, part:] = jnp.zeros((BR, wide), jnp.float32)
            else:
                diag_send[step - 1, row, :part] = value.astype(diag_send.dtype)
                diag_send[step - 1, row, part:] = jnp.zeros((BR, wide), diag_send.dtype)
            for pole in range(poles):
                sum_of = tiles[0, pole * rows * cols + place]
                for j in range(1, across):
                    sum_of = sum_of + tiles[j, pole * rows * cols + place]
                if step == 0:
                    diag_keep[row, part:, 2 * pole * BC : (2 * pole + 1) * BC] = sum_of
                else:
                    diag_send[step - 1, row, part:, 2 * pole * BC : 2 * (pole + 1) * BC] = halves(sum_of)


def density_kernel(split, *refs):
    *messages, density, tile = refs
    start = pl.multiple_of(split + lax.axis_index("pole") * BR, BR)
    for place, out in ((pl.ds(0, split), density.at[...]), (pl.ds(start, BR), tile.at[0])):
        values = [message[place, :] for message in messages]
        while len(values) > 1:
            values = [a + b for a, b in zip(values[::2], values[1::2])]
        out[...] = values[0]


def join_kernel(steps, keep, *refs):
    out = refs[-1]
    block = pl.program_id(0)
    first = 0
    for n, share in enumerate(SPLIT):
        arrived = refs[n * steps : (n + 1) * steps]

        @pl.when(jnp.logical_and(block >= first, block < first + share))
        def _():
            value = keep[...]
            for ref in arrived:
                value = value + ref[...].astype(jnp.float32)
            out[...] = value

        first += share


def halves(value):
    high = value.astype(jnp.bfloat16)
    low = (value - high.astype(jnp.float32)).astype(jnp.bfloat16)
    return jnp.concatenate([high, low], axis=1)


def regroup_kernel(poles, rows, kept, *refs):
    *rounded, own = refs[-rows:]
    arrived = refs[:-rows]
    part = own.shape[0] - BR
    r = lax.axis_index("row")

    def total(row):
        value = kept[row]
        for ref in arrived:
            value = value + ref[row].astype(jnp.float32)
        return value

    own[...] = total(r)
    for step in range(1, rows):
        value = total(lax.rem(r + step, rows))
        out = rounded[step - 1]
        out[:part] = value[:part].astype(out.dtype)
        for pole in range(poles):
            first = 2 * pole * BC
            band = value[part:, first : first + BC] + value[part:, first + BC : first + 2 * BC]
            out[part:, first : first + 2 * BC] = halves(band)


def finish_kernel(poles, table, slot, laid_dinv, own, *refs):
    diag_out, message = refs[-2:]
    arrived = refs[:-2]
    part, wide = own.shape[0] - BR, own.shape[1]
    across = wide // (2 * BC)
    total = own[...]
    for ref in arrived:
        total = total + ref[...].astype(jnp.float32)
    weight_real = table[0, slot[0]]
    weight_imag = table[1, slot[0]]
    for j in range(across):
        values = []
        for n in range(2):
            rows_of = pl.ds(2 * j + n, part, stride=2 * across)
            first = (n * across + j) * BC
            values.append(laid_dinv[rows_of, :] + total[:part, first : first + BC])
            diag_out[rows_of, :] = values[n]
        share = weight_real * values[1] + weight_imag * values[0]
        message[pl.ds(j, part, stride=across), :] = share
    for pole in range(poles):
        first = 2 * pole * BC
        band = total[part:, first : first + BC] + total[part:, first + BC : first + 2 * BC]
        start = part * across + pole * BR
        message[start : start + BR] = band


def compute(inverse, factor, dinv, ancestors, owner, weight_table, pole_slot):
    rows = lax.axis_size("row")
    cols = lax.axis_size("col")
    poles = lax.axis_size("pole")
    grid = ("row", "col")
    tile_count = poles * rows * cols
    here = inverse[0]
    wide = factor.shape[3]
    half = wide // 2
    rows_here = here.shape[1] // cols
    row_blocks = here.shape[1] // BS
    selected = ancestors.shape[1]
    part = half // (rows * cols)
    everyone = lambda r: True

    owners = [owner[:, 0]]
    for step in range(1, cols):
        pairs = shift_pairs(rows, cols, step, everyone)
        owners.append(lax.ppermute(owner[:, 0], grid, pairs))
    smem = pl.BlockSpec(memory_space=pltpu.SMEM)
    vmem = pl.BlockSpec(memory_space=pltpu.VMEM)
    whole = pl.BlockSpec(memory_space=pl.ANY)
    across = half // BC

    def laid(value):
        value = value.reshape(-1, 2, across, BC).transpose(0, 2, 1, 3)
        return value.reshape(-1, BC)

    def plain(value, shape):
        value = value.reshape(-1, across, 2, BC).transpose(0, 2, 1, 3)
        return value.reshape(shape)

    stages, sources = gather_stages(factor[0, 0], rows, cols)
    stages = [[chunk for step in stage for chunk in step] for stage in stages]
    products = 2 * row_blocks * BS * 2 * wide * selected * BS // cols
    scratch = [
        pltpu.VMEM((selected * BS, wide), jnp.bfloat16),
        pltpu.VMEM((4 * BS, wide), jnp.float32),
    ]
    row_products = jax.ShapeDtypeStruct((row_blocks, BS, wide), jnp.float32)
    groups = [(0, rows - 2)] if rows > 2 else [(0,)]
    last = tuple(stage for stage in range(rows) if stage not in groups[0])
    listing = pl.pallas_call(
        list_kernel,
        out_shape=jax.ShapeDtypeStruct((selected,), jnp.int32),
        in_specs=[smem],
        out_specs=smem,
        compiler_params=pltpu.CompilerParams(vmem_limit_bytes=MIB),
        cost_estimate=pl.CostEstimate(flops=products, bytes_accessed=8 * MIB, transcendentals=0),
        name="list_blocks",
    )(ancestors[0])
    early = []
    for group in groups:
        group_pieces = [piece for stage in group for piece in stages[stage]]
        early = [
            pl.pallas_call(
                functools.partial(early_kernel, sources, group, bool(early), rows, cols),
                out_shape=row_products,
                in_specs=[smem, vmem] + [vmem] * (len(early) + len(group_pieces)),
                out_specs=vmem,
                scratch_shapes=scratch,
                input_output_aliases={2: 0} if early else {},
                compiler_params=pltpu.CompilerParams(vmem_limit_bytes=24 * MIB),
                cost_estimate=pl.CostEstimate(
                    flops=products * len(group) // rows,
                    bytes_accessed=4 * MIB,
                    transcendentals=0,
                ),
                name="early_products",
            )(listing, here, *early, *group_pieces)
        ]
    late_owners, _ = lax.optimization_barrier((tuple(owners), early))
    all_pieces = [piece for stage in stages for piece in stage]
    others = max(1, cols - 1)
    laid_rows = rows_here * wide // BC
    sizes = [laid_rows * share // sum(SPLIT) for share in SPLIT]
    keep, *sends, total, turned = pl.pallas_call(
        functools.partial(last_kernel, sources, last, rows, cols),
        out_shape=(jax.ShapeDtypeStruct((laid_rows, BC), jnp.float32),)
        + tuple(jax.ShapeDtypeStruct((others * size, BC), jnp.bfloat16) for size in sizes)
        + (row_products, jax.ShapeDtypeStruct((row_blocks, half, 2 * BS), jnp.bfloat16)),
        in_specs=[smem] + [vmem] * (2 + len(all_pieces)),
        out_specs=(vmem,) * (3 + len(SPLIT)),
        scratch_shapes=scratch + [pltpu.VMEM((others * laid_rows, BC), jnp.float32)],
        compiler_params=pltpu.CompilerParams(vmem_limit_bytes=28 * MIB),
        cost_estimate=pl.CostEstimate(
            flops=products // 2, bytes_accessed=8 * MIB, transcendentals=0
        ),
        name="last_products",
    )(ancestors[0], here, *early, *all_pieces)
    diag_keep, diag_send = pl.pallas_call(
        functools.partial(diag_kernel, poles, rows, cols, row_blocks),
        out_shape=(
            jax.ShapeDtypeStruct((rows, part + BR, wide), jnp.float32),
            jax.ShapeDtypeStruct((others, rows, part + BR, wide), jnp.bfloat16),
        ),
        in_specs=[smem] * 4 + [vmem] * 2,
        out_specs=(vmem,) * 2,
        scratch_shapes=[
            pltpu.VMEM((half, wide), jnp.float32),
            pltpu.VMEM((half // BC, tile_count, BR, BC), jnp.float32),
        ],
        compiler_params=pltpu.CompilerParams(vmem_limit_bytes=20 * MIB),
        cost_estimate=pl.CostEstimate(
            flops=products // 2, bytes_accessed=8 * MIB, transcendentals=0
        ),
        name="diag_products",
    )(ancestors[0], weight_table, pole_slot, jnp.concatenate(late_owners), total, turned)

    everyone_pairs = [shift_pairs(rows, cols, step, everyone) for step in range(cols)]
    arrived = [
        lax.ppermute(diag_send[step - 1], grid, everyone_pairs[step])
        for step in range(1, cols)
    ]
    *rounded, own = pl.pallas_call(
        functools.partial(regroup_kernel, poles, rows),
        out_shape=(jax.ShapeDtypeStruct((part + BR, wide), jnp.bfloat16),) * (rows - 1)
        + (jax.ShapeDtypeStruct((part + BR, wide), jnp.float32),),
        in_specs=[vmem] * (1 + len(arrived)),
        out_specs=(vmem,) * rows,
        compiler_params=pltpu.CompilerParams(vmem_limit_bytes=16 * MIB),
        name="regroup",
    )(diag_keep, *arrived)
    parts = [
        lax.ppermute(rounded[step - 1], "row", [(i, (i + step) % rows) for i in range(rows)])
        for step in range(1, rows)
    ]
    laid_diag, message = pl.pallas_call(
        functools.partial(finish_kernel, poles),
        out_shape=(
            jax.ShapeDtypeStruct((part * 2 * across, BC), jnp.float32),
            jax.ShapeDtypeStruct((part * across + poles * BR, BC), jnp.float32),
        ),
        in_specs=[smem] * 2 + [vmem] * (2 + len(parts)),
        out_specs=(vmem,) * 2,
        compiler_params=pltpu.CompilerParams(vmem_limit_bytes=8 * MIB),
        name="finish",
    )(weight_table, pole_slot, laid(dinv), own, *parts)
    diag_inverse = plain(laid_diag, dinv.shape)
    messages = [message]
    for step in range(1, poles):
        messages.append(lax.ppermute(message, "pole", [(i, i ^ step) for i in range(poles)]))

    split = part * across
    laid_density, tile_sum = pl.pallas_call(
        functools.partial(density_kernel, split),
        out_shape=(
            jax.ShapeDtypeStruct((split, BC), jnp.float32),
            jax.ShapeDtypeStruct((1, BR, BC), jnp.float32),
        ),
        in_specs=[vmem] * poles,
        out_specs=(vmem,) * 2,
        compiler_params=pltpu.CompilerParams(vmem_limit_bytes=8 * MIB),
        name="density",
    )(*messages)
    density_diag = laid_density.reshape(part, 1, half)

    parts = []
    for send, size in zip(sends, sizes):
        parts += [
            lax.ppermute(send[(step - 1) * size : step * size], grid, everyone_pairs[step])
            for step in range(1, cols)
        ]
    block = laid_rows // sum(SPLIT)
    specs = [pl.BlockSpec((block, BC), lambda i: (i, 0))]
    first = 0
    for share in SPLIT:
        spec = pl.BlockSpec(
            (block, BC), lambda i, f=first, n=share: (jnp.clip(i - f, 0, n - 1), 0)
        )
        specs += [spec] * (cols - 1)
        first += share
    column = pl.pallas_call(
        functools.partial(join_kernel, cols - 1),
        grid=(sum(SPLIT),),
        out_shape=jax.ShapeDtypeStruct((laid_rows, BC), jnp.float32),
        in_specs=specs,
        out_specs=pl.BlockSpec((block, BC), lambda i: (i, 0)),
        compiler_params=pltpu.CompilerParams(vmem_limit_bytes=16 * MIB),
        name="join_columns",
    )(keep, *parts)
    column_out = plain(column, (rows_here, 1, 1, 2, half))
    return (column_out, diag_inverse, density_diag, tile_sum)


def solution(mesh):
    in_specs = (
        P("pole", None, "row", "col"),
        P("pole", None, ("row", "col"), None),
        P(("row", "col"), "pole", None, None, None),
        P(),
        P(("row", "col"), None),
        P(),
        P("pole"),
    )
    out_specs = (
        P(("row", "col"), "pole", None, None, None),
        P(("row", "col"), "pole", None, None, None),
        P(("row", "col"), None, None),
        P(("pole", "row", "col"), None, None),
    )
    return jax.shard_map(compute, mesh=mesh, in_specs=in_specs, out_specs=out_specs, check_vma=False)
```

```python
import functools

import jax
import jax.numpy as jnp
from jax import lax
from jax.experimental import pallas as pl
from jax.experimental.pallas import tpu as pltpu
from jax.sharding import PartitionSpec as P


BS = 128
BR = 8
BC = 128
MIB = 1 << 20
SPLIT = (4,)


def shift_pairs(rows, cols, step, valid):
    return [
        (r * cols + c, r * cols + (c + step) % cols)
        for r in range(rows)
        if valid(r)
        for c in range(cols)
    ]


def gather_stages(shard, rows, cols):
    grid = ("row", "col")
    if rows != 4:
        full = lax.all_gather(shard, grid, axis=0, tiled=True).reshape((rows, cols) + shard.shape)
        c = lax.axis_index("col")
        stages = []
        for row in range(rows):
            line = [lax.dynamic_index_in_dim(full[row], (c - step) % cols, 0, False) for step in range(cols)]
            stages.append([[piece] for piece in line])
        return stages, [[row] * rows for row in range(rows)]
    sources = [[0, 1, 2, 3], [1, 0, 3, 2], [2, 2, 1, 1], [3, 3, 0, 0]]
    outer = [(0, 1), (1, 0), (2, 3), (3, 2)]
    inner = [(1, 2), (2, 1)]
    r = lax.axis_index("row")
    middle = jnp.logical_or(r == 1, r == 2)
    height = shard.shape[0] // 2
    stages = [[[] for _ in range(cols)] for _ in range(rows)]
    for part in (0, 1):
        own = shard[part * height : (part + 1) * height]

        def hop(value, pairs):
            return lax.ppermute(value, "row", pairs)

        near = hop(own, outer)
        cross = hop(own, inner)
        cross_out = hop(cross, outer)
        far = hop(near, inner)
        far_out = hop(far, outer)
        line = [
            lambda: own,
            lambda: near,
            lambda: jnp.where(middle, cross, cross_out),
            lambda: jnp.where(middle, far, far_out),
        ]
        last = None
        opened = []
        for stage, make in enumerate(line):
            piece = make()
            stages[stage][0].append(piece)
            leaving = piece
            if last is not None and stage < rows - 1:
                leaving, _ = lax.optimization_barrier((piece, last))
            for step in range(1, cols):
                if stage == 1 and part == 1:
                    relayed, _ = lax.optimization_barrier((opened[step - 1], far_out))
                    stages[stage][step].append(lax.ppermute(relayed, "row", outer))
                    continue
                pairs = shift_pairs(rows, cols, step, lambda r: True)
                last = lax.ppermute(leaving, grid, pairs)
                stages[stage][step].append(last)
                if stage == 0:
                    opened.append(last)
    return stages, sources


def counts_of(ancestors, inverse, rows, cols):
    row_blocks, col_blocks = inverse.shape[1] // BS, inverse.shape[2] // BS
    r = lax.axis_index("row")
    c = lax.axis_index("col")

    def below(limit):
        total = jnp.int32(0)
        for i in range(ancestors.shape[0]):
            total = total + (ancestors[i] < limit).astype(jnp.int32)
        return total

    row_first, row_last = below(r * row_blocks), below((r + 1) * row_blocks)
    col_first, col_last = below(c * col_blocks), below((c + 1) * col_blocks)
    count = row_last - row_first
    return rows, cols, row_blocks, col_blocks, row_first, count, col_first, col_last


def source_row(sources, stage):
    r = lax.axis_index("row")
    total = jnp.int32(0)
    for row, source in enumerate(sources[stage]):
        total = total + jnp.where(r == row, source, 0)
    return total


def fill(full, pieces, sources, stage, cols):
    c = lax.axis_index("col")
    source = source_row(sources, stage)
    chunks = len(pieces) // cols
    height = pieces[0].shape[0]
    for step in range(cols):
        shard = source * cols + lax.rem(c - step + cols, cols)
        for chunk in range(chunks):
            start = pl.multiple_of((shard * chunks + chunk) * height, height)
            full[pl.ds(start, height), :] = pieces[step * chunks + chunk][...]


def multiply(acc, inverse, full, ancestors, counts, pair, source):
    rows, _, row_blocks, col_blocks = counts[:4]
    row_first, row_count, col_first, col_last = counts[4:]
    stage_blocks = ancestors.shape[0] // rows
    low = source * stage_blocks
    r = lax.axis_index("row")
    c = lax.axis_index("col")

    start = jnp.maximum(low, col_first)
    width = jnp.minimum(low + stage_blocks, col_last) - start

    def add(first, blocks):
        left = []
        for n in range(blocks):
            k = first + n
            inside = jnp.logical_and(k >= col_first, k < col_last)
            block = jnp.where(inside, ancestors[k] - c * col_blocks, 0)
            column = pl.ds(pl.multiple_of(block * BS, BS), BS)
            both = []
            for i in range(2):
                listed = ancestors[row_first + jnp.minimum(2 * pair + i, row_count - 1)]
                row = pl.multiple_of((listed - r * row_blocks) * BS, BS)
                both.append(inverse[:, pl.ds(row, BS), column].reshape(2 * BS, BS))
            value = jnp.concatenate(both, axis=0)
            left.append(value * inside.astype(value.dtype))
        place = pl.ds(pl.multiple_of(first * BS, BS), blocks * BS)
        acc[...] += jnp.dot(
            jnp.concatenate(left, axis=1), full[place, :], preferred_element_type=jnp.float32
        )

    few = stage_blocks // 2

    @pl.when(width > few)
    def _():
        add(low, stage_blocks)

    @pl.when(jnp.logical_and(width > 0, width <= few))
    def _():
        add(jnp.minimum(start, low + stage_blocks - few), few)


def combine(acc, n):
    half = acc.shape[1] // 2
    upper, lower = acc.at[2 * n * BS : (2 * n + 1) * BS], acc.at[(2 * n + 1) * BS : (2 * n + 2) * BS]
    return upper[:, :half] - lower[:, half:], upper[:, half:] + lower[:, :half]


def add_products(sources, stages, ancestors, inverse, before, full, acc, counts, store):
    row_count = counts[5]

    @pl.loop(0, (row_count + 1) // 2)
    def _(pair):
        if before is None:
            acc[...] = jnp.zeros_like(acc)
        else:
            for n in range(2):
                i = jnp.minimum(2 * pair + n, row_count - 1)
                acc[2 * n * BS : (2 * n + 1) * BS, :] = before[i]
                acc[(2 * n + 1) * BS : (2 * n + 2) * BS, :] = jnp.zeros((BS, acc.shape[1]), acc.dtype)
        for stage in stages:
            multiply(acc, inverse, full, ancestors, counts, pair, source_row(sources, stage))
        for n in range(2):

            @pl.when(2 * pair + n < row_count)
            def _():
                store(2 * pair + n, *combine(acc, n))


def list_kernel(ancestors, out):
    for i in range(ancestors.shape[0]):
        out[i] = ancestors[i]


def early_kernel(sources, stages, added, rows, cols, ancestors, inverse, *refs):
    early, turned, full, acc = refs[-4:]
    before = refs[0] if added else None
    pieces = refs[1 if added else 0 : -4]
    each = len(pieces) // len(stages)
    half = acc.shape[1] // 2
    for n, stage in enumerate(stages):
        fill(full, pieces[n * each : (n + 1) * each], sources, stage, cols)
    counts = counts_of(ancestors, inverse, rows, cols)

    def store(i, real, imag):
        early[i, :, :half] = real
        early[i, :, half:] = imag

    add_products(sources, stages, ancestors, inverse, before, full, acc, counts, store)
    turn_blocks(sources, stages, ancestors, full, counts, turned)


def brought(sources, stages, rows, selected, block):
    stage_blocks = selected // rows
    found = False
    for stage in stages:
        low = source_row(sources, stage) * stage_blocks
        found = jnp.logical_or(found, jnp.logical_and(block >= low, block < low + stage_blocks))
    return found


def turn_blocks(sources, stages, ancestors, full, counts, turned):
    half = full.shape[1] // 2
    rows, row_first, row_count = counts[0], counts[4], counts[5]

    @pl.loop(0, row_count)
    def _(i):
        block = row_first + i

        @pl.when(brought(sources, stages, rows, ancestors.shape[0], block))
        def _():
            rows_of = full[pl.ds(pl.multiple_of(block * BS, BS), BS), :]
            left = jnp.concatenate([rows_of[:, :half], rows_of[:, half:]], axis=0)
            turned[i] = left.T


def last_kernel(sources, stages, rows, cols, ancestors, inverse, early, *refs):
    keep, *sends, total, turned, full, acc, leaving = refs[-(6 + len(SPLIT)) :]
    pieces = refs[: -(6 + len(SPLIT))]
    each = len(pieces) // len(stages)
    half = acc.shape[1] // 2
    across = half // BC
    row_blocks = early.shape[0]
    own_blocks = row_blocks // cols
    r = lax.axis_index("row")
    c = lax.axis_index("col")
    for n, stage in enumerate(stages):
        fill(full, pieces[n * each : (n + 1) * each], sources, stage, cols)
    counts = counts_of(ancestors, inverse, rows, cols)
    row_first = counts[4]
    size = BS * 2 * across

    for n in range(row_blocks):
        listed = False
        for k in range(ancestors.shape[0]):
            listed = jnp.logical_or(listed, ancestors[k] == r * row_blocks + n)
        turn = lax.rem(n // own_blocks - c + cols, cols)
        within = n % own_blocks * size

        @pl.when(jnp.logical_and(jnp.logical_not(listed), turn == 0))
        def _():
            keep[within : within + size, :] = jnp.zeros((size, BC), jnp.float32)

        @pl.when(jnp.logical_and(jnp.logical_not(listed), turn > 0))
        def _():
            start = pl.multiple_of((turn - 1) * keep.shape[0] + within, size)
            leaving[pl.ds(start, size), :] = jnp.zeros((size, BC), jnp.float32)


    def store(i, real, imag):
        total[i, :, :half] = real
        total[i, :, half:] = imag
        block = ancestors[row_first + i] - r * row_blocks
        within = lax.rem(block, own_blocks) * (BS * 2 * across)
        turn = lax.rem(block // own_blocks - c + cols, cols)

        def lay(target, start):
            for j in range(across):
                for n, value in enumerate((real, imag)):
                    rows_of = pl.ds(start + 2 * j + n, BS, stride=2 * across)
                    target[rows_of, :] = -value[:, j * BC : (j + 1) * BC]

        @pl.when(turn == 0)
        def _():
            lay(keep, within)

        @pl.when(turn > 0)
        def _():
            lay(leaving, (turn - 1) * keep.shape[0] + within)

    add_products(sources, stages, ancestors, inverse, early, full, acc, counts, store)
    turn_blocks(sources, stages, ancestors, full, counts, turned)
    height = keep.shape[0]
    for step in range(cols - 1):
        first = 0
        for send, share in zip(sends, SPLIT):
            size = height * share // sum(SPLIT)
            value = leaving[step * height + first : step * height + first + size, :]
            send[step * size : (step + 1) * size, :] = value.astype(send.dtype)
            first += size


def diag_kernel(
    sources, first_stages, poles, rows, cols, row_blocks, ancestors, table, slot, owner, *refs
):
    total, first_turned, turned, diag_keep, diag_send, diag, tiles = refs
    half, wide = diag.shape
    across = half // BC
    own_blocks = row_blocks // cols
    r = lax.axis_index("row")
    c = lax.axis_index("col")

    def below(limit):
        count = jnp.int32(0)
        for i in range(ancestors.shape[0]):
            count = count + (ancestors[i] < limit).astype(jnp.int32)
        return count

    row_first = below(r * row_blocks)
    diag[...] = jnp.zeros_like(diag)
    tiles[...] = jnp.zeros_like(tiles)
    weight_real = table[0, slot[0]]
    weight_imag = table[1, slot[0]]

    row_count = below((r + 1) * row_blocks) - row_first

    def operands(i):
        real = total[i, :, :half]
        imag = total[i, :, half:]
        first = brought(sources, first_stages, rows, ancestors.shape[0], row_first + i)

        @pl.when(first)
        def _():
            turned[i] = first_turned[i]

        left = turned[i]
        real_high = real.astype(jnp.bfloat16)
        imag_high = imag.astype(jnp.bfloat16)
        real_low = (real - real_high.astype(jnp.float32)).astype(jnp.bfloat16)
        imag_low = (imag - imag_high.astype(jnp.float32)).astype(jnp.bfloat16)
        right = [
            jnp.concatenate([real_high, imag_high], axis=1),
            jnp.concatenate([-imag_high, real_high], axis=1),
            jnp.concatenate([real_low, imag_low], axis=1),
            jnp.concatenate([-imag_low, real_low], axis=1),
        ]
        block = ancestors[row_first + i] - r * row_blocks
        place = block // own_blocks
        mixed = -(weight_real * imag + weight_imag * real)
        per_device = own_blocks * (BS // BR) * across
        start = lax.rem(c - place + cols, cols) * per_device + lax.rem(block, own_blocks) * (
            BS // BR
        ) * across
        for group in range(BS // BR):
            for j in range(across):
                tile = owner[start + group * across + j]
                tiles[j, tile] += mixed[group * BR : (group + 1) * BR, j * BC : (j + 1) * BC]
        return [left, left], right

    def add(blocks):
        left, right = [], []
        for i in blocks:
            more_left, more_right = operands(i)
            left += more_left
            right += more_right
        diag[...] += jnp.dot(
            jnp.concatenate(left, axis=1),
            jnp.concatenate(right, axis=0),
            preferred_element_type=jnp.float32,
        )

    @pl.loop(0, row_count // 2)
    def _(pair):
        add([2 * pair, 2 * pair + 1])

    @pl.when(lax.rem(row_count, 2) == 1)
    def _():
        add([row_count - 1])

    part = half // (rows * cols)
    for row in range(rows):
        for step in range(cols):
            place = row * cols + lax.rem(c + step, cols)
            value = diag[pl.ds(pl.multiple_of(place * part, part), part), :]
            if step == 0:
                diag_keep[row, :part] = value
                diag_keep[row, part:] = jnp.zeros((BR, wide), jnp.float32)
            else:
                diag_send[step - 1, row, :part] = value.astype(diag_send.dtype)
                diag_send[step - 1, row, part:] = jnp.zeros((BR, wide), diag_send.dtype)
            for pole in range(poles):
                sum_of = tiles[0, pole * rows * cols + place]
                for j in range(1, across):
                    sum_of = sum_of + tiles[j, pole * rows * cols + place]
                if step == 0:
                    diag_keep[row, part:, 2 * pole * BC : (2 * pole + 1) * BC] = sum_of
                else:
                    diag_send[step - 1, row, part:, 2 * pole * BC : 2 * (pole + 1) * BC] = halves(sum_of)


def density_kernel(split, *refs):
    *messages, density, tile = refs
    start = pl.multiple_of(split + lax.axis_index("pole") * BR, BR)
    for place, out in ((pl.ds(0, split), density.at[...]), (pl.ds(start, BR), tile.at[0])):
        values = [message[place, :] for message in messages]
        while len(values) > 1:
            values = [a + b for a, b in zip(values[::2], values[1::2])]
        out[...] = values[0]


def join_kernel(steps, keep, *refs):
    out = refs[-1]
    block = pl.program_id(0)
    first = 0
    for n, share in enumerate(SPLIT):
        arrived = refs[n * steps : (n + 1) * steps]

        @pl.when(jnp.logical_and(block >= first, block < first + share))
        def _():
            value = keep[...]
            for ref in arrived:
                value = value + ref[...].astype(jnp.float32)
            out[...] = value

        first += share


def halves(value):
    high = value.astype(jnp.bfloat16)
    low = (value - high.astype(jnp.float32)).astype(jnp.bfloat16)
    return jnp.concatenate([high, low], axis=1)


def regroup_kernel(poles, rows, kept, *refs):
    *rounded, own = refs[-rows:]
    arrived = refs[:-rows]
    part = own.shape[0] - BR
    r = lax.axis_index("row")

    def total(row):
        value = kept[row]
        for ref in arrived:
            value = value + ref[row].astype(jnp.float32)
        return value

    own[...] = total(r)
    for step in range(1, rows):
        value = total(lax.rem(r + step, rows))
        out = rounded[step - 1]
        out[:part] = value[:part].astype(out.dtype)
        for pole in range(poles):
            first = 2 * pole * BC
            band = value[part:, first : first + BC] + value[part:, first + BC : first + 2 * BC]
            out[part:, first : first + 2 * BC] = halves(band)


def finish_kernel(poles, table, slot, laid_dinv, own, *refs):
    diag_out, message = refs[-2:]
    arrived = refs[:-2]
    part, wide = own.shape[0] - BR, own.shape[1]
    across = wide // (2 * BC)
    total = own[...]
    for ref in arrived:
        total = total + ref[...].astype(jnp.float32)
    weight_real = table[0, slot[0]]
    weight_imag = table[1, slot[0]]
    for j in range(across):
        values = []
        for n in range(2):
            rows_of = pl.ds(2 * j + n, part, stride=2 * across)
            first = (n * across + j) * BC
            values.append(laid_dinv[rows_of, :] + total[:part, first : first + BC])
            diag_out[rows_of, :] = values[n]
        share = weight_real * values[1] + weight_imag * values[0]
        message[pl.ds(j, part, stride=across), :] = share
    for pole in range(poles):
        first = 2 * pole * BC
        band = total[part:, first : first + BC] + total[part:, first + BC : first + 2 * BC]
        start = part * across + pole * BR
        message[start : start + BR] = band


def compute(inverse, factor, dinv, ancestors, owner, weight_table, pole_slot):
    rows = lax.axis_size("row")
    cols = lax.axis_size("col")
    poles = lax.axis_size("pole")
    grid = ("row", "col")
    tile_count = poles * rows * cols
    here = inverse[0]
    wide = factor.shape[3]
    half = wide // 2
    rows_here = here.shape[1] // cols
    row_blocks = here.shape[1] // BS
    selected = ancestors.shape[1]
    part = half // (rows * cols)
    everyone = lambda r: True

    owners = [owner[:, 0]]
    for step in range(1, cols):
        pairs = shift_pairs(rows, cols, step, everyone)
        owners.append(lax.ppermute(owner[:, 0], grid, pairs))
    smem = pl.BlockSpec(memory_space=pltpu.SMEM)
    vmem = pl.BlockSpec(memory_space=pltpu.VMEM)
    whole = pl.BlockSpec(memory_space=pl.ANY)
    across = half // BC

    def laid(value):
        value = value.reshape(-1, 2, across, BC).transpose(0, 2, 1, 3)
        return value.reshape(-1, BC)

    def plain(value, shape):
        value = value.reshape(-1, across, 2, BC).transpose(0, 2, 1, 3)
        return value.reshape(shape)

    stages, sources = gather_stages(factor[0, 0], rows, cols)
    stages = [[chunk for step in stage for chunk in step] for stage in stages]
    products = 2 * row_blocks * BS * 2 * wide * selected * BS // cols
    scratch = [
        pltpu.VMEM((selected * BS, wide), jnp.bfloat16),
        pltpu.VMEM((4 * BS, wide), jnp.float32),
    ]
    row_products = jax.ShapeDtypeStruct((row_blocks, BS, wide), jnp.float32)
    groups = [(0, rows - 2)] if rows > 2 else [(0,)]
    last = tuple(stage for stage in range(rows) if stage not in groups[0])
    listing = pl.pallas_call(
        list_kernel,
        out_shape=jax.ShapeDtypeStruct((selected,), jnp.int32),
        in_specs=[smem],
        out_specs=smem,
        compiler_params=pltpu.CompilerParams(vmem_limit_bytes=MIB),
        cost_estimate=pl.CostEstimate(
            flops=products // 3, bytes_accessed=0, transcendentals=0
        ),
        name="list_blocks",
    )(ancestors[0])
    turned_blocks = jax.ShapeDtypeStruct((row_blocks, half, 2 * BS), jnp.bfloat16)
    early_pieces = [piece for stage in groups[0] for piece in stages[stage]]
    early, first_turned = pl.pallas_call(
        functools.partial(early_kernel, sources, groups[0], False, rows, cols),
        out_shape=(row_products, turned_blocks),
        in_specs=[smem, vmem] + [vmem] * len(early_pieces),
        out_specs=(vmem,) * 2,
        scratch_shapes=scratch,
        compiler_params=pltpu.CompilerParams(vmem_limit_bytes=24 * MIB),
        cost_estimate=pl.CostEstimate(
            flops=products // 2, bytes_accessed=4 * MIB, transcendentals=0
        ),
        name="early_products",
    )(listing, here, *early_pieces)
    late_owners, _ = lax.optimization_barrier((tuple(owners), early))
    all_pieces = [piece for stage in last for piece in stages[stage]]
    others = max(1, cols - 1)
    laid_rows = rows_here * wide // BC
    sizes = [laid_rows * share // sum(SPLIT) for share in SPLIT]
    keep, *sends, total, turned = pl.pallas_call(
        functools.partial(last_kernel, sources, last, rows, cols),
        out_shape=(jax.ShapeDtypeStruct((laid_rows, BC), jnp.float32),)
        + tuple(jax.ShapeDtypeStruct((others * size, BC), jnp.bfloat16) for size in sizes)
        + (row_products, turned_blocks),
        in_specs=[smem] + [vmem] * (2 + len(all_pieces)),
        out_specs=(vmem,) * (3 + len(SPLIT)),
        scratch_shapes=scratch + [pltpu.VMEM((others * laid_rows, BC), jnp.float32)],
        compiler_params=pltpu.CompilerParams(vmem_limit_bytes=28 * MIB),
        cost_estimate=pl.CostEstimate(
            flops=products // 2, bytes_accessed=8 * MIB, transcendentals=0
        ),
        name="last_products",
    )(ancestors[0], here, early, *all_pieces)
    diag_keep, diag_send = pl.pallas_call(
        functools.partial(diag_kernel, sources, groups[0], poles, rows, cols, row_blocks),
        out_shape=(
            jax.ShapeDtypeStruct((rows, part + BR, wide), jnp.float32),
            jax.ShapeDtypeStruct((others, rows, part + BR, wide), jnp.bfloat16),
        ),
        in_specs=[smem] * 4 + [vmem] * 3,
        out_specs=(vmem,) * 2,
        scratch_shapes=[
            pltpu.VMEM((half, wide), jnp.float32),
            pltpu.VMEM((half // BC, tile_count, BR, BC), jnp.float32),
        ],
        compiler_params=pltpu.CompilerParams(vmem_limit_bytes=20 * MIB),
        cost_estimate=pl.CostEstimate(
            flops=products // 2, bytes_accessed=8 * MIB, transcendentals=0
        ),
        name="diag_products",
    )(ancestors[0], weight_table, pole_slot, jnp.concatenate(late_owners), total, first_turned, turned)

    everyone_pairs = [shift_pairs(rows, cols, step, everyone) for step in range(cols)]
    arrived = [
        lax.ppermute(diag_send[step - 1], grid, everyone_pairs[step])
        for step in range(1, cols)
    ]
    *rounded, own = pl.pallas_call(
        functools.partial(regroup_kernel, poles, rows),
        out_shape=(jax.ShapeDtypeStruct((part + BR, wide), jnp.bfloat16),) * (rows - 1)
        + (jax.ShapeDtypeStruct((part + BR, wide), jnp.float32),),
        in_specs=[vmem] * (1 + len(arrived)),
        out_specs=(vmem,) * rows,
        compiler_params=pltpu.CompilerParams(vmem_limit_bytes=16 * MIB),
        name="regroup",
    )(diag_keep, *arrived)
    parts = [
        lax.ppermute(rounded[step - 1], "row", [(i, (i + step) % rows) for i in range(rows)])
        for step in range(1, rows)
    ]
    laid_diag, message = pl.pallas_call(
        functools.partial(finish_kernel, poles),
        out_shape=(
            jax.ShapeDtypeStruct((part * 2 * across, BC), jnp.float32),
            jax.ShapeDtypeStruct((part * across + poles * BR, BC), jnp.float32),
        ),
        in_specs=[smem] * 2 + [vmem] * (2 + len(parts)),
        out_specs=(vmem,) * 2,
        compiler_params=pltpu.CompilerParams(vmem_limit_bytes=8 * MIB),
        name="finish",
    )(weight_table, pole_slot, laid(dinv), own, *parts)
    diag_inverse = plain(laid_diag, dinv.shape)
    messages = [message]
    for step in range(1, poles):
        messages.append(lax.ppermute(message, "pole", [(i, i ^ step) for i in range(poles)]))

    split = part * across
    laid_density, tile_sum = pl.pallas_call(
        functools.partial(density_kernel, split),
        out_shape=(
            jax.ShapeDtypeStruct((split, BC), jnp.float32),
            jax.ShapeDtypeStruct((1, BR, BC), jnp.float32),
        ),
        in_specs=[vmem] * poles,
        out_specs=(vmem,) * 2,
        compiler_params=pltpu.CompilerParams(vmem_limit_bytes=8 * MIB),
        name="density",
    )(*messages)
    density_diag = laid_density.reshape(part, 1, half)

    parts = []
    for send, size in zip(sends, sizes):
        parts += [
            lax.ppermute(send[(step - 1) * size : step * size], grid, everyone_pairs[step])
            for step in range(1, cols)
        ]
    block = laid_rows // sum(SPLIT)
    specs = [pl.BlockSpec((block, BC), lambda i: (i, 0))]
    first = 0
    for share in SPLIT:
        spec = pl.BlockSpec(
            (block, BC), lambda i, f=first, n=share: (jnp.clip(i - f, 0, n - 1), 0)
        )
        specs += [spec] * (cols - 1)
        first += share
    column = pl.pallas_call(
        functools.partial(join_kernel, cols - 1),
        grid=(sum(SPLIT),),
        out_shape=jax.ShapeDtypeStruct((laid_rows, BC), jnp.float32),
        in_specs=specs,
        out_specs=pl.BlockSpec((block, BC), lambda i: (i, 0)),
        compiler_params=pltpu.CompilerParams(vmem_limit_bytes=16 * MIB),
        name="join_columns",
    )(keep, *parts)
    column_out = plain(column, (rows_here, 1, 1, 2, half))
    return (column_out, diag_inverse, density_diag, tile_sum)


def solution(mesh):
    in_specs = (
        P("pole", None, "row", "col"),
        P("pole", None, ("row", "col"), None),
        P(("row", "col"), "pole", None, None, None),
        P(),
        P(("row", "col"), None),
        P(),
        P("pole"),
    )
    out_specs = (
        P(("row", "col"), "pole", None, None, None),
        P(("row", "col"), "pole", None, None, None),
        P(("row", "col"), None, None),
        P(("pole", "row", "col"), None, None),
    )
    return jax.shard_map(compute, mesh=mesh, in_specs=in_specs, out_specs=out_specs, check_vma=False)
```

```python
import functools

import jax
import jax.numpy as jnp
from jax import lax
from jax.experimental import pallas as pl
from jax.experimental.pallas import tpu as pltpu
from jax.sharding import PartitionSpec as P


BS = 128
BR = 8
BC = 128
MIB = 1 << 20
SPLIT = (4,)


def shift_pairs(rows, cols, step, valid):
    return [
        (r * cols + c, r * cols + (c + step) % cols)
        for r in range(rows)
        if valid(r)
        for c in range(cols)
    ]


def gather_stages(shard, rows, cols):
    grid = ("row", "col")
    if rows != 4:
        full = lax.all_gather(shard, grid, axis=0, tiled=True).reshape((rows, cols) + shard.shape)
        c = lax.axis_index("col")
        stages = []
        for row in range(rows):
            line = [lax.dynamic_index_in_dim(full[row], (c - step) % cols, 0, False) for step in range(cols)]
            stages.append([[piece] for piece in line])
        return stages, [[row] * rows for row in range(rows)]
    sources = [[0, 1, 2, 3], [1, 0, 3, 2], [2, 2, 1, 1], [3, 3, 0, 0]]
    outer = [(0, 1), (1, 0), (2, 3), (3, 2)]
    inner = [(1, 2), (2, 1)]
    r = lax.axis_index("row")
    middle = jnp.logical_or(r == 1, r == 2)
    height = shard.shape[0] // 2
    stages = [[[] for _ in range(cols)] for _ in range(rows)]
    for part in (0, 1):
        own = shard[part * height : (part + 1) * height]

        def hop(value, pairs):
            return lax.ppermute(value, "row", pairs)

        near = hop(own, outer)
        cross = hop(own, inner)
        cross_out = hop(cross, outer)
        far = hop(near, inner)
        far_out = hop(far, outer)
        line = [
            lambda: own,
            lambda: near,
            lambda: jnp.where(middle, cross, cross_out),
            lambda: jnp.where(middle, far, far_out),
        ]
        last = None
        opened = []
        for stage, make in enumerate(line):
            piece = make()
            stages[stage][0].append(piece)
            leaving = piece
            if last is not None and stage < rows - 1:
                leaving, _ = lax.optimization_barrier((piece, last))
            for step in range(1, cols):
                if stage == 1 and part == 1:
                    relayed, _ = lax.optimization_barrier((opened[step - 1], far_out))
                    stages[stage][step].append(lax.ppermute(relayed, "row", outer))
                    continue
                pairs = shift_pairs(rows, cols, step, lambda r: True)
                last = lax.ppermute(leaving, grid, pairs)
                stages[stage][step].append(last)
                if stage == 0:
                    opened.append(last)
    return stages, sources


def counts_of(ancestors, inverse, rows, cols):
    row_blocks, col_blocks = inverse.shape[1] // BS, inverse.shape[2] // BS
    r = lax.axis_index("row")
    c = lax.axis_index("col")

    def below(limit):
        total = jnp.int32(0)
        for i in range(ancestors.shape[0]):
            total = total + (ancestors[i] < limit).astype(jnp.int32)
        return total

    row_first, row_last = below(r * row_blocks), below((r + 1) * row_blocks)
    col_first, col_last = below(c * col_blocks), below((c + 1) * col_blocks)
    count = row_last - row_first
    return rows, cols, row_blocks, col_blocks, row_first, count, col_first, col_last


def source_row(sources, stage):
    r = lax.axis_index("row")
    total = jnp.int32(0)
    for row, source in enumerate(sources[stage]):
        total = total + jnp.where(r == row, source, 0)
    return total


def fill(full, pieces, sources, stage, cols):
    c = lax.axis_index("col")
    source = source_row(sources, stage)
    chunks = len(pieces) // cols
    height = pieces[0].shape[0]
    for step in range(cols):
        shard = source * cols + lax.rem(c - step + cols, cols)
        for chunk in range(chunks):
            start = pl.multiple_of((shard * chunks + chunk) * height, height)
            full[pl.ds(start, height), :] = pieces[step * chunks + chunk][...]


def multiply(acc, inverse, full, ancestors, counts, pair, source):
    rows, _, row_blocks, col_blocks = counts[:4]
    row_first, row_count, col_first, col_last = counts[4:]
    stage_blocks = ancestors.shape[0] // rows
    low = source * stage_blocks
    r = lax.axis_index("row")
    c = lax.axis_index("col")

    start = jnp.maximum(low, col_first)
    width = jnp.minimum(low + stage_blocks, col_last) - start

    def add(first, blocks):
        left = []
        for n in range(blocks):
            k = first + n
            inside = jnp.logical_and(k >= col_first, k < col_last)
            block = jnp.where(inside, ancestors[k] - c * col_blocks, 0)
            column = pl.ds(pl.multiple_of(block * BS, BS), BS)
            both = []
            for i in range(2):
                listed = ancestors[row_first + jnp.minimum(2 * pair + i, row_count - 1)]
                row = pl.multiple_of((listed - r * row_blocks) * BS, BS)
                both.append(inverse[:, pl.ds(row, BS), column].reshape(2 * BS, BS))
            value = jnp.concatenate(both, axis=0)
            left.append(value * inside.astype(value.dtype))
        place = pl.ds(pl.multiple_of(first * BS, BS), blocks * BS)
        acc[...] += jnp.dot(
            jnp.concatenate(left, axis=1), full[place, :], preferred_element_type=jnp.float32
        )

    few = stage_blocks // 2

    @pl.when(width > few)
    def _():
        add(low, stage_blocks)

    @pl.when(jnp.logical_and(width > 0, width <= few))
    def _():
        add(jnp.minimum(start, low + stage_blocks - few), few)


def combine(acc, n):
    half = acc.shape[1] // 2
    upper, lower = acc.at[2 * n * BS : (2 * n + 1) * BS], acc.at[(2 * n + 1) * BS : (2 * n + 2) * BS]
    return upper[:, :half] - lower[:, half:], upper[:, half:] + lower[:, :half]


def add_products(sources, stages, ancestors, inverse, before, full, acc, counts, store):
    row_count = counts[5]

    @pl.loop(0, (row_count + 1) // 2)
    def _(pair):
        if before is None:
            acc[...] = jnp.zeros_like(acc)
        else:
            for n in range(2):
                i = jnp.minimum(2 * pair + n, row_count - 1)
                acc[2 * n * BS : (2 * n + 1) * BS, :] = before[i]
                acc[(2 * n + 1) * BS : (2 * n + 2) * BS, :] = jnp.zeros((BS, acc.shape[1]), acc.dtype)
        for stage in stages:
            multiply(acc, inverse, full, ancestors, counts, pair, source_row(sources, stage))
        for n in range(2):

            @pl.when(2 * pair + n < row_count)
            def _():
                store(2 * pair + n, *combine(acc, n))


def list_kernel(ancestors, out):
    for i in range(ancestors.shape[0]):
        out[i] = ancestors[i]


def early_kernel(sources, stages, added, rows, cols, ancestors, inverse, *refs):
    early, turned, full, acc = refs[-4:]
    before = refs[0] if added else None
    pieces = refs[1 if added else 0 : -4]
    each = len(pieces) // len(stages)
    half = acc.shape[1] // 2
    for n, stage in enumerate(stages):
        fill(full, pieces[n * each : (n + 1) * each], sources, stage, cols)
    counts = counts_of(ancestors, inverse, rows, cols)

    def store(i, real, imag):
        early[i, :, :half] = real
        early[i, :, half:] = imag

    add_products(sources, stages, ancestors, inverse, before, full, acc, counts, store)
    turn_blocks(sources, stages, ancestors, full, counts, turned)


def brought(sources, stages, rows, selected, block):
    stage_blocks = selected // rows
    found = False
    for stage in stages:
        low = source_row(sources, stage) * stage_blocks
        found = jnp.logical_or(found, jnp.logical_and(block >= low, block < low + stage_blocks))
    return found


def turn_blocks(sources, stages, ancestors, full, counts, turned):
    half = full.shape[1] // 2
    rows, row_first, row_count = counts[0], counts[4], counts[5]

    @pl.loop(0, row_count)
    def _(i):
        block = row_first + i

        @pl.when(brought(sources, stages, rows, ancestors.shape[0], block))
        def _():
            rows_of = full[pl.ds(pl.multiple_of(block * BS, BS), BS), :]
            left = jnp.concatenate([rows_of[:, :half], rows_of[:, half:]], axis=0)
            turned[i] = left.T


def last_kernel(sources, stages, rows, cols, ancestors, inverse, early, *refs):
    keep, *sends, total, turned, full, acc, leaving = refs[-(6 + len(SPLIT)) :]
    pieces = refs[: -(6 + len(SPLIT))]
    each = len(pieces) // len(stages)
    half = acc.shape[1] // 2
    across = half // BC
    row_blocks = early.shape[0]
    own_blocks = row_blocks // cols
    r = lax.axis_index("row")
    c = lax.axis_index("col")
    for n, stage in enumerate(stages):
        fill(full, pieces[n * each : (n + 1) * each], sources, stage, cols)
    counts = counts_of(ancestors, inverse, rows, cols)
    row_first = counts[4]
    size = BS * 2 * across

    for n in range(row_blocks):
        listed = False
        for k in range(ancestors.shape[0]):
            listed = jnp.logical_or(listed, ancestors[k] == r * row_blocks + n)
        turn = lax.rem(n // own_blocks - c + cols, cols)
        within = n % own_blocks * size

        @pl.when(jnp.logical_and(jnp.logical_not(listed), turn == 0))
        def _():
            keep[within : within + size, :] = jnp.zeros((size, BC), jnp.float32)

        @pl.when(jnp.logical_and(jnp.logical_not(listed), turn > 0))
        def _():
            start = pl.multiple_of((turn - 1) * keep.shape[0] + within, size)
            leaving[pl.ds(start, size), :] = jnp.zeros((size, BC), jnp.float32)


    def store(i, real, imag):
        total[i, :, :half] = real
        total[i, :, half:] = imag
        block = ancestors[row_first + i] - r * row_blocks
        within = lax.rem(block, own_blocks) * (BS * 2 * across)
        turn = lax.rem(block // own_blocks - c + cols, cols)

        def lay(target, start):
            for j in range(across):
                for n, value in enumerate((real, imag)):
                    rows_of = pl.ds(start + 2 * j + n, BS, stride=2 * across)
                    target[rows_of, :] = -value[:, j * BC : (j + 1) * BC]

        @pl.when(turn == 0)
        def _():
            lay(keep, within)

        @pl.when(turn > 0)
        def _():
            lay(leaving, (turn - 1) * keep.shape[0] + within)

    add_products(sources, stages, ancestors, inverse, early, full, acc, counts, store)
    turn_blocks(sources, stages, ancestors, full, counts, turned)
    height = keep.shape[0]
    for step in range(cols - 1):
        first = 0
        for send, share in zip(sends, SPLIT):
            size = height * share // sum(SPLIT)
            value = leaving[step * height + first : step * height + first + size, :]
            send[step * size : (step + 1) * size, :] = value.astype(send.dtype)
            first += size


def diag_kernel(
    sources, first_stages, poles, rows, cols, row_blocks, ancestors, table, slot, owner, *refs
):
    total, first_turned, turned, diag_keep, diag_send, diag, tiles = refs
    half, wide = diag.shape
    across = half // BC
    own_blocks = row_blocks // cols
    r = lax.axis_index("row")
    c = lax.axis_index("col")

    def below(limit):
        count = jnp.int32(0)
        for i in range(ancestors.shape[0]):
            count = count + (ancestors[i] < limit).astype(jnp.int32)
        return count

    row_first = below(r * row_blocks)
    diag[...] = jnp.zeros_like(diag)
    tiles[...] = jnp.zeros_like(tiles)
    weight_real = table[0, slot[0]]
    weight_imag = table[1, slot[0]]

    @pl.loop(0, below((r + 1) * row_blocks) - row_first)
    def _(i):
        real = total[i, :, :half]
        imag = total[i, :, half:]
        first = brought(sources, first_stages, rows, ancestors.shape[0], row_first + i)

        @pl.when(first)
        def _():
            turned[i] = first_turned[i]

        left = turned[i]
        real_high = real.astype(jnp.bfloat16)
        imag_high = imag.astype(jnp.bfloat16)
        real_low = (real - real_high.astype(jnp.float32)).astype(jnp.bfloat16)
        imag_low = (imag - imag_high.astype(jnp.float32)).astype(jnp.bfloat16)
        right = jnp.concatenate(
            [
                jnp.concatenate([real_high, imag_high], axis=1),
                jnp.concatenate([-imag_high, real_high], axis=1),
                jnp.concatenate([real_low, imag_low], axis=1),
                jnp.concatenate([-imag_low, real_low], axis=1),
            ],
            axis=0,
        )
        diag[...] += jnp.dot(
            jnp.concatenate([left, left], axis=1), right, preferred_element_type=jnp.float32
        )
        block = ancestors[row_first + i] - r * row_blocks
        place = block // own_blocks
        mixed = -(weight_real * imag + weight_imag * real)
        per_device = own_blocks * (BS // BR) * across
        first = lax.rem(c - place + cols, cols) * per_device + lax.rem(block, own_blocks) * (
            BS // BR
        ) * across
        for group in range(BS // BR):
            for j in range(across):
                tile = owner[first + group * across + j]
                tiles[j, tile] += mixed[group * BR : (group + 1) * BR, j * BC : (j + 1) * BC]

    part = half // (rows * cols)
    for row in range(rows):
        for step in range(cols):
            place = row * cols + lax.rem(c + step, cols)
            value = diag[pl.ds(pl.multiple_of(place * part, part), part), :]
            if step == 0:
                diag_keep[row, :part] = value
                diag_keep[row, part:] = jnp.zeros((BR, wide), jnp.float32)
            else:
                diag_send[step - 1, row, :part] = value.astype(diag_send.dtype)
                diag_send[step - 1, row, part:] = jnp.zeros((BR, wide), diag_send.dtype)
            for pole in range(poles):
                sum_of = tiles[0, pole * rows * cols + place]
                for j in range(1, across):
                    sum_of = sum_of + tiles[j, pole * rows * cols + place]
                if step == 0:
                    diag_keep[row, part:, 2 * pole * BC : (2 * pole + 1) * BC] = sum_of
                else:
                    diag_send[step - 1, row, part:, 2 * pole * BC : 2 * (pole + 1) * BC] = halves(sum_of)


def density_kernel(split, *refs):
    *messages, density, tile = refs
    start = pl.multiple_of(split + lax.axis_index("pole") * BR, BR)
    for place, out in ((pl.ds(0, split), density.at[...]), (pl.ds(start, BR), tile.at[0])):
        values = [message[place, :] for message in messages]
        while len(values) > 1:
            values = [a + b for a, b in zip(values[::2], values[1::2])]
        out[...] = values[0]


def join_kernel(steps, keep, *refs):
    out = refs[-1]
    block = pl.program_id(0)
    first = 0
    for n, share in enumerate(SPLIT):
        arrived = refs[n * steps : (n + 1) * steps]

        @pl.when(jnp.logical_and(block >= first, block < first + share))
        def _():
            value = keep[...]
            for ref in arrived:
                value = value + ref[...].astype(jnp.float32)
            out[...] = value

        first += share


def halves(value):
    high = value.astype(jnp.bfloat16)
    low = (value - high.astype(jnp.float32)).astype(jnp.bfloat16)
    return jnp.concatenate([high, low], axis=1)


def regroup_kernel(poles, rows, kept, *refs):
    *rounded, own = refs[-rows:]
    arrived = refs[:-rows]
    part = own.shape[0] - BR
    r = lax.axis_index("row")

    def total(row):
        value = kept[row]
        for ref in arrived:
            value = value + ref[row].astype(jnp.float32)
        return value

    own[...] = total(r)
    for step in range(1, rows):
        value = total(lax.rem(r + step, rows))
        out = rounded[step - 1]
        out[:part] = value[:part].astype(out.dtype)
        for pole in range(poles):
            first = 2 * pole * BC
            band = value[part:, first : first + BC] + value[part:, first + BC : first + 2 * BC]
            out[part:, first : first + 2 * BC] = halves(band)


def finish_kernel(poles, table, slot, laid_dinv, own, *refs):
    diag_out, message = refs[-2:]
    arrived = refs[:-2]
    part, wide = own.shape[0] - BR, own.shape[1]
    across = wide // (2 * BC)
    total = own[...]
    for ref in arrived:
        total = total + ref[...].astype(jnp.float32)
    weight_real = table[0, slot[0]]
    weight_imag = table[1, slot[0]]
    for j in range(across):
        values = []
        for n in range(2):
            rows_of = pl.ds(2 * j + n, part, stride=2 * across)
            first = (n * across + j) * BC
            values.append(laid_dinv[rows_of, :] + total[:part, first : first + BC])
            diag_out[rows_of, :] = values[n]
        share = weight_real * values[1] + weight_imag * values[0]
        message[pl.ds(j, part, stride=across), :] = share
    for pole in range(poles):
        first = 2 * pole * BC
        band = total[part:, first : first + BC] + total[part:, first + BC : first + 2 * BC]
        start = part * across + pole * BR
        message[start : start + BR] = band


def compute(inverse, factor, dinv, ancestors, owner, weight_table, pole_slot):
    rows = lax.axis_size("row")
    cols = lax.axis_size("col")
    poles = lax.axis_size("pole")
    grid = ("row", "col")
    tile_count = poles * rows * cols
    here = inverse[0]
    wide = factor.shape[3]
    half = wide // 2
    rows_here = here.shape[1] // cols
    row_blocks = here.shape[1] // BS
    selected = ancestors.shape[1]
    part = half // (rows * cols)
    everyone = lambda r: True

    owners = [owner[:, 0]]
    for step in range(1, cols):
        pairs = shift_pairs(rows, cols, step, everyone)
        owners.append(lax.ppermute(owner[:, 0], grid, pairs))
    smem = pl.BlockSpec(memory_space=pltpu.SMEM)
    vmem = pl.BlockSpec(memory_space=pltpu.VMEM)
    whole = pl.BlockSpec(memory_space=pl.ANY)
    across = half // BC

    def laid(value):
        value = value.reshape(-1, 2, across, BC).transpose(0, 2, 1, 3)
        return value.reshape(-1, BC)

    def plain(value, shape):
        value = value.reshape(-1, across, 2, BC).transpose(0, 2, 1, 3)
        return value.reshape(shape)

    stages, sources = gather_stages(factor[0, 0], rows, cols)
    stages = [[chunk for step in stage for chunk in step] for stage in stages]
    products = 2 * row_blocks * BS * 2 * wide * selected * BS // cols
    scratch = [
        pltpu.VMEM((selected * BS, wide), jnp.bfloat16),
        pltpu.VMEM((4 * BS, wide), jnp.float32),
    ]
    row_products = jax.ShapeDtypeStruct((row_blocks, BS, wide), jnp.float32)
    groups = [(0, rows - 2)] if rows > 2 else [(0,)]
    last = tuple(stage for stage in range(rows) if stage not in groups[0])
    listing = pl.pallas_call(
        list_kernel,
        out_shape=jax.ShapeDtypeStruct((selected,), jnp.int32),
        in_specs=[smem],
        out_specs=smem,
        compiler_params=pltpu.CompilerParams(vmem_limit_bytes=MIB),
        cost_estimate=pl.CostEstimate(
            flops=products // 3, bytes_accessed=0, transcendentals=0
        ),
        name="list_blocks",
    )(ancestors[0])
    turned_blocks = jax.ShapeDtypeStruct((row_blocks, half, 2 * BS), jnp.bfloat16)
    early_pieces = [piece for stage in groups[0] for piece in stages[stage]]
    early, first_turned = pl.pallas_call(
        functools.partial(early_kernel, sources, groups[0], False, rows, cols),
        out_shape=(row_products, turned_blocks),
        in_specs=[smem, vmem] + [vmem] * len(early_pieces),
        out_specs=(vmem,) * 2,
        scratch_shapes=scratch,
        compiler_params=pltpu.CompilerParams(vmem_limit_bytes=24 * MIB),
        cost_estimate=pl.CostEstimate(
            flops=products // 2, bytes_accessed=4 * MIB, transcendentals=0
        ),
        name="early_products",
    )(listing, here, *early_pieces)
    late_owners, _ = lax.optimization_barrier((tuple(owners), early))
    all_pieces = [piece for stage in last for piece in stages[stage]]
    others = max(1, cols - 1)
    laid_rows = rows_here * wide // BC
    sizes = [laid_rows * share // sum(SPLIT) for share in SPLIT]
    keep, *sends, total, turned = pl.pallas_call(
        functools.partial(last_kernel, sources, last, rows, cols),
        out_shape=(jax.ShapeDtypeStruct((laid_rows, BC), jnp.float32),)
        + tuple(jax.ShapeDtypeStruct((others * size, BC), jnp.bfloat16) for size in sizes)
        + (row_products, turned_blocks),
        in_specs=[smem] + [vmem] * (2 + len(all_pieces)),
        out_specs=(vmem,) * (3 + len(SPLIT)),
        scratch_shapes=scratch + [pltpu.VMEM((others * laid_rows, BC), jnp.float32)],
        compiler_params=pltpu.CompilerParams(vmem_limit_bytes=28 * MIB),
        cost_estimate=pl.CostEstimate(
            flops=products // 2, bytes_accessed=8 * MIB, transcendentals=0
        ),
        name="last_products",
    )(ancestors[0], here, early, *all_pieces)
    diag_keep, diag_send = pl.pallas_call(
        functools.partial(diag_kernel, sources, groups[0], poles, rows, cols, row_blocks),
        out_shape=(
            jax.ShapeDtypeStruct((rows, part + BR, wide), jnp.float32),
            jax.ShapeDtypeStruct((others, rows, part + BR, wide), jnp.bfloat16),
        ),
        in_specs=[smem] * 4 + [vmem] * 3,
        out_specs=(vmem,) * 2,
        scratch_shapes=[
            pltpu.VMEM((half, wide), jnp.float32),
            pltpu.VMEM((half // BC, tile_count, BR, BC), jnp.float32),
        ],
        compiler_params=pltpu.CompilerParams(vmem_limit_bytes=20 * MIB),
        cost_estimate=pl.CostEstimate(
            flops=products // 2, bytes_accessed=8 * MIB, transcendentals=0
        ),
        name="diag_products",
    )(ancestors[0], weight_table, pole_slot, jnp.concatenate(late_owners), total, first_turned, turned)

    everyone_pairs = [shift_pairs(rows, cols, step, everyone) for step in range(cols)]
    arrived = [
        lax.ppermute(diag_send[step - 1], grid, everyone_pairs[step])
        for step in range(1, cols)
    ]
    *rounded, own = pl.pallas_call(
        functools.partial(regroup_kernel, poles, rows),
        out_shape=(jax.ShapeDtypeStruct((part + BR, wide), jnp.bfloat16),) * (rows - 1)
        + (jax.ShapeDtypeStruct((part + BR, wide), jnp.float32),),
        in_specs=[vmem] * (1 + len(arrived)),
        out_specs=(vmem,) * rows,
        compiler_params=pltpu.CompilerParams(vmem_limit_bytes=16 * MIB),
        name="regroup",
    )(diag_keep, *arrived)
    parts = [
        lax.ppermute(rounded[step - 1], "row", [(i, (i + step) % rows) for i in range(rows)])
        for step in range(1, rows)
    ]
    laid_diag, message = pl.pallas_call(
        functools.partial(finish_kernel, poles),
        out_shape=(
            jax.ShapeDtypeStruct((part * 2 * across, BC), jnp.float32),
            jax.ShapeDtypeStruct((part * across + poles * BR, BC), jnp.float32),
        ),
        in_specs=[smem] * 2 + [vmem] * (2 + len(parts)),
        out_specs=(vmem,) * 2,
        compiler_params=pltpu.CompilerParams(vmem_limit_bytes=8 * MIB),
        name="finish",
    )(weight_table, pole_slot, laid(dinv), own, *parts)
    diag_inverse = plain(laid_diag, dinv.shape)
    messages = [message]
    for step in range(1, poles):
        messages.append(lax.ppermute(message, "pole", [(i, i ^ step) for i in range(poles)]))

    split = part * across
    laid_density, tile_sum = pl.pallas_call(
        functools.partial(density_kernel, split),
        out_shape=(
            jax.ShapeDtypeStruct((split, BC), jnp.float32),
            jax.ShapeDtypeStruct((1, BR, BC), jnp.float32),
        ),
        in_specs=[vmem] * poles,
        out_specs=(vmem,) * 2,
        compiler_params=pltpu.CompilerParams(vmem_limit_bytes=8 * MIB),
        name="density",
    )(*messages)
    density_diag = laid_density.reshape(part, 1, half)

    parts = []
    for send, size in zip(sends, sizes):
        parts += [
            lax.ppermute(send[(step - 1) * size : step * size], grid, everyone_pairs[step])
            for step in range(1, cols)
        ]
    block = laid_rows // sum(SPLIT)
    specs = [pl.BlockSpec((block, BC), lambda i: (i, 0))]
    first = 0
    for share in SPLIT:
        spec = pl.BlockSpec(
            (block, BC), lambda i, f=first, n=share: (jnp.clip(i - f, 0, n - 1), 0)
        )
        specs += [spec] * (cols - 1)
        first += share
    column = pl.pallas_call(
        functools.partial(join_kernel, cols - 1),
        grid=(sum(SPLIT),),
        out_shape=jax.ShapeDtypeStruct((laid_rows, BC), jnp.float32),
        in_specs=specs,
        out_specs=pl.BlockSpec((block, BC), lambda i: (i, 0)),
        compiler_params=pltpu.CompilerParams(vmem_limit_bytes=16 * MIB),
        name="join_columns",
    )(keep, *parts)
    column_out = plain(column, (rows_here, 1, 1, 2, half))
    return (column_out, diag_inverse, density_diag, tile_sum)


def solution(mesh):
    in_specs = (
        P("pole", None, "row", "col"),
        P("pole", None, ("row", "col"), None),
        P(("row", "col"), "pole", None, None, None),
        P(),
        P(("row", "col"), None),
        P(),
        P("pole"),
    )
    out_specs = (
        P(("row", "col"), "pole", None, None, None),
        P(("row", "col"), "pole", None, None, None),
        P(("row", "col"), None, None),
        P(("pole", "row", "col"), None, None),
    )
    return jax.shard_map(compute, mesh=mesh, in_specs=in_specs, out_specs=out_specs, check_vma=False)
```

```python
import functools

import jax
import jax.numpy as jnp
from jax import lax
from jax.experimental import pallas as pl
from jax.experimental.pallas import tpu as pltpu
from jax.sharding import PartitionSpec as P


BS = 128
BR = 8
BC = 128
MIB = 1 << 20


def shift_pairs(rows, cols, step, valid):
    return [
        (r * cols + c, r * cols + (c + step) % cols)
        for r in range(rows)
        if valid(r)
        for c in range(cols)
    ]


def gather_stages(shard, rows, cols):
    grid = ("row", "col")
    if rows != 4:
        full = lax.all_gather(shard, grid, axis=0, tiled=True).reshape((rows, cols) + shard.shape)
        c = lax.axis_index("col")
        stages = []
        for row in range(rows):
            line = [lax.dynamic_index_in_dim(full[row], (c - step) % cols, 0, False) for step in range(cols)]
            stages.append([[piece] for piece in line])
        return stages, [[row] * rows for row in range(rows)]
    sources = [[0, 1, 2, 3], [1, 0, 3, 2], [2, 2, 1, 1], [3, 3, 0, 0]]
    outer = [(0, 1), (1, 0), (2, 3), (3, 2)]
    inner = [(1, 2), (2, 1)]
    r = lax.axis_index("row")
    middle = jnp.logical_or(r == 1, r == 2)
    height = shard.shape[0] // 2
    stages = [[[] for _ in range(cols)] for _ in range(rows)]
    for part in (0, 1):
        own = shard[part * height : (part + 1) * height]

        def hop(value, pairs):
            return lax.ppermute(value, "row", pairs)

        near = hop(own, outer)
        cross = hop(own, inner)
        cross_out = hop(cross, outer)
        far = hop(near, inner)
        far_out = hop(far, outer)
        line = [
            lambda: own,
            lambda: near,
            lambda: jnp.where(middle, cross, cross_out),
            lambda: jnp.where(middle, far, far_out),
        ]
        last = None
        opened = []
        for stage, make in enumerate(line):
            piece = make()
            stages[stage][0].append(piece)
            leaving = piece
            if last is not None and stage < rows - 1:
                leaving, _ = lax.optimization_barrier((piece, last))
            for step in range(1, cols):
                if stage == 1 and part == 1:
                    relayed, _ = lax.optimization_barrier((opened[step - 1], far_out))
                    stages[stage][step].append(lax.ppermute(relayed, "row", outer))
                    continue
                pairs = shift_pairs(rows, cols, step, lambda r: True)
                last = lax.ppermute(leaving, grid, pairs)
                stages[stage][step].append(last)
                if stage == 0:
                    opened.append(last)
    return stages, sources


def counts_of(ancestors, inverse, rows, cols):
    row_blocks, col_blocks = inverse.shape[1] // BS, inverse.shape[2] // BS
    r = lax.axis_index("row")
    c = lax.axis_index("col")

    def below(limit):
        total = jnp.int32(0)
        for i in range(ancestors.shape[0]):
            total = total + (ancestors[i] < limit).astype(jnp.int32)
        return total

    row_first, row_last = below(r * row_blocks), below((r + 1) * row_blocks)
    col_first, col_last = below(c * col_blocks), below((c + 1) * col_blocks)
    count = row_last - row_first
    return rows, cols, row_blocks, col_blocks, row_first, count, col_first, col_last


def source_row(sources, stage):
    r = lax.axis_index("row")
    total = jnp.int32(0)
    for row, source in enumerate(sources[stage]):
        total = total + jnp.where(r == row, source, 0)
    return total


def fill(full, pieces, sources, stage, cols):
    c = lax.axis_index("col")
    source = source_row(sources, stage)
    chunks = len(pieces) // cols
    height = pieces[0].shape[0]
    for step in range(cols):
        shard = source * cols + lax.rem(c - step + cols, cols)
        for chunk in range(chunks):
            start = pl.multiple_of((shard * chunks + chunk) * height, height)
            full[pl.ds(start, height), :] = pieces[step * chunks + chunk][...]


def multiply(acc, inverse, full, ancestors, counts, pair, source):
    rows, _, row_blocks, col_blocks = counts[:4]
    row_first, row_count, col_first, col_last = counts[4:]
    stage_blocks = ancestors.shape[0] // rows
    low = source * stage_blocks
    r = lax.axis_index("row")
    c = lax.axis_index("col")

    start = jnp.maximum(low, col_first)
    width = jnp.minimum(low + stage_blocks, col_last) - start

    def add(first, blocks):
        left = []
        for n in range(blocks):
            k = first + n
            inside = jnp.logical_and(k >= col_first, k < col_last)
            block = jnp.where(inside, ancestors[k] - c * col_blocks, 0)
            column = pl.ds(pl.multiple_of(block * BS, BS), BS)
            both = []
            for i in range(2):
                listed = ancestors[row_first + jnp.minimum(2 * pair + i, row_count - 1)]
                row = pl.multiple_of((listed - r * row_blocks) * BS, BS)
                both.append(inverse[:, pl.ds(row, BS), column].reshape(2 * BS, BS))
            value = jnp.concatenate(both, axis=0)
            left.append(value * inside.astype(value.dtype))
        place = pl.ds(pl.multiple_of(first * BS, BS), blocks * BS)
        acc[...] += jnp.dot(
            jnp.concatenate(left, axis=1), full[place, :], preferred_element_type=jnp.float32
        )

    few = stage_blocks // 2

    @pl.when(width > few)
    def _():
        add(low, stage_blocks)

    @pl.when(jnp.logical_and(width > 0, width <= few))
    def _():
        add(jnp.minimum(start, low + stage_blocks - few), few)


def combine(acc, n):
    half = acc.shape[1] // 2
    upper, lower = acc.at[2 * n * BS : (2 * n + 1) * BS], acc.at[(2 * n + 1) * BS : (2 * n + 2) * BS]
    return upper[:, :half] - lower[:, half:], upper[:, half:] + lower[:, :half]


def add_products(sources, stages, ancestors, inverse, before, full, acc, counts, store):
    row_count = counts[5]

    @pl.loop(0, (row_count + 1) // 2)
    def _(pair):
        if before is None:
            acc[...] = jnp.zeros_like(acc)
        else:
            for n in range(2):
                i = jnp.minimum(2 * pair + n, row_count - 1)
                acc[2 * n * BS : (2 * n + 1) * BS, :] = before[i]
                acc[(2 * n + 1) * BS : (2 * n + 2) * BS, :] = jnp.zeros((BS, acc.shape[1]), acc.dtype)
        for stage in stages:
            multiply(acc, inverse, full, ancestors, counts, pair, source_row(sources, stage))
        for n in range(2):

            @pl.when(2 * pair + n < row_count)
            def _():
                store(2 * pair + n, *combine(acc, n))


def list_kernel(ancestors, out):
    for i in range(ancestors.shape[0]):
        out[i] = ancestors[i]


def early_kernel(sources, stages, added, rows, cols, ancestors, inverse, *refs):
    early, turned, full, acc = refs[-4:]
    before = refs[0] if added else None
    pieces = refs[1 if added else 0 : -4]
    each = len(pieces) // len(stages)
    half = acc.shape[1] // 2
    for n, stage in enumerate(stages):
        fill(full, pieces[n * each : (n + 1) * each], sources, stage, cols)
    counts = counts_of(ancestors, inverse, rows, cols)

    def store(i, real, imag):
        early[i, :, :half] = real
        early[i, :, half:] = imag

    add_products(sources, stages, ancestors, inverse, before, full, acc, counts, store)
    turn_blocks(sources, stages, ancestors, full, counts, turned)


def brought(sources, stages, rows, selected, block):
    stage_blocks = selected // rows
    found = False
    for stage in stages:
        low = source_row(sources, stage) * stage_blocks
        found = jnp.logical_or(found, jnp.logical_and(block >= low, block < low + stage_blocks))
    return found


def turn_blocks(sources, stages, ancestors, full, counts, turned):
    half = full.shape[1] // 2
    rows, row_first, row_count = counts[0], counts[4], counts[5]

    @pl.loop(0, row_count)
    def _(i):
        block = row_first + i

        @pl.when(brought(sources, stages, rows, ancestors.shape[0], block))
        def _():
            rows_of = full[pl.ds(pl.multiple_of(block * BS, BS), BS), :]
            left = jnp.concatenate([rows_of[:, :half], rows_of[:, half:]], axis=0)
            turned[i] = left.T


def last_kernel(sources, stages, rows, cols, ancestors, inverse, early, *refs):
    total, turned, full, acc = refs[-4:]
    pieces = refs[:-4]
    each = len(pieces) // len(stages)
    half = acc.shape[1] // 2
    for n, stage in enumerate(stages):
        fill(full, pieces[n * each : (n + 1) * each], sources, stage, cols)
    counts = counts_of(ancestors, inverse, rows, cols)

    def store(i, real, imag):
        total[i, :, :half] = real
        total[i, :, half:] = imag

    add_products(sources, stages, ancestors, inverse, early, full, acc, counts, store)
    turn_blocks(sources, stages, ancestors, full, counts, turned)


def lay_kernel(cols, ancestors, total, keep, send, leaving):
    row_blocks, _, wide = total.shape
    half = wide // 2
    across = half // BC
    own_blocks = row_blocks // cols
    size = BS * 2 * across
    r = lax.axis_index("row")
    c = lax.axis_index("col")

    for n in range(row_blocks):
        slot = jnp.int32(0)
        listed = False
        for k in range(ancestors.shape[0]):
            slot = slot + jnp.logical_and(
                ancestors[k] >= r * row_blocks, ancestors[k] < r * row_blocks + n
            ).astype(jnp.int32)
            listed = jnp.logical_or(listed, ancestors[k] == r * row_blocks + n)
        turn = lax.rem(n // own_blocks - c + cols, cols)
        within = n % own_blocks * size
        start = pl.multiple_of((turn - 1) * keep.shape[0] + within, size)

        def lay(target, start):
            for j in range(across):
                for m in range(2):
                    first = m * half + j * BC
                    rows_of = pl.ds(start + 2 * j + m, BS, stride=2 * across)
                    target[rows_of, :] = -total[slot, :, first : first + BC]

        @pl.when(jnp.logical_and(listed, turn == 0))
        def _():
            lay(keep, within)

        @pl.when(jnp.logical_and(listed, turn > 0))
        def _():
            lay(leaving, start)

        @pl.when(jnp.logical_and(jnp.logical_not(listed), turn == 0))
        def _():
            keep[within : within + size, :] = jnp.zeros((size, BC), jnp.float32)

        @pl.when(jnp.logical_and(jnp.logical_not(listed), turn > 0))
        def _():
            leaving[pl.ds(start, size), :] = jnp.zeros((size, BC), jnp.float32)

    send[...] = leaving[...].astype(send.dtype)


def diag_kernel(
    sources, first_stages, poles, rows, cols, row_blocks, ancestors, table, slot, owner, *refs
):
    total, first_turned, turned, diag_keep, diag_send, diag, tiles = refs
    half, wide = diag.shape
    across = half // BC
    own_blocks = row_blocks // cols
    r = lax.axis_index("row")
    c = lax.axis_index("col")

    def below(limit):
        count = jnp.int32(0)
        for i in range(ancestors.shape[0]):
            count = count + (ancestors[i] < limit).astype(jnp.int32)
        return count

    row_first = below(r * row_blocks)
    diag[...] = jnp.zeros_like(diag)
    tiles[...] = jnp.zeros_like(tiles)
    weight_real = table[0, slot[0]]
    weight_imag = table[1, slot[0]]

    @pl.loop(0, below((r + 1) * row_blocks) - row_first)
    def _(i):
        real = total[i, :, :half]
        imag = total[i, :, half:]
        first = brought(sources, first_stages, rows, ancestors.shape[0], row_first + i)

        @pl.when(first)
        def _():
            turned[i] = first_turned[i]

        left = turned[i]
        real_high = real.astype(jnp.bfloat16)
        imag_high = imag.astype(jnp.bfloat16)
        real_low = (real - real_high.astype(jnp.float32)).astype(jnp.bfloat16)
        imag_low = (imag - imag_high.astype(jnp.float32)).astype(jnp.bfloat16)
        right = jnp.concatenate(
            [
                jnp.concatenate([real_high, imag_high], axis=1),
                jnp.concatenate([-imag_high, real_high], axis=1),
                jnp.concatenate([real_low, imag_low], axis=1),
                jnp.concatenate([-imag_low, real_low], axis=1),
            ],
            axis=0,
        )
        diag[...] += jnp.dot(
            jnp.concatenate([left, left], axis=1), right, preferred_element_type=jnp.float32
        )
        block = ancestors[row_first + i] - r * row_blocks
        place = block // own_blocks
        mixed = -(weight_real * imag + weight_imag * real)
        per_device = own_blocks * (BS // BR) * across
        first = lax.rem(c - place + cols, cols) * per_device + lax.rem(block, own_blocks) * (
            BS // BR
        ) * across
        for group in range(BS // BR):
            for j in range(across):
                tile = owner[first + group * across + j]
                tiles[j, tile] += mixed[group * BR : (group + 1) * BR, j * BC : (j + 1) * BC]

    part = half // (rows * cols)
    for row in range(rows):
        for step in range(cols):
            place = row * cols + lax.rem(c + step, cols)
            value = diag[pl.ds(pl.multiple_of(place * part, part), part), :]
            if step == 0:
                diag_keep[row, :part] = value
                diag_keep[row, part:] = jnp.zeros((BR, wide), jnp.float32)
            else:
                diag_send[step - 1, row, :part] = value.astype(diag_send.dtype)
                diag_send[step - 1, row, part:] = jnp.zeros((BR, wide), diag_send.dtype)
            for pole in range(poles):
                sum_of = tiles[0, pole * rows * cols + place]
                for j in range(1, across):
                    sum_of = sum_of + tiles[j, pole * rows * cols + place]
                if step == 0:
                    diag_keep[row, part:, 2 * pole * BC : (2 * pole + 1) * BC] = sum_of
                else:
                    diag_send[step - 1, row, part:, 2 * pole * BC : 2 * (pole + 1) * BC] = halves(sum_of)


def density_kernel(split, *refs):
    *messages, density, tile = refs
    start = pl.multiple_of(split + lax.axis_index("pole") * BR, BR)
    for place, out in ((pl.ds(0, split), density.at[...]), (pl.ds(start, BR), tile.at[0])):
        values = [message[place, :] for message in messages]
        while len(values) > 1:
            values = [a + b for a, b in zip(values[::2], values[1::2])]
        out[...] = values[0]


def join_kernel(keep, *refs):
    *arrived, out = refs
    value = keep[...]
    for ref in arrived:
        value = value + ref[...].astype(jnp.float32)
    out[...] = value


def halves(value):
    high = value.astype(jnp.bfloat16)
    low = (value - high.astype(jnp.float32)).astype(jnp.bfloat16)
    return jnp.concatenate([high, low], axis=1)


def regroup_kernel(poles, rows, kept, *refs):
    *rounded, own = refs[-rows:]
    arrived = refs[:-rows]
    part = own.shape[0] - BR
    r = lax.axis_index("row")

    def total(row):
        value = kept[row]
        for ref in arrived:
            value = value + ref[row].astype(jnp.float32)
        return value

    own[...] = total(r)
    for step in range(1, rows):
        value = total(lax.rem(r + step, rows))
        out = rounded[step - 1]
        out[:part] = value[:part].astype(out.dtype)
        for pole in range(poles):
            first = 2 * pole * BC
            band = value[part:, first : first + BC] + value[part:, first + BC : first + 2 * BC]
            out[part:, first : first + 2 * BC] = halves(band)


def finish_kernel(poles, table, slot, laid_dinv, own, *refs):
    diag_out, message = refs[-2:]
    arrived = refs[:-2]
    part, wide = own.shape[0] - BR, own.shape[1]
    across = wide // (2 * BC)
    total = own[...]
    for ref in arrived:
        total = total + ref[...].astype(jnp.float32)
    weight_real = table[0, slot[0]]
    weight_imag = table[1, slot[0]]
    for j in range(across):
        values = []
        for n in range(2):
            rows_of = pl.ds(2 * j + n, part, stride=2 * across)
            first = (n * across + j) * BC
            values.append(laid_dinv[rows_of, :] + total[:part, first : first + BC])
            diag_out[rows_of, :] = values[n]
        share = weight_real * values[1] + weight_imag * values[0]
        message[pl.ds(j, part, stride=across), :] = share
    for pole in range(poles):
        first = 2 * pole * BC
        band = total[part:, first : first + BC] + total[part:, first + BC : first + 2 * BC]
        start = part * across + pole * BR
        message[start : start + BR] = band


def compute(inverse, factor, dinv, ancestors, owner, weight_table, pole_slot):
    rows = lax.axis_size("row")
    cols = lax.axis_size("col")
    poles = lax.axis_size("pole")
    grid = ("row", "col")
    tile_count = poles * rows * cols
    here = inverse[0]
    wide = factor.shape[3]
    half = wide // 2
    rows_here = here.shape[1] // cols
    row_blocks = here.shape[1] // BS
    selected = ancestors.shape[1]
    part = half // (rows * cols)
    everyone = lambda r: True

    owners = [owner[:, 0]]
    for step in range(1, cols):
        pairs = shift_pairs(rows, cols, step, everyone)
        owners.append(lax.ppermute(owner[:, 0], grid, pairs))
    smem = pl.BlockSpec(memory_space=pltpu.SMEM)
    vmem = pl.BlockSpec(memory_space=pltpu.VMEM)
    whole = pl.BlockSpec(memory_space=pl.ANY)
    across = half // BC

    def laid(value):
        value = value.reshape(-1, 2, across, BC).transpose(0, 2, 1, 3)
        return value.reshape(-1, BC)

    def plain(value, shape):
        value = value.reshape(-1, across, 2, BC).transpose(0, 2, 1, 3)
        return value.reshape(shape)

    stages, sources = gather_stages(factor[0, 0], rows, cols)
    stages = [[chunk for step in stage for chunk in step] for stage in stages]
    products = 2 * row_blocks * BS * 2 * wide * selected * BS // cols
    scratch = [
        pltpu.VMEM((selected * BS, wide), jnp.bfloat16),
        pltpu.VMEM((4 * BS, wide), jnp.float32),
    ]
    row_products = jax.ShapeDtypeStruct((row_blocks, BS, wide), jnp.float32)
    groups = [(0, rows - 2)] if rows > 2 else [(0,)]
    last = tuple(stage for stage in range(rows) if stage not in groups[0])
    listing = pl.pallas_call(
        list_kernel,
        out_shape=jax.ShapeDtypeStruct((selected,), jnp.int32),
        in_specs=[smem],
        out_specs=smem,
        compiler_params=pltpu.CompilerParams(vmem_limit_bytes=MIB),
        cost_estimate=pl.CostEstimate(
            flops=products // 3, bytes_accessed=0, transcendentals=0
        ),
        name="list_blocks",
    )(ancestors[0])
    turned_blocks = jax.ShapeDtypeStruct((row_blocks, half, 2 * BS), jnp.bfloat16)
    early_pieces = [piece for stage in groups[0] for piece in stages[stage]]
    early, first_turned = pl.pallas_call(
        functools.partial(early_kernel, sources, groups[0], False, rows, cols),
        out_shape=(row_products, turned_blocks),
        in_specs=[smem, vmem] + [vmem] * len(early_pieces),
        out_specs=(vmem,) * 2,
        scratch_shapes=scratch,
        compiler_params=pltpu.CompilerParams(vmem_limit_bytes=24 * MIB),
        cost_estimate=pl.CostEstimate(
            flops=products // 2, bytes_accessed=4 * MIB, transcendentals=0
        ),
        name="early_products",
    )(listing, here, *early_pieces)
    late_owners, _ = lax.optimization_barrier((tuple(owners), early))
    all_pieces = [piece for stage in last for piece in stages[stage]]
    others = max(1, cols - 1)
    laid_rows = rows_here * wide // BC
    total, turned = pl.pallas_call(
        functools.partial(last_kernel, sources, last, rows, cols),
        out_shape=(row_products, turned_blocks),
        in_specs=[smem] + [vmem] * (2 + len(all_pieces)),
        out_specs=(vmem,) * 2,
        scratch_shapes=scratch,
        compiler_params=pltpu.CompilerParams(vmem_limit_bytes=24 * MIB),
        cost_estimate=pl.CostEstimate(
            flops=products // 2, bytes_accessed=8 * MIB, transcendentals=0
        ),
        name="last_products",
    )(ancestors[0], here, early, *all_pieces)
    diag_keep, diag_send = pl.pallas_call(
        functools.partial(diag_kernel, sources, groups[0], poles, rows, cols, row_blocks),
        out_shape=(
            jax.ShapeDtypeStruct((rows, part + BR, wide), jnp.float32),
            jax.ShapeDtypeStruct((others, rows, part + BR, wide), jnp.bfloat16),
        ),
        in_specs=[smem] * 4 + [vmem] * 3,
        out_specs=(vmem,) * 2,
        scratch_shapes=[
            pltpu.VMEM((half, wide), jnp.float32),
            pltpu.VMEM((half // BC, tile_count, BR, BC), jnp.float32),
        ],
        compiler_params=pltpu.CompilerParams(vmem_limit_bytes=20 * MIB),
        cost_estimate=pl.CostEstimate(
            flops=products // 2, bytes_accessed=8 * MIB, transcendentals=0
        ),
        name="diag_products",
    )(ancestors[0], weight_table, pole_slot, jnp.concatenate(late_owners), total, first_turned, turned)

    everyone_pairs = [shift_pairs(rows, cols, step, everyone) for step in range(cols)]
    arrived = [
        lax.ppermute(diag_send[step - 1], grid, everyone_pairs[step])
        for step in range(1, cols)
    ]
    *rounded, own = pl.pallas_call(
        functools.partial(regroup_kernel, poles, rows),
        out_shape=(jax.ShapeDtypeStruct((part + BR, wide), jnp.bfloat16),) * (rows - 1)
        + (jax.ShapeDtypeStruct((part + BR, wide), jnp.float32),),
        in_specs=[vmem] * (1 + len(arrived)),
        out_specs=(vmem,) * rows,
        compiler_params=pltpu.CompilerParams(vmem_limit_bytes=16 * MIB),
        name="regroup",
    )(diag_keep, *arrived)
    parts = [
        lax.ppermute(rounded[step - 1], "row", [(i, (i + step) % rows) for i in range(rows)])
        for step in range(1, rows)
    ]
    laid_diag, message = pl.pallas_call(
        functools.partial(finish_kernel, poles),
        out_shape=(
            jax.ShapeDtypeStruct((part * 2 * across, BC), jnp.float32),
            jax.ShapeDtypeStruct((part * across + poles * BR, BC), jnp.float32),
        ),
        in_specs=[smem] * 2 + [vmem] * (2 + len(parts)),
        out_specs=(vmem,) * 2,
        compiler_params=pltpu.CompilerParams(vmem_limit_bytes=8 * MIB),
        name="finish",
    )(weight_table, pole_slot, laid(dinv), own, *parts)
    diag_inverse = plain(laid_diag, dinv.shape)
    messages = [message]
    for step in range(1, poles):
        messages.append(lax.ppermute(message, "pole", [(i, i ^ step) for i in range(poles)]))

    split = part * across
    laid_density, tile_sum = pl.pallas_call(
        functools.partial(density_kernel, split),
        out_shape=(
            jax.ShapeDtypeStruct((split, BC), jnp.float32),
            jax.ShapeDtypeStruct((1, BR, BC), jnp.float32),
        ),
        in_specs=[vmem] * poles,
        out_specs=(vmem,) * 2,
        compiler_params=pltpu.CompilerParams(vmem_limit_bytes=8 * MIB),
        name="density",
    )(*messages)
    density_diag = laid_density.reshape(part, 1, half)

    keep, send = pl.pallas_call(
        functools.partial(lay_kernel, cols),
        out_shape=(
            jax.ShapeDtypeStruct((laid_rows, BC), jnp.float32),
            jax.ShapeDtypeStruct((others * laid_rows, BC), jnp.bfloat16),
        ),
        in_specs=[smem, vmem],
        out_specs=(vmem,) * 2,
        scratch_shapes=[pltpu.VMEM((others * laid_rows, BC), jnp.float32)],
        compiler_params=pltpu.CompilerParams(vmem_limit_bytes=20 * MIB),
        cost_estimate=pl.CostEstimate(flops=0, bytes_accessed=8 * MIB, transcendentals=0),
        name="lay_columns",
    )(ancestors[0], total)
    parts = [
        lax.ppermute(send[(step - 1) * laid_rows : step * laid_rows], grid, everyone_pairs[step])
        for step in range(1, cols)
    ]
    block = laid_rows // 4
    column = pl.pallas_call(
        join_kernel,
        grid=(4,),
        out_shape=jax.ShapeDtypeStruct((laid_rows, BC), jnp.float32),
        in_specs=[pl.BlockSpec((block, BC), lambda i: (i, 0))] * cols,
        out_specs=pl.BlockSpec((block, BC), lambda i: (i, 0)),
        compiler_params=pltpu.CompilerParams(vmem_limit_bytes=16 * MIB),
        name="join_columns",
    )(keep, *parts)
    column_out = plain(column, (rows_here, 1, 1, 2, half))
    return (column_out, diag_inverse, density_diag, tile_sum)


def solution(mesh):
    in_specs = (
        P("pole", None, "row", "col"),
        P("pole", None, ("row", "col"), None),
        P(("row", "col"), "pole", None, None, None),
        P(),
        P(("row", "col"), None),
        P(),
        P("pole"),
    )
    out_specs = (
        P(("row", "col"), "pole", None, None, None),
        P(("row", "col"), "pole", None, None, None),
        P(("row", "col"), None, None),
        P(("pole", "row", "col"), None, None),
    )
    return jax.shard_map(compute, mesh=mesh, in_specs=in_specs, out_specs=out_specs, check_vma=False)
```

```python
import functools

import jax
import jax.numpy as jnp
from jax import lax
from jax.experimental import pallas as pl
from jax.experimental.pallas import tpu as pltpu
from jax.sharding import PartitionSpec as P


BS = 128
BR = 8
BC = 128
MIB = 1 << 20


def shift_pairs(rows, cols, step, valid):
    return [
        (r * cols + c, r * cols + (c + step) % cols)
        for r in range(rows)
        if valid(r)
        for c in range(cols)
    ]


def gather_stages(shard, rows, cols):
    grid = ("row", "col")
    if rows != 4:
        full = lax.all_gather(shard, grid, axis=0, tiled=True).reshape((rows, cols) + shard.shape)
        c = lax.axis_index("col")
        stages = []
        for row in range(rows):
            line = [lax.dynamic_index_in_dim(full[row], (c - step) % cols, 0, False) for step in range(cols)]
            stages.append([[piece] for piece in line])
        return stages, [[row] * rows for row in range(rows)]
    sources = [[0, 1, 2, 3], [1, 0, 3, 2], [2, 2, 1, 1], [3, 3, 0, 0]]
    outer = [(0, 1), (1, 0), (2, 3), (3, 2)]
    inner = [(1, 2), (2, 1)]
    r = lax.axis_index("row")
    middle = jnp.logical_or(r == 1, r == 2)
    height = shard.shape[0] // 2
    stages = [[[] for _ in range(cols)] for _ in range(rows)]
    for part in (0, 1):
        own = shard[part * height : (part + 1) * height]

        def hop(value, pairs):
            return lax.ppermute(value, "row", pairs)

        near = hop(own, outer)
        cross = hop(own, inner)
        cross_out = hop(cross, outer)
        far = hop(near, inner)
        far_out = hop(far, outer)
        line = [
            lambda: own,
            lambda: near,
            lambda: jnp.where(middle, cross, cross_out),
            lambda: jnp.where(middle, far, far_out),
        ]
        last = None
        opened = []
        for stage, make in enumerate(line):
            piece = make()
            stages[stage][0].append(piece)
            leaving = piece
            if last is not None and stage < rows - 1:
                leaving, _ = lax.optimization_barrier((piece, last))
            for step in range(1, cols):
                if stage == 1 and part == 1:
                    relayed, _ = lax.optimization_barrier((opened[step - 1], far_out))
                    stages[stage][step].append(lax.ppermute(relayed, "row", outer))
                    continue
                pairs = shift_pairs(rows, cols, step, lambda r: True)
                last = lax.ppermute(leaving, grid, pairs)
                stages[stage][step].append(last)
                if stage == 0:
                    opened.append(last)
    return stages, sources


def counts_of(ancestors, inverse, rows, cols):
    row_blocks, col_blocks = inverse.shape[1] // BS, inverse.shape[2] // BS
    r = lax.axis_index("row")
    c = lax.axis_index("col")

    def below(limit):
        total = jnp.int32(0)
        for i in range(ancestors.shape[0]):
            total = total + (ancestors[i] < limit).astype(jnp.int32)
        return total

    row_first, row_last = below(r * row_blocks), below((r + 1) * row_blocks)
    col_first, col_last = below(c * col_blocks), below((c + 1) * col_blocks)
    count = row_last - row_first
    return rows, cols, row_blocks, col_blocks, row_first, count, col_first, col_last


def source_row(sources, stage):
    r = lax.axis_index("row")
    total = jnp.int32(0)
    for row, source in enumerate(sources[stage]):
        total = total + jnp.where(r == row, source, 0)
    return total


def fill(full, pieces, sources, stage, cols):
    c = lax.axis_index("col")
    source = source_row(sources, stage)
    chunks = len(pieces) // cols
    height = pieces[0].shape[0]
    for step in range(cols):
        shard = source * cols + lax.rem(c - step + cols, cols)
        for chunk in range(chunks):
            start = pl.multiple_of((shard * chunks + chunk) * height, height)
            full[pl.ds(start, height), :] = pieces[step * chunks + chunk][...]


def multiply(acc, inverse, full, ancestors, counts, pair, source):
    rows, _, row_blocks, col_blocks = counts[:4]
    row_first, row_count, col_first, col_last = counts[4:]
    stage_blocks = ancestors.shape[0] // rows
    low = source * stage_blocks
    r = lax.axis_index("row")
    c = lax.axis_index("col")

    start = jnp.maximum(low, col_first)
    width = jnp.minimum(low + stage_blocks, col_last) - start

    def add(first, blocks):
        left = []
        for n in range(blocks):
            k = first + n
            inside = jnp.logical_and(k >= col_first, k < col_last)
            block = jnp.where(inside, ancestors[k] - c * col_blocks, 0)
            column = pl.ds(pl.multiple_of(block * BS, BS), BS)
            both = []
            for i in range(2):
                listed = ancestors[row_first + jnp.minimum(2 * pair + i, row_count - 1)]
                row = pl.multiple_of((listed - r * row_blocks) * BS, BS)
                both.append(inverse[:, pl.ds(row, BS), column].reshape(2 * BS, BS))
            value = jnp.concatenate(both, axis=0)
            left.append(value * inside.astype(value.dtype))
        place = pl.ds(pl.multiple_of(first * BS, BS), blocks * BS)
        acc[...] += jnp.dot(
            jnp.concatenate(left, axis=1), full[place, :], preferred_element_type=jnp.float32
        )

    few = stage_blocks // 2

    @pl.when(width > few)
    def _():
        add(low, stage_blocks)

    @pl.when(jnp.logical_and(width > 0, width <= few))
    def _():
        add(jnp.minimum(start, low + stage_blocks - few), few)


def combine(acc, n):
    half = acc.shape[1] // 2
    upper, lower = acc.at[2 * n * BS : (2 * n + 1) * BS], acc.at[(2 * n + 1) * BS : (2 * n + 2) * BS]
    return upper[:, :half] - lower[:, half:], upper[:, half:] + lower[:, :half]


def add_products(sources, stages, ancestors, inverse, before, full, acc, counts, store):
    row_count = counts[5]

    @pl.loop(0, (row_count + 1) // 2)
    def _(pair):
        if before is None:
            acc[...] = jnp.zeros_like(acc)
        else:
            for n in range(2):
                i = jnp.minimum(2 * pair + n, row_count - 1)
                acc[2 * n * BS : (2 * n + 1) * BS, :] = before[i]
                acc[(2 * n + 1) * BS : (2 * n + 2) * BS, :] = jnp.zeros((BS, acc.shape[1]), acc.dtype)
        for stage in stages:
            multiply(acc, inverse, full, ancestors, counts, pair, source_row(sources, stage))
        for n in range(2):

            @pl.when(2 * pair + n < row_count)
            def _():
                store(2 * pair + n, *combine(acc, n))


def list_kernel(ancestors, out):
    for i in range(ancestors.shape[0]):
        out[i] = ancestors[i]


def early_kernel(sources, stages, added, rows, cols, ancestors, inverse, *refs):
    early, turned, full, acc = refs[-4:]
    before = refs[0] if added else None
    pieces = refs[1 if added else 0 : -4]
    each = len(pieces) // len(stages)
    half = acc.shape[1] // 2
    for n, stage in enumerate(stages):
        fill(full, pieces[n * each : (n + 1) * each], sources, stage, cols)
    counts = counts_of(ancestors, inverse, rows, cols)

    def store(i, real, imag):
        early[i, :, :half] = real
        early[i, :, half:] = imag

    add_products(sources, stages, ancestors, inverse, before, full, acc, counts, store)
    turn_blocks(sources, stages, ancestors, full, counts, turned)


def brought(sources, stages, rows, selected, block):
    stage_blocks = selected // rows
    found = False
    for stage in stages:
        low = source_row(sources, stage) * stage_blocks
        found = jnp.logical_or(found, jnp.logical_and(block >= low, block < low + stage_blocks))
    return found


def turn_blocks(sources, stages, ancestors, full, counts, turned):
    half = full.shape[1] // 2
    rows, row_first, row_count = counts[0], counts[4], counts[5]

    @pl.loop(0, row_count)
    def _(i):
        block = row_first + i

        @pl.when(brought(sources, stages, rows, ancestors.shape[0], block))
        def _():
            rows_of = full[pl.ds(pl.multiple_of(block * BS, BS), BS), :]
            left = jnp.concatenate([rows_of[:, :half], rows_of[:, half:]], axis=0)
            turned[i] = left.T


def last_kernel(sources, stages, rows, cols, ancestors, inverse, early, *refs):
    total, turned, full, acc = refs[-4:]
    pieces = refs[:-4]
    each = len(pieces) // len(stages)
    half = acc.shape[1] // 2
    for n, stage in enumerate(stages):
        fill(full, pieces[n * each : (n + 1) * each], sources, stage, cols)
    counts = counts_of(ancestors, inverse, rows, cols)

    def store(i, real, imag):
        total[i, :, :half] = real
        total[i, :, half:] = imag

    add_products(sources, stages, ancestors, inverse, early, full, acc, counts, store)
    turn_blocks(sources, stages, ancestors, full, counts, turned)


def lay_kernel(cols, ancestors, total, keep, send, leaving):
    row_blocks, _, wide = total.shape
    half = wide // 2
    across = half // BC
    own_blocks = row_blocks // cols
    size = BS * 2 * across
    r = lax.axis_index("row")
    c = lax.axis_index("col")

    for n in range(row_blocks):
        slot = jnp.int32(0)
        listed = False
        for k in range(ancestors.shape[0]):
            slot = slot + jnp.logical_and(
                ancestors[k] >= r * row_blocks, ancestors[k] < r * row_blocks + n
            ).astype(jnp.int32)
            listed = jnp.logical_or(listed, ancestors[k] == r * row_blocks + n)
        turn = lax.rem(n // own_blocks - c + cols, cols)
        within = n % own_blocks * size
        start = pl.multiple_of((turn - 1) * keep.shape[0] + within, size)

        def lay(target, start):
            for j in range(across):
                for m in range(2):
                    first = m * half + j * BC
                    rows_of = pl.ds(start + 2 * j + m, BS, stride=2 * across)
                    target[rows_of, :] = -total[slot, :, first : first + BC]

        @pl.when(jnp.logical_and(listed, turn == 0))
        def _():
            lay(keep, within)

        @pl.when(jnp.logical_and(listed, turn > 0))
        def _():
            lay(leaving, start)

        @pl.when(jnp.logical_and(jnp.logical_not(listed), turn == 0))
        def _():
            keep[within : within + size, :] = jnp.zeros((size, BC), jnp.float32)

        @pl.when(jnp.logical_and(jnp.logical_not(listed), turn > 0))
        def _():
            leaving[pl.ds(start, size), :] = jnp.zeros((size, BC), jnp.float32)

    send[...] = leaving[...].astype(send.dtype)


def diag_kernel(
    imaginary, sources, first_stages, poles, rows, cols, row_blocks, ancestors, table, slot, owner, *refs
):
    total, first_turned, turned, diag_keep, diag_send, diag, tiles = refs
    half = diag.shape[1]
    across = half // BC
    own_blocks = row_blocks // cols
    r = lax.axis_index("row")
    c = lax.axis_index("col")

    def below(limit):
        count = jnp.int32(0)
        for i in range(ancestors.shape[0]):
            count = count + (ancestors[i] < limit).astype(jnp.int32)
        return count

    row_first = below(r * row_blocks)
    diag[...] = jnp.zeros_like(diag)
    if imaginary:
        tiles[...] = jnp.zeros_like(tiles)
    weight_real = table[0, slot[0]]
    weight_imag = table[1, slot[0]]

    @pl.loop(0, below((r + 1) * row_blocks) - row_first)
    def _(i):
        real = total[i, :, :half]
        imag = total[i, :, half:]
        first = brought(sources, first_stages, rows, ancestors.shape[0], row_first + i)

        left = jnp.where(first, first_turned[i], turned[i])
        real_high = real.astype(jnp.bfloat16)
        imag_high = imag.astype(jnp.bfloat16)
        real_low = (real - real_high.astype(jnp.float32)).astype(jnp.bfloat16)
        imag_low = (imag - imag_high.astype(jnp.float32)).astype(jnp.bfloat16)
        if imaginary:
            right = [imag_high, real_high, imag_low, real_low]
        else:
            right = [real_high, -imag_high, real_low, -imag_low]
        diag[...] += jnp.dot(
            jnp.concatenate([left, left], axis=1),
            jnp.concatenate(right, axis=0),
            preferred_element_type=jnp.float32,
        )
        if not imaginary:
            return
        block = ancestors[row_first + i] - r * row_blocks
        place = block // own_blocks
        mixed = -(weight_real * imag + weight_imag * real)
        per_device = own_blocks * (BS // BR) * across
        first = lax.rem(c - place + cols, cols) * per_device + lax.rem(block, own_blocks) * (
            BS // BR
        ) * across
        for group in range(BS // BR):
            for j in range(across):
                tile = owner[first + group * across + j]
                tiles[j, tile] += mixed[group * BR : (group + 1) * BR, j * BC : (j + 1) * BC]

    part = half // (rows * cols)
    for row in range(rows):
        for step in range(cols):
            place = row * cols + lax.rem(c + step, cols)
            value = diag[pl.ds(pl.multiple_of(place * part, part), part), :]
            if step == 0:
                diag_keep[row, :part] = value
            else:
                diag_send[step - 1, row, :part] = value.astype(diag_send.dtype)
            for pole in range(poles if imaginary else 0):
                sum_of = tiles[0, pole * rows * cols + place]
                for j in range(1, across):
                    sum_of = sum_of + tiles[j, pole * rows * cols + place]
                start, first = band_of(pole, part, half)
                if step == 0:
                    both = jnp.concatenate([sum_of, jnp.zeros((BR, BC), jnp.float32)], axis=1)
                    diag_keep[row, start : start + BR, first : first + 2 * BC] = both
                else:
                    both = halves(sum_of)
                    diag_send[step - 1, row, start : start + BR, first : first + 2 * BC] = both


def band_of(pole, part, half):
    across = half // (2 * BC)
    return part + pole // across * BR, pole % across * 2 * BC


def density_kernel(split, *refs):
    *messages, density, tile = refs
    start = pl.multiple_of(split + lax.axis_index("pole") * BR, BR)
    for place, out in ((pl.ds(0, split), density.at[...]), (pl.ds(start, BR), tile.at[0])):
        values = [message[place, :] for message in messages]
        while len(values) > 1:
            values = [a + b for a, b in zip(values[::2], values[1::2])]
        out[...] = values[0]


def join_kernel(keep, *refs):
    *arrived, out = refs
    value = keep[...]
    for ref in arrived:
        value = value + ref[...].astype(jnp.float32)
    out[...] = value


def halves(value):
    high = value.astype(jnp.bfloat16)
    low = (value - high.astype(jnp.float32)).astype(jnp.bfloat16)
    return jnp.concatenate([high, low], axis=1)


def regroup_kernel(poles, rows, others, real_kept, imag_kept, *refs):
    *rounded, own = refs[-rows:]
    real_arrived, imag_arrived = refs[:others], refs[others:-rows]
    part = own.shape[0] - BR
    half = own.shape[1] // 2
    r = lax.axis_index("row")

    def total(kept, arrived, row):
        value = kept[row]
        for ref in arrived:
            value = value + ref[row].astype(jnp.float32)
        return value

    for step in range(rows):
        row = lax.rem(r + step, rows)
        out = own if step == 0 else rounded[step - 1]
        imag = total(imag_kept, imag_arrived, row)
        out[:part, :half] = total(real_kept, real_arrived, row).astype(out.dtype)
        out[:part, half:] = imag[:part].astype(out.dtype)
        for pole in range(poles):
            start, first = band_of(pole, part, half)
            band = imag[start : start + BR, first : first + 2 * BC]
            if step > 0:
                band = halves(band[:, :BC] + band[:, BC:])
            out[part:, 2 * pole * BC : 2 * (pole + 1) * BC] = band


def finish_kernel(poles, table, slot, laid_dinv, own, *refs):
    diag_out, message = refs[-2:]
    arrived = refs[:-2]
    part, wide = own.shape[0] - BR, own.shape[1]
    across = wide // (2 * BC)
    total = own[...]
    for ref in arrived:
        total = total + ref[...].astype(jnp.float32)
    weight_real = table[0, slot[0]]
    weight_imag = table[1, slot[0]]
    for j in range(across):
        values = []
        for n in range(2):
            rows_of = pl.ds(2 * j + n, part, stride=2 * across)
            first = (n * across + j) * BC
            values.append(laid_dinv[rows_of, :] + total[:part, first : first + BC])
            diag_out[rows_of, :] = values[n]
        share = weight_real * values[1] + weight_imag * values[0]
        message[pl.ds(j, part, stride=across), :] = share
    for pole in range(poles):
        first = 2 * pole * BC
        band = total[part:, first : first + BC] + total[part:, first + BC : first + 2 * BC]
        start = part * across + pole * BR
        message[start : start + BR] = band


def compute(inverse, factor, dinv, ancestors, owner, weight_table, pole_slot):
    rows = lax.axis_size("row")
    cols = lax.axis_size("col")
    poles = lax.axis_size("pole")
    grid = ("row", "col")
    tile_count = poles * rows * cols
    here = inverse[0]
    wide = factor.shape[3]
    half = wide // 2
    rows_here = here.shape[1] // cols
    row_blocks = here.shape[1] // BS
    selected = ancestors.shape[1]
    part = half // (rows * cols)
    everyone = lambda r: True

    owners = [owner[:, 0]]
    for step in range(1, cols):
        pairs = shift_pairs(rows, cols, step, everyone)
        owners.append(lax.ppermute(owner[:, 0], grid, pairs))
    smem = pl.BlockSpec(memory_space=pltpu.SMEM)
    vmem = pl.BlockSpec(memory_space=pltpu.VMEM)
    whole = pl.BlockSpec(memory_space=pl.ANY)
    across = half // BC

    def laid(value):
        value = value.reshape(-1, 2, across, BC).transpose(0, 2, 1, 3)
        return value.reshape(-1, BC)

    def plain(value, shape):
        value = value.reshape(-1, across, 2, BC).transpose(0, 2, 1, 3)
        return value.reshape(shape)

    stages, sources = gather_stages(factor[0, 0], rows, cols)
    stages = [[chunk for step in stage for chunk in step] for stage in stages]
    products = 2 * row_blocks * BS * 2 * wide * selected * BS // cols
    scratch = [
        pltpu.VMEM((selected * BS, wide), jnp.bfloat16),
        pltpu.VMEM((4 * BS, wide), jnp.float32),
    ]
    row_products = jax.ShapeDtypeStruct((row_blocks, BS, wide), jnp.float32)
    groups = [(0, rows - 2)] if rows > 2 else [(0,)]
    last = tuple(stage for stage in range(rows) if stage not in groups[0])
    listing = pl.pallas_call(
        list_kernel,
        out_shape=jax.ShapeDtypeStruct((selected,), jnp.int32),
        in_specs=[smem],
        out_specs=smem,
        compiler_params=pltpu.CompilerParams(vmem_limit_bytes=MIB),
        cost_estimate=pl.CostEstimate(
            flops=products // 3, bytes_accessed=0, transcendentals=0
        ),
        name="list_blocks",
    )(ancestors[0])
    turned_blocks = jax.ShapeDtypeStruct((row_blocks, half, 2 * BS), jnp.bfloat16)
    early_pieces = [piece for stage in groups[0] for piece in stages[stage]]
    early, first_turned = pl.pallas_call(
        functools.partial(early_kernel, sources, groups[0], False, rows, cols),
        out_shape=(row_products, turned_blocks),
        in_specs=[smem, vmem] + [vmem] * len(early_pieces),
        out_specs=(vmem,) * 2,
        scratch_shapes=scratch,
        compiler_params=pltpu.CompilerParams(vmem_limit_bytes=24 * MIB),
        cost_estimate=pl.CostEstimate(
            flops=products // 2, bytes_accessed=4 * MIB, transcendentals=0
        ),
        name="early_products",
    )(listing, here, *early_pieces)
    late_owners, _ = lax.optimization_barrier((tuple(owners), early))
    all_pieces = [piece for stage in last for piece in stages[stage]]
    others = max(1, cols - 1)
    laid_rows = rows_here * wide // BC
    total, turned = pl.pallas_call(
        functools.partial(last_kernel, sources, last, rows, cols),
        out_shape=(row_products, turned_blocks),
        in_specs=[smem] + [vmem] * (2 + len(all_pieces)),
        out_specs=(vmem,) * 2,
        scratch_shapes=scratch,
        compiler_params=pltpu.CompilerParams(vmem_limit_bytes=24 * MIB),
        cost_estimate=pl.CostEstimate(
            flops=products // 2, bytes_accessed=8 * MIB, transcendentals=0
        ),
        name="last_products",
    )(ancestors[0], here, early, *all_pieces)
    everyone_pairs = [shift_pairs(rows, cols, step, everyone) for step in range(cols)]
    band_rows = -(-poles * 2 * BC // half) * BR
    kept, arrived = [], []
    for imaginary, height in ((False, part), (True, part + band_rows)):
        diag_keep, diag_send = pl.pallas_call(
            functools.partial(
                diag_kernel, imaginary, sources, groups[0], poles, rows, cols, row_blocks
            ),
            out_shape=(
                jax.ShapeDtypeStruct((rows, height, half), jnp.float32),
                jax.ShapeDtypeStruct((others, rows, height, half), jnp.bfloat16),
            ),
            in_specs=[smem] * 4 + [vmem] * 3,
            out_specs=(vmem,) * 2,
            scratch_shapes=[
                pltpu.VMEM((half, half), jnp.float32),
                pltpu.VMEM((half // BC, tile_count, BR, BC), jnp.float32),
            ],
            compiler_params=pltpu.CompilerParams(vmem_limit_bytes=20 * MIB),
            cost_estimate=pl.CostEstimate(
                flops=products // 4, bytes_accessed=4 * MIB, transcendentals=0
            ),
            name="diag_products",
        )(
            ancestors[0],
            weight_table,
            pole_slot,
            jnp.concatenate(late_owners),
            total,
            first_turned,
            turned,
        )
        kept.append(diag_keep)
        arrived += [
            lax.ppermute(diag_send[step - 1], grid, everyone_pairs[step])
            for step in range(1, cols)
        ]

    *rounded, own = pl.pallas_call(
        functools.partial(regroup_kernel, poles, rows, cols - 1),
        out_shape=(jax.ShapeDtypeStruct((part + BR, wide), jnp.bfloat16),) * (rows - 1)
        + (jax.ShapeDtypeStruct((part + BR, wide), jnp.float32),),
        in_specs=[vmem] * (2 + len(arrived)),
        out_specs=(vmem,) * rows,
        compiler_params=pltpu.CompilerParams(vmem_limit_bytes=16 * MIB),
        name="regroup",
    )(*kept, *arrived)
    parts = [
        lax.ppermute(rounded[step - 1], "row", [(i, (i + step) % rows) for i in range(rows)])
        for step in range(1, rows)
    ]
    laid_diag, message = pl.pallas_call(
        functools.partial(finish_kernel, poles),
        out_shape=(
            jax.ShapeDtypeStruct((part * 2 * across, BC), jnp.float32),
            jax.ShapeDtypeStruct((part * across + poles * BR, BC), jnp.float32),
        ),
        in_specs=[smem] * 2 + [vmem] * (2 + len(parts)),
        out_specs=(vmem,) * 2,
        compiler_params=pltpu.CompilerParams(vmem_limit_bytes=8 * MIB),
        name="finish",
    )(weight_table, pole_slot, laid(dinv), own, *parts)
    diag_inverse = plain(laid_diag, dinv.shape)
    messages = [message]
    for step in range(1, poles):
        messages.append(lax.ppermute(message, "pole", [(i, i ^ step) for i in range(poles)]))

    split = part * across
    laid_density, tile_sum = pl.pallas_call(
        functools.partial(density_kernel, split),
        out_shape=(
            jax.ShapeDtypeStruct((split, BC), jnp.float32),
            jax.ShapeDtypeStruct((1, BR, BC), jnp.float32),
        ),
        in_specs=[vmem] * poles,
        out_specs=(vmem,) * 2,
        compiler_params=pltpu.CompilerParams(vmem_limit_bytes=8 * MIB),
        name="density",
    )(*messages)
    density_diag = laid_density.reshape(part, 1, half)

    keep, send = pl.pallas_call(
        functools.partial(lay_kernel, cols),
        out_shape=(
            jax.ShapeDtypeStruct((laid_rows, BC), jnp.float32),
            jax.ShapeDtypeStruct((others * laid_rows, BC), jnp.bfloat16),
        ),
        in_specs=[smem, vmem],
        out_specs=(vmem,) * 2,
        scratch_shapes=[pltpu.VMEM((others * laid_rows, BC), jnp.float32)],
        compiler_params=pltpu.CompilerParams(vmem_limit_bytes=20 * MIB),
        cost_estimate=pl.CostEstimate(flops=0, bytes_accessed=8 * MIB, transcendentals=0),
        name="lay_columns",
    )(ancestors[0], total)
    parts = [
        lax.ppermute(send[(step - 1) * laid_rows : step * laid_rows], grid, everyone_pairs[step])
        for step in range(1, cols)
    ]
    block = laid_rows // 4
    column = pl.pallas_call(
        join_kernel,
        grid=(4,),
        out_shape=jax.ShapeDtypeStruct((laid_rows, BC), jnp.float32),
        in_specs=[pl.BlockSpec((block, BC), lambda i: (i, 0))] * cols,
        out_specs=pl.BlockSpec((block, BC), lambda i: (i, 0)),
        compiler_params=pltpu.CompilerParams(vmem_limit_bytes=16 * MIB),
        name="join_columns",
    )(keep, *parts)
    column_out = plain(column, (rows_here, 1, 1, 2, half))
    return (column_out, diag_inverse, density_diag, tile_sum)


def solution(mesh):
    in_specs = (
        P("pole", None, "row", "col"),
        P("pole", None, ("row", "col"), None),
        P(("row", "col"), "pole", None, None, None),
        P(),
        P(("row", "col"), None),
        P(),
        P("pole"),
    )
    out_specs = (
        P(("row", "col"), "pole", None, None, None),
        P(("row", "col"), "pole", None, None, None),
        P(("row", "col"), None, None),
        P(("pole", "row", "col"), None, None),
    )
    return jax.shard_map(compute, mesh=mesh, in_specs=in_specs, out_specs=out_specs, check_vma=False)
```

```python
import functools

import jax
import jax.numpy as jnp
from jax import lax
from jax.experimental import pallas as pl
from jax.experimental.pallas import tpu as pltpu
from jax.sharding import PartitionSpec as P


BS = 128
BR = 8
BC = 128
MIB = 1 << 20


def shift_pairs(rows, cols, step, valid):
    return [
        (r * cols + c, r * cols + (c + step) % cols)
        for r in range(rows)
        if valid(r)
        for c in range(cols)
    ]


def gather_stages(shard, rows, cols):
    grid = ("row", "col")
    if rows != 4:
        full = lax.all_gather(shard, grid, axis=0, tiled=True).reshape((rows, cols) + shard.shape)
        c = lax.axis_index("col")
        stages = []
        for row in range(rows):
            line = [lax.dynamic_index_in_dim(full[row], (c - step) % cols, 0, False) for step in range(cols)]
            stages.append([[piece] for piece in line])
        return stages, [[row] * rows for row in range(rows)]
    sources = [[0, 1, 2, 3], [1, 0, 3, 2], [2, 2, 1, 1], [3, 3, 0, 0]]
    outer = [(0, 1), (1, 0), (2, 3), (3, 2)]
    inner = [(1, 2), (2, 1)]
    r = lax.axis_index("row")
    middle = jnp.logical_or(r == 1, r == 2)
    height = shard.shape[0] // 2
    stages = [[[] for _ in range(cols)] for _ in range(rows)]
    for part in (0, 1):
        own = shard[part * height : (part + 1) * height]

        def hop(value, pairs):
            return lax.ppermute(value, "row", pairs)

        near = hop(own, outer)
        cross = hop(own, inner)
        cross_out = hop(cross, outer)
        far = hop(near, inner)
        far_out = hop(far, outer)
        line = [
            lambda: own,
            lambda: near,
            lambda: jnp.where(middle, cross, cross_out),
            lambda: jnp.where(middle, far, far_out),
        ]
        last = None
        opened = []
        for stage, make in enumerate(line):
            piece = make()
            stages[stage][0].append(piece)
            leaving = piece
            if last is not None and stage < rows - 1:
                leaving, _ = lax.optimization_barrier((piece, last))
            for step in range(1, cols):
                if stage == 1 and part == 1:
                    relayed, _ = lax.optimization_barrier((opened[step - 1], far_out))
                    stages[stage][step].append(lax.ppermute(relayed, "row", outer))
                    continue
                pairs = shift_pairs(rows, cols, step, lambda r: True)
                last = lax.ppermute(leaving, grid, pairs)
                stages[stage][step].append(last)
                if stage == 0:
                    opened.append(last)
    return stages, sources


def counts_of(ancestors, inverse, rows, cols):
    row_blocks, col_blocks = inverse.shape[1] // BS, inverse.shape[2] // BS
    r = lax.axis_index("row")
    c = lax.axis_index("col")

    def below(limit):
        total = jnp.int32(0)
        for i in range(ancestors.shape[0]):
            total = total + (ancestors[i] < limit).astype(jnp.int32)
        return total

    row_first, row_last = below(r * row_blocks), below((r + 1) * row_blocks)
    col_first, col_last = below(c * col_blocks), below((c + 1) * col_blocks)
    count = row_last - row_first
    return rows, cols, row_blocks, col_blocks, row_first, count, col_first, col_last


def source_row(sources, stage):
    r = lax.axis_index("row")
    total = jnp.int32(0)
    for row, source in enumerate(sources[stage]):
        total = total + jnp.where(r == row, source, 0)
    return total


def fill(full, pieces, sources, stage, cols):
    c = lax.axis_index("col")
    source = source_row(sources, stage)
    chunks = len(pieces) // cols
    height = pieces[0].shape[0]
    for step in range(cols):
        shard = source * cols + lax.rem(c - step + cols, cols)
        for chunk in range(chunks):
            start = pl.multiple_of((shard * chunks + chunk) * height, height)
            full[pl.ds(start, height), :] = pieces[step * chunks + chunk][...]


def multiply(acc, inverse, full, ancestors, counts, pair, source):
    rows, _, row_blocks, col_blocks = counts[:4]
    row_first, row_count, col_first, col_last = counts[4:]
    stage_blocks = ancestors.shape[0] // rows
    low = source * stage_blocks
    r = lax.axis_index("row")
    c = lax.axis_index("col")

    start = jnp.maximum(low, col_first)
    width = jnp.minimum(low + stage_blocks, col_last) - start

    def add(first, blocks):
        left = []
        for n in range(blocks):
            k = first + n
            inside = jnp.logical_and(k >= col_first, k < col_last)
            block = jnp.where(inside, ancestors[k] - c * col_blocks, 0)
            column = pl.ds(pl.multiple_of(block * BS, BS), BS)
            both = []
            for i in range(2):
                listed = ancestors[row_first + jnp.minimum(2 * pair + i, row_count - 1)]
                row = pl.multiple_of((listed - r * row_blocks) * BS, BS)
                both.append(inverse[:, pl.ds(row, BS), column].reshape(2 * BS, BS))
            value = jnp.concatenate(both, axis=0)
            left.append(value * inside.astype(value.dtype))
        place = pl.ds(pl.multiple_of(first * BS, BS), blocks * BS)
        acc[...] += jnp.dot(
            jnp.concatenate(left, axis=1), full[place, :], preferred_element_type=jnp.float32
        )

    few = stage_blocks // 2

    @pl.when(width > few)
    def _():
        add(low, stage_blocks)

    @pl.when(jnp.logical_and(width > 0, width <= few))
    def _():
        add(jnp.minimum(start, low + stage_blocks - few), few)


def combine(acc, n):
    half = acc.shape[1] // 2
    upper, lower = acc.at[2 * n * BS : (2 * n + 1) * BS], acc.at[(2 * n + 1) * BS : (2 * n + 2) * BS]
    return upper[:, :half] - lower[:, half:], upper[:, half:] + lower[:, :half]


def add_products(sources, stages, ancestors, inverse, before, full, acc, counts, store):
    row_count = counts[5]

    @pl.loop(0, (row_count + 1) // 2)
    def _(pair):
        if before is None:
            acc[...] = jnp.zeros_like(acc)
        else:
            for n in range(2):
                i = jnp.minimum(2 * pair + n, row_count - 1)
                acc[2 * n * BS : (2 * n + 1) * BS, :] = before[i]
                acc[(2 * n + 1) * BS : (2 * n + 2) * BS, :] = jnp.zeros((BS, acc.shape[1]), acc.dtype)
        for stage in stages:
            multiply(acc, inverse, full, ancestors, counts, pair, source_row(sources, stage))
        for n in range(2):

            @pl.when(2 * pair + n < row_count)
            def _():
                store(2 * pair + n, *combine(acc, n))


def list_kernel(ancestors, out):
    for i in range(ancestors.shape[0]):
        out[i] = ancestors[i]


def early_kernel(sources, stages, added, rows, cols, ancestors, inverse, *refs):
    early, turned, full, acc = refs[-4:]
    before = refs[0] if added else None
    pieces = refs[1 if added else 0 : -4]
    each = len(pieces) // len(stages)
    half = acc.shape[1] // 2
    for n, stage in enumerate(stages):
        fill(full, pieces[n * each : (n + 1) * each], sources, stage, cols)
    counts = counts_of(ancestors, inverse, rows, cols)

    def store(i, real, imag):
        early[i, :, :half] = real
        early[i, :, half:] = imag

    add_products(sources, stages, ancestors, inverse, before, full, acc, counts, store)
    turn_blocks(sources, stages, ancestors, full, counts, turned)


def brought(sources, stages, rows, selected, block):
    stage_blocks = selected // rows
    found = False
    for stage in stages:
        low = source_row(sources, stage) * stage_blocks
        found = jnp.logical_or(found, jnp.logical_and(block >= low, block < low + stage_blocks))
    return found


def turn_blocks(sources, stages, ancestors, full, counts, turned):
    half = full.shape[1] // 2
    rows, row_first, row_count = counts[0], counts[4], counts[5]

    @pl.loop(0, row_count)
    def _(i):
        block = row_first + i

        @pl.when(brought(sources, stages, rows, ancestors.shape[0], block))
        def _():
            rows_of = full[pl.ds(pl.multiple_of(block * BS, BS), BS), :]
            left = jnp.concatenate([rows_of[:, :half], rows_of[:, half:]], axis=0)
            turned[i] = left.T


def last_kernel(sources, stages, rows, cols, ancestors, inverse, early, *refs):
    total, turned, full, acc = refs[-4:]
    pieces = refs[:-4]
    each = len(pieces) // len(stages)
    half = acc.shape[1] // 2
    for n, stage in enumerate(stages):
        fill(full, pieces[n * each : (n + 1) * each], sources, stage, cols)
    counts = counts_of(ancestors, inverse, rows, cols)

    def store(i, real, imag):
        total[i, :, :half] = real
        total[i, :, half:] = imag

    add_products(sources, stages, ancestors, inverse, early, full, acc, counts, store)
    turn_blocks(sources, stages, ancestors, full, counts, turned)


def lay_kernel(cols, ancestors, total, keep, send, leaving):
    row_blocks, _, wide = total.shape
    half = wide // 2
    across = half // BC
    own_blocks = row_blocks // cols
    size = BS * 2 * across
    r = lax.axis_index("row")
    c = lax.axis_index("col")

    for n in range(row_blocks):
        slot = jnp.int32(0)
        listed = False
        for k in range(ancestors.shape[0]):
            slot = slot + jnp.logical_and(
                ancestors[k] >= r * row_blocks, ancestors[k] < r * row_blocks + n
            ).astype(jnp.int32)
            listed = jnp.logical_or(listed, ancestors[k] == r * row_blocks + n)
        turn = lax.rem(n // own_blocks - c + cols, cols)
        within = n % own_blocks * size
        start = pl.multiple_of((turn - 1) * keep.shape[0] + within, size)

        def lay(target, start):
            for j in range(across):
                for m in range(2):
                    first = m * half + j * BC
                    rows_of = pl.ds(start + 2 * j + m, BS, stride=2 * across)
                    target[rows_of, :] = -total[slot, :, first : first + BC]

        @pl.when(jnp.logical_and(listed, turn == 0))
        def _():
            lay(keep, within)

        @pl.when(jnp.logical_and(listed, turn > 0))
        def _():
            lay(leaving, start)

        @pl.when(jnp.logical_and(jnp.logical_not(listed), turn == 0))
        def _():
            keep[within : within + size, :] = jnp.zeros((size, BC), jnp.float32)

        @pl.when(jnp.logical_and(jnp.logical_not(listed), turn > 0))
        def _():
            leaving[pl.ds(start, size), :] = jnp.zeros((size, BC), jnp.float32)

    send[...] = leaving[...].astype(send.dtype)


def diag_kernel(
    imaginary, sources, first_stages, poles, rows, cols, row_blocks, ancestors, table, slot, owner, *refs
):
    total, first_turned, turned, diag_keep, diag_send, diag, tiles = refs
    half = diag.shape[1]
    across = half // BC
    own_blocks = row_blocks // cols
    r = lax.axis_index("row")
    c = lax.axis_index("col")

    def below(limit):
        count = jnp.int32(0)
        for i in range(ancestors.shape[0]):
            count = count + (ancestors[i] < limit).astype(jnp.int32)
        return count

    row_first = below(r * row_blocks)
    diag[...] = jnp.zeros_like(diag)
    if imaginary:
        tiles[...] = jnp.zeros_like(tiles)
    weight_real = table[0, slot[0]]
    weight_imag = table[1, slot[0]]

    @pl.loop(0, below((r + 1) * row_blocks) - row_first)
    def _(i):
        real = total[i, :, :half]
        imag = total[i, :, half:]
        first = brought(sources, first_stages, rows, ancestors.shape[0], row_first + i)

        left = jnp.where(first, first_turned[i], turned[i])
        real_high = real.astype(jnp.bfloat16)
        imag_high = imag.astype(jnp.bfloat16)
        real_low = (real - real_high.astype(jnp.float32)).astype(jnp.bfloat16)
        imag_low = (imag - imag_high.astype(jnp.float32)).astype(jnp.bfloat16)
        if imaginary:
            right = [imag_high, real_high, imag_low, real_low]
        else:
            right = [real_high, -imag_high, real_low, -imag_low]
        diag[...] += jnp.dot(
            jnp.concatenate([left, left], axis=1),
            jnp.concatenate(right, axis=0),
            preferred_element_type=jnp.float32,
        )
        if not imaginary:
            return
        block = ancestors[row_first + i] - r * row_blocks
        place = block // own_blocks
        mixed = -(weight_real * imag + weight_imag * real)
        per_device = own_blocks * (BS // BR) * across
        first = lax.rem(c - place + cols, cols) * per_device + lax.rem(block, own_blocks) * (
            BS // BR
        ) * across
        for group in range(BS // BR):
            for j in range(across):
                tile = owner[first + group * across + j]
                tiles[j, tile] += mixed[group * BR : (group + 1) * BR, j * BC : (j + 1) * BC]

    part = half // (rows * cols)
    for row in range(rows):
        for step in range(cols):
            place = row * cols + lax.rem(c + step, cols)
            value = diag[pl.ds(pl.multiple_of(place * part, part), part), :]
            if step == 0:
                diag_keep[row, :part] = value
            else:
                diag_send[step - 1, row, :part] = value.astype(diag_send.dtype)
            for pole in range(poles if imaginary else 0):
                sum_of = tiles[0, pole * rows * cols + place]
                for j in range(1, across):
                    sum_of = sum_of + tiles[j, pole * rows * cols + place]
                start, first = band_of(pole, part, half)
                if step == 0:
                    both = jnp.concatenate([sum_of, jnp.zeros((BR, BC), jnp.float32)], axis=1)
                    diag_keep[row, start : start + BR, first : first + 2 * BC] = both
                else:
                    both = halves(sum_of)
                    diag_send[step - 1, row, start : start + BR, first : first + 2 * BC] = both


def band_of(pole, part, half):
    across = half // (2 * BC)
    return part + pole // across * BR, pole % across * 2 * BC


def settle_kernel(laid_dinv, own, *refs):
    *arrived, diag_out = refs
    part, wide = own.shape[0] - BR, own.shape[1]
    across = wide // (2 * BC)
    total = own[:part, :]
    for ref in arrived:
        total = total + ref[:part, :].astype(jnp.float32)
    for j in range(across):
        for n in range(2):
            rows_of = pl.ds(2 * j + n, part, stride=2 * across)
            first = (n * across + j) * BC
            diag_out[rows_of, :] = laid_dinv[rows_of, :] + total[:, first : first + BC]


def density_kernel(split, *refs):
    *messages, density, tile = refs
    start = pl.multiple_of(split + lax.axis_index("pole") * BR, BR)
    for place, out in ((pl.ds(0, split), density.at[...]), (pl.ds(start, BR), tile.at[0])):
        values = [message[place, :] for message in messages]
        while len(values) > 1:
            values = [a + b for a, b in zip(values[::2], values[1::2])]
        out[...] = values[0]


def join_kernel(keep, *refs):
    *arrived, out = refs
    value = keep[...]
    for ref in arrived:
        value = value + ref[...].astype(jnp.float32)
    out[...] = value


def halves(value):
    high = value.astype(jnp.bfloat16)
    low = (value - high.astype(jnp.float32)).astype(jnp.bfloat16)
    return jnp.concatenate([high, low], axis=1)


def regroup_kernel(poles, rows, others, real_kept, imag_kept, *refs):
    *rounded, own = refs[-rows:]
    real_arrived, imag_arrived = refs[:others], refs[others:-rows]
    part = own.shape[0] - BR
    half = own.shape[1] // 2
    r = lax.axis_index("row")

    def total(kept, arrived, row):
        value = kept[row]
        for ref in arrived:
            value = value + ref[row].astype(jnp.float32)
        return value

    for step in range(rows):
        row = lax.rem(r + step, rows)
        out = own if step == 0 else rounded[step - 1]
        imag = total(imag_kept, imag_arrived, row)
        out[:part, :half] = total(real_kept, real_arrived, row).astype(out.dtype)
        out[:part, half:] = imag[:part].astype(out.dtype)
        for pole in range(poles):
            start, first = band_of(pole, part, half)
            band = imag[start : start + BR, first : first + 2 * BC]
            if step > 0:
                band = halves(band[:, :BC] + band[:, BC:])
            out[part:, 2 * pole * BC : 2 * (pole + 1) * BC] = band


def finish_kernel(poles, table, slot, laid_dinv, own, *refs):
    *arrived, message = refs
    part, wide = own.shape[0] - BR, own.shape[1]
    across = wide // (2 * BC)
    total = own[...]
    for ref in arrived:
        total = total + ref[...].astype(jnp.float32)
    weight_real = table[0, slot[0]]
    weight_imag = table[1, slot[0]]
    for j in range(across):
        values = []
        for n in range(2):
            rows_of = pl.ds(2 * j + n, part, stride=2 * across)
            first = (n * across + j) * BC
            values.append(laid_dinv[rows_of, :] + total[:part, first : first + BC])
        share = weight_real * values[1] + weight_imag * values[0]
        message[pl.ds(j, part, stride=across), :] = share
    for pole in range(poles):
        first = 2 * pole * BC
        band = total[part:, first : first + BC] + total[part:, first + BC : first + 2 * BC]
        start = part * across + pole * BR
        message[start : start + BR] = band


def compute(inverse, factor, dinv, ancestors, owner, weight_table, pole_slot):
    rows = lax.axis_size("row")
    cols = lax.axis_size("col")
    poles = lax.axis_size("pole")
    grid = ("row", "col")
    tile_count = poles * rows * cols
    here = inverse[0]
    wide = factor.shape[3]
    half = wide // 2
    rows_here = here.shape[1] // cols
    row_blocks = here.shape[1] // BS
    selected = ancestors.shape[1]
    part = half // (rows * cols)
    everyone = lambda r: True

    owners = [owner[:, 0]]
    for step in range(1, cols):
        pairs = shift_pairs(rows, cols, step, everyone)
        owners.append(lax.ppermute(owner[:, 0], grid, pairs))
    smem = pl.BlockSpec(memory_space=pltpu.SMEM)
    vmem = pl.BlockSpec(memory_space=pltpu.VMEM)
    whole = pl.BlockSpec(memory_space=pl.ANY)
    across = half // BC

    def laid(value):
        value = value.reshape(-1, 2, across, BC).transpose(0, 2, 1, 3)
        return value.reshape(-1, BC)

    def plain(value, shape):
        value = value.reshape(-1, across, 2, BC).transpose(0, 2, 1, 3)
        return value.reshape(shape)

    stages, sources = gather_stages(factor[0, 0], rows, cols)
    stages = [[chunk for step in stage for chunk in step] for stage in stages]
    products = 2 * row_blocks * BS * 2 * wide * selected * BS // cols
    scratch = [
        pltpu.VMEM((selected * BS, wide), jnp.bfloat16),
        pltpu.VMEM((4 * BS, wide), jnp.float32),
    ]
    row_products = jax.ShapeDtypeStruct((row_blocks, BS, wide), jnp.float32)
    groups = [(0, rows - 2)] if rows > 2 else [(0,)]
    last = tuple(stage for stage in range(rows) if stage not in groups[0])
    listing = pl.pallas_call(
        list_kernel,
        out_shape=jax.ShapeDtypeStruct((selected,), jnp.int32),
        in_specs=[smem],
        out_specs=smem,
        compiler_params=pltpu.CompilerParams(vmem_limit_bytes=MIB),
        cost_estimate=pl.CostEstimate(
            flops=products // 3, bytes_accessed=0, transcendentals=0
        ),
        name="list_blocks",
    )(ancestors[0])
    turned_blocks = jax.ShapeDtypeStruct((row_blocks, half, 2 * BS), jnp.bfloat16)
    early_pieces = [piece for stage in groups[0] for piece in stages[stage]]
    early, first_turned = pl.pallas_call(
        functools.partial(early_kernel, sources, groups[0], False, rows, cols),
        out_shape=(row_products, turned_blocks),
        in_specs=[smem, vmem] + [vmem] * len(early_pieces),
        out_specs=(vmem,) * 2,
        scratch_shapes=scratch,
        compiler_params=pltpu.CompilerParams(vmem_limit_bytes=24 * MIB),
        cost_estimate=pl.CostEstimate(
            flops=products // 2, bytes_accessed=4 * MIB, transcendentals=0
        ),
        name="early_products",
    )(listing, here, *early_pieces)
    late_owners, _ = lax.optimization_barrier((tuple(owners), early))
    all_pieces = [piece for stage in last for piece in stages[stage]]
    others = max(1, cols - 1)
    laid_rows = rows_here * wide // BC
    total, turned = pl.pallas_call(
        functools.partial(last_kernel, sources, last, rows, cols),
        out_shape=(row_products, turned_blocks),
        in_specs=[smem] + [vmem] * (2 + len(all_pieces)),
        out_specs=(vmem,) * 2,
        scratch_shapes=scratch,
        compiler_params=pltpu.CompilerParams(vmem_limit_bytes=24 * MIB),
        cost_estimate=pl.CostEstimate(
            flops=products // 2, bytes_accessed=8 * MIB, transcendentals=0
        ),
        name="last_products",
    )(ancestors[0], here, early, *all_pieces)
    everyone_pairs = [shift_pairs(rows, cols, step, everyone) for step in range(cols)]
    band_rows = -(-poles * 2 * BC // half) * BR
    kept, arrived = [], []
    for imaginary, height in ((False, part), (True, part + band_rows)):
        diag_keep, diag_send = pl.pallas_call(
            functools.partial(
                diag_kernel, imaginary, sources, groups[0], poles, rows, cols, row_blocks
            ),
            out_shape=(
                jax.ShapeDtypeStruct((rows, height, half), jnp.float32),
                jax.ShapeDtypeStruct((others, rows, height, half), jnp.bfloat16),
            ),
            in_specs=[smem] * 4 + [vmem] * 3,
            out_specs=(vmem,) * 2,
            scratch_shapes=[
                pltpu.VMEM((half, half), jnp.float32),
                pltpu.VMEM((half // BC, tile_count, BR, BC), jnp.float32),
            ],
            compiler_params=pltpu.CompilerParams(vmem_limit_bytes=20 * MIB),
            cost_estimate=pl.CostEstimate(
                flops=products // 4, bytes_accessed=4 * MIB, transcendentals=0
            ),
            name="diag_products",
        )(
            ancestors[0],
            weight_table,
            pole_slot,
            jnp.concatenate(late_owners),
            total,
            first_turned,
            turned,
        )
        kept.append(diag_keep)
        arrived += [
            lax.ppermute(diag_send[step - 1], grid, everyone_pairs[step])
            for step in range(1, cols)
        ]

    *rounded, own = pl.pallas_call(
        functools.partial(regroup_kernel, poles, rows, cols - 1),
        out_shape=(jax.ShapeDtypeStruct((part + BR, wide), jnp.bfloat16),) * (rows - 1)
        + (jax.ShapeDtypeStruct((part + BR, wide), jnp.float32),),
        in_specs=[vmem] * (2 + len(arrived)),
        out_specs=(vmem,) * rows,
        compiler_params=pltpu.CompilerParams(vmem_limit_bytes=16 * MIB),
        name="regroup",
    )(*kept, *arrived)
    parts = [
        lax.ppermute(rounded[step - 1], "row", [(i, (i + step) % rows) for i in range(rows)])
        for step in range(1, rows)
    ]
    message = pl.pallas_call(
        functools.partial(finish_kernel, poles),
        out_shape=jax.ShapeDtypeStruct((part * across + poles * BR, BC), jnp.float32),
        in_specs=[smem] * 2 + [vmem] * (2 + len(parts)),
        out_specs=vmem,
        compiler_params=pltpu.CompilerParams(vmem_limit_bytes=8 * MIB),
        name="finish",
    )(weight_table, pole_slot, laid(dinv), own, *parts)
    laid_diag = pl.pallas_call(
        settle_kernel,
        out_shape=jax.ShapeDtypeStruct((part * 2 * across, BC), jnp.float32),
        in_specs=[vmem] * (2 + len(parts)),
        out_specs=vmem,
        compiler_params=pltpu.CompilerParams(vmem_limit_bytes=8 * MIB),
        name="settle",
    )(laid(dinv), own, *parts)
    diag_inverse = plain(laid_diag, dinv.shape)
    messages = [message]
    for step in range(1, poles):
        messages.append(lax.ppermute(message, "pole", [(i, i ^ step) for i in range(poles)]))

    split = part * across
    laid_density, tile_sum = pl.pallas_call(
        functools.partial(density_kernel, split),
        out_shape=(
            jax.ShapeDtypeStruct((split, BC), jnp.float32),
            jax.ShapeDtypeStruct((1, BR, BC), jnp.float32),
        ),
        in_specs=[vmem] * poles,
        out_specs=(vmem,) * 2,
        compiler_params=pltpu.CompilerParams(vmem_limit_bytes=8 * MIB),
        name="density",
    )(*messages)
    density_diag = laid_density.reshape(part, 1, half)

    keep, send = pl.pallas_call(
        functools.partial(lay_kernel, cols),
        out_shape=(
            jax.ShapeDtypeStruct((laid_rows, BC), jnp.float32),
            jax.ShapeDtypeStruct((others * laid_rows, BC), jnp.bfloat16),
        ),
        in_specs=[smem, vmem],
        out_specs=(vmem,) * 2,
        scratch_shapes=[pltpu.VMEM((others * laid_rows, BC), jnp.float32)],
        compiler_params=pltpu.CompilerParams(vmem_limit_bytes=20 * MIB),
        cost_estimate=pl.CostEstimate(flops=0, bytes_accessed=8 * MIB, transcendentals=0),
        name="lay_columns",
    )(ancestors[0], total)
    parts = [
        lax.ppermute(send[(step - 1) * laid_rows : step * laid_rows], grid, everyone_pairs[step])
        for step in range(1, cols)
    ]
    block = laid_rows // 4
    column = pl.pallas_call(
        join_kernel,
        grid=(4,),
        out_shape=jax.ShapeDtypeStruct((laid_rows, BC), jnp.float32),
        in_specs=[pl.BlockSpec((block, BC), lambda i: (i, 0))] * cols,
        out_specs=pl.BlockSpec((block, BC), lambda i: (i, 0)),
        compiler_params=pltpu.CompilerParams(vmem_limit_bytes=16 * MIB),
        name="join_columns",
    )(keep, *parts)
    column_out = plain(column, (rows_here, 1, 1, 2, half))
    return (column_out, diag_inverse, density_diag, tile_sum)


def solution(mesh):
    in_specs = (
        P("pole", None, "row", "col"),
        P("pole", None, ("row", "col"), None),
        P(("row", "col"), "pole", None, None, None),
        P(),
        P(("row", "col"), None),
        P(),
        P("pole"),
    )
    out_specs = (
        P(("row", "col"), "pole", None, None, None),
        P(("row", "col"), "pole", None, None, None),
        P(("row", "col"), None, None),
        P(("pole", "row", "col"), None, None),
    )
    return jax.shard_map(compute, mesh=mesh, in_specs=in_specs, out_specs=out_specs, check_vma=False)
```
